256 devices in a mesh: dp: 4 (over y_hi, core), slab: 64 (over y_lo, x, z).
Axes of the slice: x: 4, y: 4 (y_hi: 2, y_lo: 2; y = y_hi * 2 + y_lo), z: 8, core: 2. Of those that a mesh axis runs over, the one named last changes fastest.
Arguments:
- u_field: bfloat16 [4, 128, 32, 128, 128], P('dp', 'slab'), may hold values from -6 to 6
- preact: bfloat16 [4, 128, 32, 128, 128], P('dp', 'slab'), may hold values from -6 to 6
- cotangent: bfloat16 [4, 128, 32, 128, 128], P('dp', 'slab'), may hold values from -6 to 6
- weights: bfloat16 [16, 256, 2048], P(None, 'slab'), may hold values from -6 to 6
Outputs:
- grad_weights: float32 [16, 256, 2048], P('dp', 'slab')
- grad_field: bfloat16 [4, 128, 32, 128, 128], P('dp', 'slab')
The draws below stay inside these ranges and needn't reach their ends.
All inputs are finite; a program needn't handle non-finite values.
Results may differ from the reference program's by a relative error of at most 0.0055.
Values sent between devices are 32-bit elements; how exact they have to be, the bound alone decides.
No kernel may reach another device: no remote copies, remote signals or barrier semaphores. Data moves between devices by JAX's collectives and lax.ppermute only.
A program may use at most 64 MiB of HBM per device.

```python
import math
import jax
import jax.numpy as jnp
from jax import lax

C = 32
NX = 128
NY = 128
NZ = 128
MX = 16
MY = 16
MZ = 16
KYZ = 256
SAMPLES = 4


def steps_of(key, extent, cuts, smallest, top_value):
    factor_of, own = 1.0, jax.random.fold_in(key, 6)
    for axis_at, blocks in cuts:
        steps = jnp.exp(jax.random.uniform(jax.random.fold_in(own, axis_at), (blocks,), jnp.float32, smallest / len(cuts), top_value / len(cuts)))
        factor_of = factor_of * jnp.repeat(steps, extent[axis_at] // blocks).reshape([-1 if axis == axis_at else 1 for axis in range(len(extent))])
    return factor_of


def scatter_about(rng, extent, scale, limit, cuts=(), held_as=jnp.bfloat16):
    entries = scale * jax.random.normal(rng, extent, jnp.float32)
    if cuts:
        entries = entries * steps_of(rng, extent, cuts, -0.22, 0.18)
    return jnp.clip(entries, -limit, limit).astype(held_as)


def setup_inputs(seed: int = 0) -> dict:
    key_of = jax.random.split(jax.random.key(seed), 5)
    u_field = scatter_about(key_of[0], (SAMPLES, NX, C, NY, NZ), 1.0, 6.0, ((0, 4), (1, 64)))
    preact = scatter_about(key_of[1], (SAMPLES, NX, C, NY, NZ), 1.0, 6.0, ((0, 4), (1, 64)))
    cotangent = scatter_about(key_of[2], (SAMPLES, NX, C, NY, NZ), 1.0, 6.0, ((0, 4), (1, 64)))
    weights = scatter_about(key_of[3], (MX, KYZ, 2 * C * C), 1.0, 6.0, ((1, 64),))
    return dict(u_field=u_field, preact=preact, cotangent=cotangent, weights=weights)


exact_mode = lax.Precision.HIGHEST

def signed_freqs(count):
    index = jnp.arange(count, dtype=jnp.int32)
    return jnp.where(index < count // 2, index, index - count).astype(jnp.int32)

def twiddles(length, freqs):
    product = jnp.arange(length, dtype=jnp.int32)[:, None] * freqs[None, :] % length
    angle = product.astype(jnp.float32) * (2.0 * math.pi / length)
    return (jnp.cos(angle), jnp.sin(angle))

def gelu_slope(pre):
    return 0.5 * (1.0 + lax.erf(pre * (1.0 / math.sqrt(2.0)))) + pre * jnp.exp(-0.5 * pre * pre) * (1.0 / math.sqrt(2.0 * math.pi))

def transform_planes(field, zcos_low, zsin_low, cos_y, sin_y):
    wide = field.astype(jnp.float32)
    plane_real = jnp.einsum('xcyz,zk->xcyk', wide, zcos_low.astype(jnp.float32), precision=exact_mode)
    plane_imag = jnp.einsum('xcyz,zk->xcyk', wide, zsin_low.astype(jnp.float32), precision=exact_mode)
    out_real = jnp.einsum('xcyk,ym->mkxc', plane_real, cos_y, precision=exact_mode) + jnp.einsum('xcyk,ym->mkxc', plane_imag, sin_y, precision=exact_mode)
    out_imag = jnp.einsum('xcyk,ym->mkxc', plane_imag, cos_y, precision=exact_mode) - jnp.einsum('xcyk,ym->mkxc', plane_real, sin_y, precision=exact_mode)
    return (out_real, out_imag)

def transform_rows(part_real, part_imag, cos_x, sin_x):
    out_real = jnp.einsum('mkxc,xn->nmkc', part_real, cos_x, precision=exact_mode) + jnp.einsum('mkxc,xn->nmkc', part_imag, sin_x, precision=exact_mode)
    out_imag = jnp.einsum('mkxc,xn->nmkc', part_imag, cos_x, precision=exact_mode) - jnp.einsum('mkxc,xn->nmkc', part_real, sin_x, precision=exact_mode)
    return (out_real, out_imag)

def reference(u_field, preact, cotangent, weights):
    cos_x, sin_x = twiddles(NX, signed_freqs(MX))
    cos_y, sin_y = twiddles(NY, signed_freqs(MY))
    cos_z, sin_z = twiddles(NZ, jnp.arange(MZ, dtype=jnp.int32))
    zcos_low = cos_z.astype(jnp.bfloat16)
    zsin_low = (-sin_z).astype(jnp.bfloat16)
    mode_scale = (jnp.where(jnp.arange(MZ) == 0, 1.0, 2.0) / (NX * NY * NZ)).astype(jnp.float32)
    split_weights = weights.astype(jnp.float32).reshape(MX, MY, MZ, 2, C, C)
    weight_real = split_weights[:, :, :, 0]
    weight_imag = split_weights[:, :, :, 1]
    grad_real = jnp.zeros((MX, MY, MZ, C, C), jnp.float32)
    grad_imag = jnp.zeros((MX, MY, MZ, C, C), jnp.float32)
    results = []
    for sample in range(SAMPLES):
        slope = gelu_slope(preact[sample].astype(jnp.float32))
        grad_out = (cotangent[sample].astype(jnp.float32) * slope).astype(jnp.bfloat16)
        ub_real, ub_imag = transform_planes(u_field[sample], zcos_low, zsin_low, cos_y, sin_y)
        gb_real, gb_imag = transform_planes(grad_out, zcos_low, zsin_low, cos_y, sin_y)
        gb_real = gb_real * mode_scale[None, :, None, None]
        gb_imag = gb_imag * mode_scale[None, :, None, None]
        u_real, u_imag = transform_rows(ub_real, ub_imag, cos_x, sin_x)
        g_real, g_imag = transform_rows(gb_real, gb_imag, cos_x, sin_x)
        grad_real = grad_real + jnp.einsum('nmki,nmko->nmkio', u_real, g_real, precision=exact_mode) + jnp.einsum('nmki,nmko->nmkio', u_imag, g_imag, precision=exact_mode)
        grad_imag = grad_imag + jnp.einsum('nmki,nmko->nmkio', u_real, g_imag, precision=exact_mode) - jnp.einsum('nmki,nmko->nmkio', u_imag, g_real, precision=exact_mode)
        back_real = jnp.einsum('nmkio,nmko->nmki', weight_real, g_real, precision=exact_mode) + jnp.einsum('nmkio,nmko->nmki', weight_imag, g_imag, precision=exact_mode)
        back_imag = jnp.einsum('nmkio,nmko->nmki', weight_real, g_imag, precision=exact_mode) - jnp.einsum('nmkio,nmko->nmki', weight_imag, g_real, precision=exact_mode)
        rows_real = jnp.einsum('nmkc,xn->mkxc', back_real, cos_x, precision=exact_mode) - jnp.einsum('nmkc,xn->mkxc', back_imag, sin_x, precision=exact_mode)
        rows_imag = jnp.einsum('nmkc,xn->mkxc', back_imag, cos_x, precision=exact_mode) + jnp.einsum('nmkc,xn->mkxc', back_real, sin_x, precision=exact_mode)
        plane_real = jnp.einsum('mkxc,ym->xcyk', rows_real, cos_y, precision=exact_mode) - jnp.einsum('mkxc,ym->xcyk', rows_imag, sin_y, precision=exact_mode)
        plane_imag = jnp.einsum('mkxc,ym->xcyk', rows_imag, cos_y, precision=exact_mode) + jnp.einsum('mkxc,ym->xcyk', rows_real, sin_y, precision=exact_mode)
        field_grad = jnp.einsum('xcyk,zk->xcyz', plane_real, cos_z, precision=exact_mode) - jnp.einsum('xcyk,zk->xcyz', plane_imag, sin_z, precision=exact_mode)
        results.append(field_grad.astype(jnp.bfloat16))
    grad_weights = jnp.stack([grad_real, grad_imag], axis=3).reshape(MX, KYZ, 2 * C * C)
    return (grad_weights, jnp.stack(results))
```

```python
import math

import jax
import jax.numpy as jnp
from jax import lax
from jax.sharding import PartitionSpec as P

C = 32
NX = 128
NY = 128
NZ = 128
MX = 16
MY = 16
MZ = 16


exact_mode = lax.Precision.HIGHEST


def signed_freqs(count):
    index = jnp.arange(count, dtype=jnp.int32)
    return jnp.where(index < count // 2, index, index - count)


def twiddles(length, freqs):
    product = jnp.arange(length, dtype=jnp.int32)[:, None] * freqs[None, :] % length
    angle = product.astype(jnp.float32) * (2.0 * math.pi / length)
    return (jnp.cos(angle), jnp.sin(angle))


def gelu_slope(pre):
    return 0.5 * (1.0 + lax.erf(pre * (1.0 / math.sqrt(2.0)))) + pre * jnp.exp(-0.5 * pre * pre) * (
        1.0 / math.sqrt(2.0 * math.pi)
    )


def transform_planes(field, zcos_low, zsin_low, cos_y, sin_y):
    plane_real = jnp.einsum("xcyz,zk->xcyk", field, zcos_low, preferred_element_type=jnp.float32)
    plane_imag = jnp.einsum("xcyz,zk->xcyk", field, zsin_low, preferred_element_type=jnp.float32)
    out_real = jnp.einsum("xcyk,ym->mkxc", plane_real, cos_y, precision=exact_mode) + jnp.einsum(
        "xcyk,ym->mkxc", plane_imag, sin_y, precision=exact_mode
    )
    out_imag = jnp.einsum("xcyk,ym->mkxc", plane_imag, cos_y, precision=exact_mode) - jnp.einsum(
        "xcyk,ym->mkxc", plane_real, sin_y, precision=exact_mode
    )
    return (out_real, out_imag)


def body(u_field, preact, cotangent, weights):
    planes = u_field.shape[1]
    slab_count = lax.axis_size("slab")
    owned_rows = MY * MZ // slab_count
    cos_x, sin_x = twiddles(NX, signed_freqs(MX))
    cos_y, sin_y = twiddles(NY, signed_freqs(MY))
    cos_z, sin_z = twiddles(NZ, jnp.arange(MZ, dtype=jnp.int32))
    zcos_low = cos_z.astype(jnp.bfloat16)
    zsin_low = (-sin_z).astype(jnp.bfloat16)
    mode_scale = (jnp.where(jnp.arange(MZ) == 0, 1.0, 2.0) / (NX * NY * NZ)).astype(jnp.float32)
    slope = gelu_slope(preact[0].astype(jnp.float32))
    grad_out = (cotangent[0].astype(jnp.float32) * slope).astype(jnp.bfloat16)
    ub_real, ub_imag = transform_planes(u_field[0], zcos_low, zsin_low, cos_y, sin_y)
    gb_real, gb_imag = transform_planes(grad_out, zcos_low, zsin_low, cos_y, sin_y)
    gb_real = gb_real * mode_scale[None, :, None, None]
    gb_imag = gb_imag * mode_scale[None, :, None, None]
    partial_value = jnp.stack([ub_real, ub_imag, gb_real, gb_imag], axis=3).reshape(
        MY * MZ, planes, 4 * C
    )
    moved = lax.all_to_all(partial_value, "slab", split_axis=0, concat_axis=1, tiled=True)
    count = moved.shape[1]
    cos_part = cos_x
    sin_part = sin_x
    split = moved.reshape(moved.shape[0], count, 2, 2, C)
    part_real = split[:, :, :, 0]
    part_imag = split[:, :, :, 1]
    out_real = jnp.einsum("nxfc,xm->nmfc", part_real, cos_part, precision=exact_mode) + jnp.einsum(
        "nxfc,xm->nmfc", part_imag, sin_part, precision=exact_mode
    )
    out_imag = jnp.einsum("nxfc,xm->nmfc", part_imag, cos_part, precision=exact_mode) - jnp.einsum(
        "nxfc,xm->nmfc", part_real, sin_part, precision=exact_mode
    )
    owned = jnp.stack([out_real, out_imag], axis=3).reshape(moved.shape[0], MX, 4 * C)
    owned_split = owned.reshape(owned_rows, MX, 2, 2, C)
    g_real = owned_split[:, :, 1, 0]
    g_imag = owned_split[:, :, 1, 1]
    split_weights = weights.astype(jnp.float32).reshape(MX, owned_rows, 2, C, C)
    weight_real = split_weights[:, :, 0]
    weight_imag = split_weights[:, :, 1]
    back_real = jnp.einsum("mkio,kmo->kmi", weight_real, g_real, precision=exact_mode) + jnp.einsum(
        "mkio,kmo->kmi", weight_imag, g_imag, precision=exact_mode
    )
    back_imag = jnp.einsum("mkio,kmo->kmi", weight_real, g_imag, precision=exact_mode) - jnp.einsum(
        "mkio,kmo->kmi", weight_imag, g_real, precision=exact_mode
    )
    swapped = lax.all_to_all(owned[:, :, None, :], "dp", split_axis=1, concat_axis=2, tiled=True)
    mode_share = swapped.shape[1]
    swap_split = swapped.reshape(owned_rows, mode_share, swapped.shape[2], 2, 2, C)
    su_real = swap_split[:, :, :, 0, 0]
    su_imag = swap_split[:, :, :, 0, 1]
    sg_real = swap_split[:, :, :, 1, 0]
    sg_imag = swap_split[:, :, :, 1, 1]
    grad_real = jnp.einsum("kmsi,kmso->mkio", su_real, sg_real, precision=exact_mode) + jnp.einsum(
        "kmsi,kmso->mkio", su_imag, sg_imag, precision=exact_mode
    )
    grad_imag = jnp.einsum("kmsi,kmso->mkio", su_real, sg_imag, precision=exact_mode) - jnp.einsum(
        "kmsi,kmso->mkio", su_imag, sg_real, precision=exact_mode
    )
    grad_weights = jnp.stack([grad_real, grad_imag], axis=2).reshape(
        mode_share, owned_rows, 2 * C * C
    )
    rows_real = jnp.einsum("kmc,xm->xkc", back_real, cos_x, precision=exact_mode) - jnp.einsum(
        "kmc,xm->xkc", back_imag, sin_x, precision=exact_mode
    )
    rows_imag = jnp.einsum("kmc,xm->xkc", back_imag, cos_x, precision=exact_mode) + jnp.einsum(
        "kmc,xm->xkc", back_real, sin_x, precision=exact_mode
    )
    spread = jnp.stack([rows_real, rows_imag], axis=2).reshape(slab_count, planes, owned_rows, 2 * C)
    spread = lax.all_to_all(spread, "slab", split_axis=0, concat_axis=0, tiled=True)
    spread = spread.transpose(0, 2, 1, 3).reshape(MY * MZ, planes, 2 * C)
    spread_split = spread.reshape(MY, MZ, planes, 2, C)
    rows_real = spread_split[:, :, :, 0]
    rows_imag = spread_split[:, :, :, 1]
    plane_real = jnp.einsum("mkxc,ym->xcyk", rows_real, cos_y, precision=exact_mode) - jnp.einsum(
        "mkxc,ym->xcyk", rows_imag, sin_y, precision=exact_mode
    )
    plane_imag = jnp.einsum("mkxc,ym->xcyk", rows_imag, cos_y, precision=exact_mode) + jnp.einsum(
        "mkxc,ym->xcyk", rows_real, sin_y, precision=exact_mode
    )
    field_grad = jnp.einsum("xcyk,zk->xcyz", plane_real, cos_z, precision=exact_mode) - jnp.einsum(
        "xcyk,zk->xcyz", plane_imag, sin_z, precision=exact_mode
    )
    return (grad_weights, field_grad.astype(jnp.bfloat16)[None])


def solution(mesh):
    placed = (
        P("dp", "slab", None, None, None),
        P("dp", "slab", None, None, None),
        P("dp", "slab", None, None, None),
        P(None, "slab", None),
    )
    return jax.shard_map(
        body,
        mesh=mesh,
        in_specs=placed,
        out_specs=(P("dp", "slab", None), P("dp", "slab", None, None, None)),
        check_vma=False,
    )
```

```python
import math

import jax
import jax.numpy as jnp
import numpy as np
from jax import lax
from jax.experimental import pallas as pl
from jax.experimental.pallas import tpu as pltpu
from jax.sharding import PartitionSpec as P

C = 32
NX = 128
NY = 128
NZ = 128
MX = 16
MY = 16
MZ = 16
SLABS = 64
PLANES = NX // SLABS
IMGS = PLANES * C
OWN = MY * MZ // SLABS
F32 = jnp.float32
BF16 = jnp.bfloat16
STEP = 8


def np_twiddles(length, freqs):
    product = (np.arange(length, dtype=np.int64)[:, None] * freqs[None, :]) % length
    angle = product.astype(np.float32) * np.float32(2.0 * math.pi / length)
    return np.cos(angle).astype(np.float32), np.sin(angle).astype(np.float32)


def signed(count):
    index = np.arange(count)
    return np.where(index < count // 2, index, index - count)


def split_np(table):
    high = table.astype(jnp.bfloat16)
    low = (table - high.astype(np.float32)).astype(jnp.bfloat16)
    return high, low


def make_tables():
    cx, sx = np_twiddles(NX, signed(MX))
    cy, sy = np_twiddles(NY, signed(MY))
    cz, sz = np_twiddles(NZ, np.arange(MZ))
    t = {}
    rows = np.concatenate([cy.T, sy.T], 0)
    t["fwd_y"] = np.concatenate(split_np(rows), 0)
    low_c = cz.astype(jnp.bfloat16).astype(np.float32)
    low_s = (-sz).astype(jnp.bfloat16).astype(np.float32)
    real = np.concatenate([low_c, low_s], 0).T
    imag = np.concatenate([low_s, -low_c], 0).T
    wz = np.stack([real.reshape(4, 4, 2 * NZ), imag.reshape(4, 4, 2 * NZ)], 1)
    t["fwd_z"] = wz.reshape(2 * MZ, 2 * NZ).astype(jnp.bfloat16)
    mode_scale = np.where(np.arange(MZ) == 0, 1.0, 2.0) / (NX * NY * NZ)
    per_row = np.broadcast_to(mode_scale.reshape(4, 1, 4), (4, 2, 4)).reshape(2 * MZ, 1)
    is_g = (np.arange(128) // C) % 2 == 1
    t["scale"] = np.where(is_g[None, :], per_row, 1.0).astype(np.float32)
    cxs, sxs = cx.reshape(SLABS, PLANES, MX), sx.reshape(SLABS, PLANES, MX)
    lx = np.zeros((PLANES, 2, MX, 2, SLABS), np.float32)
    for xx in range(PLANES):
        lx[xx, 0, :, 0] = cxs[:, xx].T
        lx[xx, 0, :, 1] = sxs[:, xx].T
        lx[xx, 1, :, 0] = -sxs[:, xx].T
        lx[xx, 1, :, 1] = cxs[:, xx].T
    t["fwd_x"] = np.concatenate(split_np(lx.reshape(PLANES * 2 * MX, 2 * SLABS)), 0)
    rep = np.zeros((128, 2, 4, C), np.float32)
    for part in range(2):
        for ch in range(C):
            rep[part * 64 + 32 + ch, part, :, ch] = 1.0
    t["rep_g"] = rep.reshape(128, 256).astype(jnp.bfloat16)
    rep = np.zeros((128, 2, C, C), np.float32)
    for part in range(2):
        for ch in range(C):
            rep[part * 64 + ch, part, ch, :] = 1.0
    t["rep_u"] = rep.reshape(128, 2048).astype(jnp.bfloat16)
    red = np.zeros((2, C, C, 4, C), np.float32)
    for i in range(C):
        red[0, i, :, 0, i] = 1.0
        red[1, i, :, 1, i] = 1.0
        red[1, i, :, 2, i] = -1.0
        red[0, i, :, 3, i] = 1.0
    t["red"] = red.reshape(2048, 128).astype(jnp.bfloat16)
    ld = np.stack([cxs, sxs], 2).reshape(SLABS, PLANES * 2 * MX)
    high, low = split_np(ld)
    t["inv_x"] = np.concatenate([high, high, low], 1)
    tz = np.concatenate([cz.T, sz.T], 1)
    tz = np.broadcast_to(tz[None], (MY, MZ, 2 * NZ)).reshape(MY * MZ, 2 * NZ)
    t["inv_z_hi"], t["inv_z_lo"] = split_np(tz)
    ly = np.concatenate([cy, -sy], 1)
    high, low = split_np(ly)
    t["inv_y"] = np.concatenate([high, high, low], 1)
    return t


T = make_tables()


def split(value):
    high = value.astype(BF16)
    return high, (value - high.astype(F32)).astype(BF16)


def mm(a, b):
    return jnp.dot(a, b, preferred_element_type=F32)


def mm_nt(a, b):
    return lax.dot_general(a, b, (((1,), (1,)), ((), ())), preferred_element_type=F32)


def forward_kernel(u_ref, p_ref, c_ref, ty_ref, wz_ref, sc_ref, o_ref, xc_ref, xs_ref):
    step = pl.program_id(0)
    ty = ty_ref[...]
    for j in range(STEP):
        k = step * STEP + j
        pre = p_ref[j].astype(F32)
        slope = 0.5 * (1.0 + lax.erf(pre * (1.0 / math.sqrt(2.0)))) + pre * jnp.exp(
            -0.5 * pre * pre
        ) * (1.0 / math.sqrt(2.0 * math.pi))
        grad_out = (c_ref[j].astype(F32) * slope).astype(BF16)
        both = jnp.concatenate([u_ref[j], grad_out], axis=1)
        part = mm(ty, both)
        part = part[:32] + part[32:]
        base = (k // C) * 64 + k % C
        xc_ref[pl.ds(base, MY, stride=128), :] = part[:16, :128]
        xs_ref[pl.ds(base, MY, stride=128), :] = part[16:, :128]
        xc_ref[pl.ds(base + 32, MY, stride=128), :] = part[:16, 128:]
        xs_ref[pl.ds(base + 32, MY, stride=128), :] = part[16:, 128:]

    @pl.when(step == pl.num_programs(0) - 1)
    def _():
        wz = wz_ref[...]
        scale = sc_ref[...]
        for b in range(MY):
            rows = slice(b * 128, (b + 1) * 128)
            chi, clo = split(xc_ref[rows, :])
            shi, slo = split(xs_ref[rows, :])
            high = jnp.concatenate([chi, shi], axis=1)
            low = jnp.concatenate([clo, slo], axis=1)
            res = (mm_nt(wz, high) + mm_nt(wz, low)) * scale
            for q in range(4):
                o_ref[b * 4 + q] = res[q * 8 : (q + 1) * 8]


def forward(u, pre, cot):
    block = pl.BlockSpec((STEP, NY, NZ), lambda i: (i, 0, 0))

    def whole(shape):
        return pl.BlockSpec(shape, lambda i: (0,) * len(shape))

    return pl.pallas_call(
        forward_kernel,
        grid=(IMGS // STEP,),
        out_shape=jax.ShapeDtypeStruct((SLABS, 8, 128), F32),
        in_specs=[block, block, block, whole((64, 128)), whole((32, 256)), whole((32, 128))],
        out_specs=whole((SLABS, 8, 128)),
        scratch_shapes=[pltpu.VMEM((MY * 128, 128), F32), pltpu.VMEM((MY * 128, 128), F32)],
        name="fwd_local",
    )(u, pre, cot, T["fwd_y"], T["fwd_z"], T["scale"])


def middle_kernel(m_ref, w_ref, lx_ref, rg_ref, red_ref, ld_ref, own_ref, d_ref, wf_ref, q_ref):
    lx = lx_ref[...]
    lane = lax.broadcasted_iota(jnp.int32, (MX, 128), 1)
    left = lane < 64
    for a in range(MX):
        wf_ref[pl.ds(4 * a, 4), :] = w_ref[a].astype(F32)
    for cr in range(OWN):
        rhs = jnp.concatenate(
            [m_ref[pl.ds(cr, SLABS, stride=8), :], m_ref[pl.ds(4 + cr, SLABS, stride=8), :]], axis=0
        )
        hi, lo = split(rhs)
        res = mm(lx, hi)
        res = res[:64] + res[64:] + mm(lx[:64], lo)
        summed = res[:32] + pltpu.roll(res[32:], 64, 1)
        own_ref[pl.ds(cr, MX, stride=OWN), :] = jnp.where(
            left, summed[:16], pltpu.roll(summed[16:], 64, 1)
        )
    hi, lo = split(own_ref[...])
    rg = rg_ref[...]
    grep = mm(hi, rg) + mm(lo, rg)
    g_real, g_imag = grep[:, :128], grep[:, 128:]
    acc = jnp.zeros((MX * OWN, 128), F32)
    for t in range(8):
        w_real = wf_ref[:, t * 128 : (t + 1) * 128]
        w_imag = wf_ref[:, 1024 + t * 128 : 1024 + (t + 1) * 128]
        rhi, rlo = split(w_real * g_real + w_imag * g_imag)
        ihi, ilo = split(w_real * g_imag - w_imag * g_real)
        red_r = red_ref[pl.ds(t * 128, 128), :]
        red_i = red_ref[pl.ds(1024 + t * 128, 128), :]
        red = jnp.concatenate([red_r, red_i], axis=0)
        acc += mm(jnp.concatenate([rhi, ihi], axis=1), red)
        acc += mm(jnp.concatenate([rlo, ilo], axis=1), red)
    q_ref[...] = acc
    ld = ld_ref[...]
    for cr in range(OWN):
        q = q_ref[pl.ds(cr, MX, stride=OWN), :]
        r = pltpu.roll(q, 64, 1)
        zero = jnp.zeros_like(q)
        rhs = jnp.concatenate(
            [
                jnp.where(left, q, zero),
                jnp.where(left, r, zero),
                jnp.where(left, zero, r),
                jnp.where(left, zero, q),
            ],
            axis=0,
        )
        hi, lo = split(rhs)
        d_ref[pl.ds(cr, SLABS, stride=OWN), :] = mm(ld, jnp.concatenate([hi, lo, hi], axis=0))


def middle(moved, weights):
    return pl.pallas_call(
        middle_kernel,
        out_shape=(
            jax.ShapeDtypeStruct((MX * OWN, 128), F32),
            jax.ShapeDtypeStruct((SLABS * OWN, 128), F32),
        ),
        scratch_shapes=[pltpu.VMEM((MX * OWN, 2048), F32), pltpu.VMEM((MX * OWN, 128), F32)],
        name="middle",
    )(moved, weights, T["fwd_x"], T["rep_g"], T["red"], T["inv_x"])


def weight_grad_kernel(s_ref, rg_ref, ru_ref, o_ref):
    hi, lo = split(s_ref[...])
    rg = rg_ref[...]
    grep = mm(hi, rg) + mm(lo, rg)
    g_real, g_imag = grep[:, :128], grep[:, 128:]
    both = jnp.concatenate([hi, lo], axis=0)
    for t in range(8):
        ru = jnp.concatenate(
            [ru_ref[:, t * 128 : (t + 1) * 128], ru_ref[:, 1024 + t * 128 : 1024 + (t + 1) * 128]],
            axis=1,
        )
        urep = mm(both, ru)
        urep = urep[:64] + urep[64:]
        u_real, u_imag = urep[:, :128], urep[:, 128:]
        real = g_real * u_real + g_imag * u_imag
        imag = g_imag * u_real - g_real * u_imag
        real = real[:16] + real[16:32] + real[32:48] + real[48:]
        imag = imag[:16] + imag[16:32] + imag[32:48] + imag[48:]
        for a in range(4):
            o_ref[a, :, t * 128 : (t + 1) * 128] = real[a * 4 : (a + 1) * 4]
            o_ref[a, :, 1024 + t * 128 : 1024 + (t + 1) * 128] = imag[a * 4 : (a + 1) * 4]


def weight_grad(swapped):
    return pl.pallas_call(
        weight_grad_kernel,
        out_shape=jax.ShapeDtypeStruct((4, OWN, 2 * C * C), F32),
        name="weight_grad",
    )(swapped, T["rep_g"], T["rep_u"])


def inverse_kernel(d_ref, thi_ref, tlo_ref, ly_ref, o_ref, f_ref):
    step = pl.program_id(0)

    @pl.when(step == 0)
    def _():
        hi, lo = split(d_ref[...].T)
        thi = thi_ref[...]
        tlo = tlo_ref[...]
        group = lax.broadcasted_iota(jnp.int32, (128, 256), 1) // MZ
        for b in range(MY):
            keep = group == b
            zero = jnp.zeros_like(hi)
            hib = jnp.where(keep, hi, zero)
            lob = jnp.where(keep, lo, zero)
            h = mm(hib, thi) + mm(hib, tlo) + mm(lob, thi)
            for xx in range(PLANES):
                real = h[xx * 64 : xx * 64 + 32]
                imag = h[xx * 64 + 32 : xx * 64 + 64]
                at = xx * C * 32 + b
                f_ref[pl.ds(at, C, stride=32), :] = real[:, :128] - imag[:, 128:]
                f_ref[pl.ds(at + 16, C, stride=32), :] = real[:, 128:] + imag[:, :128]

    ly = ly_ref[...]
    for j in range(0, STEP, 2):
        at = pl.multiple_of((step * STEP + j) * 32, 64)
        pair = jnp.concatenate([f_ref[pl.ds(at, 32), :], f_ref[pl.ds(at + 32, 32), :]], axis=1)
        hi, lo = split(pair)
        res = mm(ly, jnp.concatenate([hi, lo, hi], axis=0)).astype(BF16)
        o_ref[j] = res[:, :128]
        o_ref[j + 1] = res[:, 128:]


def inverse(spread):
    def whole(shape):
        return pl.BlockSpec(shape, lambda i: (0,) * len(shape))

    return pl.pallas_call(
        inverse_kernel,
        grid=(IMGS // STEP,),
        out_shape=jax.ShapeDtypeStruct((IMGS, NY, NZ), BF16),
        in_specs=[whole((256, 128)), whole((256, 256)), whole((256, 256)), whole((128, 96))],
        out_specs=pl.BlockSpec((STEP, NY, NZ), lambda i: (i, 0, 0)),
        scratch_shapes=[pltpu.VMEM((IMGS * 32, 128), F32)],
        name="inv_local",
    )(spread, T["inv_z_hi"], T["inv_z_lo"], T["inv_y"])


def body(u_field, preact, cotangent, weights):
    shape = (IMGS, NY, NZ)
    partial = forward(u_field.reshape(shape), preact.reshape(shape), cotangent.reshape(shape))
    moved = lax.all_to_all(partial, "slab", split_axis=0, concat_axis=0, tiled=True)
    owned, back = middle(moved.reshape(SLABS * 8, 128), weights)
    swapped = lax.all_to_all(owned, "dp", split_axis=0, concat_axis=0, tiled=True)
    spread = lax.all_to_all(back, "slab", split_axis=0, concat_axis=0, tiled=True)
    grad_weights = weight_grad(swapped)
    field_grad = inverse(spread)
    return grad_weights, field_grad.reshape(1, PLANES, C, NY, NZ)


def solution(mesh):
    placed = (
        P("dp", "slab", None, None, None),
        P("dp", "slab", None, None, None),
        P("dp", "slab", None, None, None),
        P(None, "slab", None),
    )
    return jax.shard_map(
        body,
        mesh=mesh,
        in_specs=placed,
        out_specs=(P("dp", "slab", None), P("dp", "slab", None, None, None)),
        check_vma=False,
    )
```

```python
import math

import jax
import jax.numpy as jnp
import numpy as np
from jax import lax
from jax.experimental import pallas as pl
from jax.experimental.pallas import tpu as pltpu
from jax.sharding import PartitionSpec as P

C = 32
NX = 128
NY = 128
NZ = 128
MX = 16
MY = 16
MZ = 16
SLABS = 64
PLANES = NX // SLABS
IMGS = PLANES * C
OWN = MY * MZ // SLABS
F32 = jnp.float32
BF16 = jnp.bfloat16
STEP = 16
MID_LOW = True
UNROLL = 0
OSTEP = 8
PAD = 132
IPAD = 36
FWD_LOW = False
INV_TERMS = 2


def np_twiddles(length, freqs):
    product = (np.arange(length, dtype=np.int64)[:, None] * freqs[None, :]) % length
    angle = product.astype(np.float32) * np.float32(2.0 * math.pi / length)
    return np.cos(angle).astype(np.float32), np.sin(angle).astype(np.float32)


def signed(count):
    index = np.arange(count)
    return np.where(index < count // 2, index, index - count)


def split_np(table):
    high = table.astype(jnp.bfloat16)
    low = (table - high.astype(np.float32)).astype(jnp.bfloat16)
    return high, low


def make_tables():
    cx, sx = np_twiddles(NX, signed(MX))
    cy, sy = np_twiddles(NY, signed(MY))
    cz, sz = np_twiddles(NZ, np.arange(MZ))
    t = {}
    rows = np.concatenate([cy.T, sy.T], 0)
    t["fwd_y"] = np.concatenate(split_np(rows), 0)
    low_c = cz.astype(jnp.bfloat16).astype(np.float32)
    low_s = (-sz).astype(jnp.bfloat16).astype(np.float32)
    real = np.concatenate([low_c, low_s], 0).T
    imag = np.concatenate([low_s, -low_c], 0).T
    wz = np.stack([real.reshape(4, 4, 2 * NZ), imag.reshape(4, 4, 2 * NZ)], 1)
    t["fwd_z"] = wz.reshape(2 * MZ, 2 * NZ).astype(jnp.bfloat16)
    mode_scale = np.where(np.arange(MZ) == 0, 0.5, 1.0) / (NX * NY * NZ)
    per_row = np.broadcast_to(mode_scale.reshape(4, 1, 4), (4, 2, 4)).reshape(2 * MZ, 1)
    is_g = (np.arange(128) // C) % 2 == 1
    t["scale"] = np.where(is_g[None, :], per_row, 1.0).astype(np.float32)
    cxs, sxs = cx.reshape(SLABS, PLANES, MX), sx.reshape(SLABS, PLANES, MX)
    lx = np.zeros((PLANES, 2, MX, 2, SLABS), np.float32)
    for xx in range(PLANES):
        lx[xx, 0, :, 0] = cxs[:, xx].T
        lx[xx, 0, :, 1] = sxs[:, xx].T
        lx[xx, 1, :, 0] = -sxs[:, xx].T
        lx[xx, 1, :, 1] = cxs[:, xx].T
    t["fwd_x"] = np.concatenate(split_np(lx.reshape(PLANES * 2 * MX, 2 * SLABS)), 0)
    rep = np.zeros((128, 2, 4, C), np.float32)
    for part in range(2):
        for ch in range(C):
            rep[part * 64 + 32 + ch, part, :, ch] = 1.0
    t["rep_g"] = rep.reshape(128, 256).astype(jnp.bfloat16)
    rep = np.zeros((2, 2, 8, 4, 2, 4, C), np.float32)
    for part in range(2):
        for r in range(4):
            rep[part, 0, :, r, part, r, :] = 1.0
    t["rep_u"] = rep.reshape(128, 256).astype(jnp.bfloat16)
    red = np.zeros((2, 4, C, 4, 8, 4), np.float32)
    for r in range(4):
        red[0, r, :, 0, :, r] = 1.0
        red[1, r, :, 1, :, r] = 1.0
        red[1, r, :, 2, :, r] = -1.0
        red[0, r, :, 3, :, r] = 1.0
    t["red"] = red.reshape(256, 128).astype(jnp.bfloat16)
    ld = np.stack([cxs, sxs], 2).reshape(SLABS, PLANES * 2 * MX)
    high, low = split_np(ld)
    t["inv_x"] = np.concatenate([high, high, low], 1)
    tz = np.concatenate([cz.T, sz.T], 1)
    tz = np.broadcast_to(tz[None], (MY, MZ, 2 * NZ)).reshape(MY * MZ, 2 * NZ)
    t["inv_z_hi"], t["inv_z_lo"] = split_np(tz)
    ly = np.concatenate([cy, -sy], 1)
    high, low = split_np(ly)
    t["inv_y"] = np.concatenate([high, high, low], 1)
    return t


T = make_tables()


def split(value):
    high = value.astype(BF16)
    return high, (value - high.astype(F32)).astype(BF16)


def mm(a, b):
    return jnp.dot(a, b, preferred_element_type=F32)


def mm_nt(a, b):
    return lax.dot_general(a, b, (((1,), (1,)), ((), ())), preferred_element_type=F32)


def loop(count, step):
    if UNROLL == 0:
        for n in range(count):
            step(n, 0)
    else:
        lax.fori_loop(0, count, step, 0, unroll=UNROLL)


HBM = pl.BlockSpec(memory_space=pltpu.HBM)


def forward_kernel(
    u_hbm, p_hbm, c_hbm, ty_hbm, wz_hbm, sc_hbm, o_hbm, o_ref, u_ref, p_ref, c_ref, ty_ref, wz_ref, sc_ref, xc_ref, xs_ref, sems, tsems, osems
):
    def chunk(src, dst, row, step):
        at = pl.ds(step * STEP, STEP)
        return pltpu.make_async_copy(src.at[at], dst.at[at], sems.at[row, step])

    table = pltpu.make_async_copy(ty_hbm, ty_ref, tsems.at[0])
    late = [
        pltpu.make_async_copy(wz_hbm, wz_ref, tsems.at[1]),
        pltpu.make_async_copy(sc_hbm, sc_ref, tsems.at[2]),
    ]
    for step in range(IMGS // STEP):
        chunk(p_hbm, p_ref, 1, step).start()
        chunk(c_hbm, c_ref, 2, step).start()
        chunk(u_hbm, u_ref, 0, step).start()
        if step == 0:
            table.start()
    for one in late:
        one.start()
    table.wait()

    def slopes(step):
        chunk(p_hbm, p_ref, 1, step).wait()
        chunk(c_hbm, c_ref, 2, step).wait()
        chunk(u_hbm, u_ref, 0, step).wait()
        for k in range(step * STEP, (step + 1) * STEP):
            arg = p_ref[k].astype(F32) * math.sqrt(0.5)
            bell = jnp.exp2((arg * (-math.log2(math.e))) * arg) * (2.0 / math.sqrt(math.pi))
            slope = (lax.erf(arg) + 1.0) + arg * bell
            c_ref[k] = (c_ref[k].astype(F32) * slope).astype(BF16)

    def images(step):
        ty = ty_ref[...]
        for k in range(step * STEP, (step + 1) * STEP):
            both = jnp.concatenate([u_ref[k], c_ref[k]], axis=1)
            part = mm(ty, both)
            part = part[:32] + part[32:]
            base = (k // C) * 64 + k % C
            xc_ref[pl.ds(base, MY, stride=PAD), :] = part[:16, :128]
            xs_ref[pl.ds(base, MY, stride=PAD), :] = part[16:, :128]
            xc_ref[pl.ds(base + 32, MY, stride=PAD), :] = part[:16, 128:]
            xs_ref[pl.ds(base + 32, MY, stride=PAD), :] = part[16:, 128:]

    for step in range(IMGS // STEP + 1):
        if step < IMGS // STEP:
            slopes(step)
        if step > 0:
            images(step - 1)
    for one in late:
        one.wait()
    wz = wz_ref[...]
    scale = sc_ref[...]

    def send(part):
        at = pl.ds(part * 16, 16)
        return pltpu.make_async_copy(o_ref.at[at], o_hbm.at[at], osems.at[part])

    for b in range(MY):
        rows = slice(b * PAD, b * PAD + 128)
        chi, clo = split(xc_ref[rows, :])
        shi, slo = split(xs_ref[rows, :])
        res = mm_nt(wz, jnp.concatenate([chi, shi], axis=1))
        if FWD_LOW:
            res += mm_nt(wz, jnp.concatenate([clo, slo], axis=1))
        res = res * scale
        for q in range(4):
            o_ref[b * 4 + q] = res[q * 8 : (q + 1) * 8]
        if b % 4 == 3:
            send(b // 4).start()
    for part in range(4):
        send(part).wait()


def forward(u, pre, cot):
    big = pltpu.VMEM((IMGS, NY, NZ), BF16)
    flat = pltpu.VMEM((MY * PAD, 128), F32)
    return pl.pallas_call(
        forward_kernel,
        out_shape=jax.ShapeDtypeStruct((SLABS, 8, 128), F32),
        in_specs=[HBM] * 6,
        out_specs=HBM,
        scratch_shapes=[
            pltpu.VMEM((SLABS, 8, 128), F32),
            big,
            big,
            big,
            pltpu.VMEM((64, 128), BF16),
            pltpu.VMEM((32, 256), BF16),
            pltpu.VMEM((32, 128), F32),
            flat,
            flat,
            pltpu.SemaphoreType.DMA((3, IMGS // STEP)),
            pltpu.SemaphoreType.DMA((3,)),
            pltpu.SemaphoreType.DMA((4,)),
        ],
        compiler_params=pltpu.CompilerParams(vmem_limit_bytes=12 << 20),
        name="fwd_local",
    )(u, pre, cot, T["fwd_y"], T["fwd_z"], T["scale"])


def middle_kernel(
    mine_ref, m_ref, w_ref, lx_ref, rg_ref, red_ref, ld_ref, own0_ref, own1_ref, own2_ref, own3_ref, d_ref, wf_ref, own_ref, q_ref
):
    for a in range(MX):
        wf_ref[pl.ds(4 * a, 4), :] = w_ref[a].astype(F32)
    lx = lx_ref[...]
    lane = lax.broadcasted_iota(jnp.int32, (MX, 128), 1)
    left = lane < 64
    for cr in range(OWN):
        rhs = jnp.concatenate(
            [m_ref[pl.ds(cr, SLABS, stride=8), :], m_ref[pl.ds(4 + cr, SLABS, stride=8), :]], axis=0
        )
        hi, lo = split(rhs)
        res = mm(lx, hi)
        res = res[:64] + res[64:] + mm(lx[:64], lo)
        summed = res[:32] + pltpu.roll(res[32:], 64, 1)
        own_ref[pl.ds(cr, MX, stride=OWN), :] = jnp.where(
            left, summed[:16], pltpu.roll(summed[16:], 64, 1)
        )
    mine = mine_ref[0]
    for other, ref in enumerate((own0_ref, own1_ref, own2_ref, own3_ref)):
        ref[...] = own_ref[pl.ds(pl.multiple_of((mine ^ other) * 16, 16), 16), :]
    hi, lo = split(own_ref[...])
    rg = rg_ref[...]
    grep = mm(hi, rg) + mm(lo, rg)
    g_real, g_imag = grep[:, :128], grep[:, 128:]
    acc = jnp.zeros((MX * OWN, 128), F32)
    slot = (lax.broadcasted_iota(jnp.int32, (MX * OWN, 128), 1) // 4) % 8
    red = red_ref[...]
    for t in range(8):
        w_real = wf_ref[:, t * 128 : (t + 1) * 128]
        w_imag = wf_ref[:, 1024 + t * 128 : 1024 + (t + 1) * 128]
        rhi, rlo = split(w_real * g_real + w_imag * g_imag)
        ihi, ilo = split(w_real * g_imag - w_imag * g_real)
        res = mm(jnp.concatenate([rhi, ihi], axis=1), red)
        if MID_LOW:
            res += mm(jnp.concatenate([rlo, ilo], axis=1), red)
        acc = jnp.where(slot == t, res, acc)
    q_ref[...] = acc
    ld = ld_ref[...]
    for cr in range(OWN):
        q = q_ref[pl.ds(cr, MX, stride=OWN), :]
        r = pltpu.roll(q, 64, 1)
        zero = jnp.zeros_like(q)
        rhs = jnp.concatenate(
            [
                jnp.where(left, q, zero),
                jnp.where(left, r, zero),
                jnp.where(left, zero, r),
                jnp.where(left, zero, q),
            ],
            axis=0,
        )
        hi, lo = split(rhs)
        d_ref[pl.ds(cr, SLABS, stride=OWN), :] = mm(ld, jnp.concatenate([hi, lo, hi], axis=0))


def middle(mine, moved, weights):
    return pl.pallas_call(
        middle_kernel,
        out_shape=(jax.ShapeDtypeStruct((16, 128), F32),) * 4
        + (jax.ShapeDtypeStruct((SLABS * OWN, 128), F32),),
        in_specs=[pl.BlockSpec(memory_space=pltpu.SMEM)] + [pl.BlockSpec(memory_space=pltpu.VMEM)] * 6,
        scratch_shapes=[
            pltpu.VMEM((MX * OWN, 2048), F32),
            pltpu.VMEM((MX * OWN, 128), F32),
            pltpu.VMEM((MX * OWN, 128), F32),
        ],
        compiler_params=pltpu.CompilerParams(vmem_limit_bytes=8 << 20),
        name="middle",
    )(mine, moved, weights, T["fwd_x"], T["rep_g"], T["red"], T["inv_x"])


def weight_grad_kernel(s0_ref, s1_ref, s2_ref, s3_ref, rg_ref, ru_ref, o_ref):
    full = jnp.concatenate([s0_ref[...], s1_ref[...], s2_ref[...], s3_ref[...]], axis=0)
    hi, lo = split(full)
    rg = rg_ref[...]
    ru = ru_ref[...]
    grep = mm(hi, rg) + mm(lo, rg)
    g_real, g_imag = grep[:, :128], grep[:, 128:]
    slot = (lax.broadcasted_iota(jnp.int32, (64, 128), 1) // 4) % 8
    for t in range(8):
        hit, lot = split(jnp.where(slot == t, full, jnp.zeros_like(full)))
        urep = mm(hit, ru) + mm(lot, ru)
        u_real, u_imag = urep[:, :128], urep[:, 128:]
        real = g_real * u_real + g_imag * u_imag
        imag = g_imag * u_real - g_real * u_imag
        real = real[:16] + real[16:32] + real[32:48] + real[48:]
        imag = imag[:16] + imag[16:32] + imag[32:48] + imag[48:]
        for a in range(4):
            o_ref[a, :, t * 128 : (t + 1) * 128] = real[a * 4 : (a + 1) * 4]
            o_ref[a, :, 1024 + t * 128 : 1024 + (t + 1) * 128] = imag[a * 4 : (a + 1) * 4]


def weight_grad(parts):
    return pl.pallas_call(
        weight_grad_kernel,
        out_shape=jax.ShapeDtypeStruct((4, OWN, 2 * C * C), F32),
        compiler_params=pltpu.CompilerParams(vmem_limit_bytes=4 << 20),
        name="weight_grad",
    )(*parts, T["rep_g"], T["rep_u"])


def inverse_kernel(d_ref, thi_ref, tlo_ref, ly_ref, o_hbm, o_ref, f_ref, osems):
    hi, lo = split(d_ref[...].T)
    thi = thi_ref[...]
    tlo = tlo_ref[...]
    group = lax.broadcasted_iota(jnp.int32, (128, 256), 1) // MZ
    for b in range(MY):
        keep = group == b
        zero = jnp.zeros_like(hi)
        hib = jnp.where(keep, hi, zero)
        h = mm(hib, thi)
        if INV_TERMS > 1:
            h += mm(hib, tlo)
        if INV_TERMS > 2:
            h += mm(jnp.where(keep, lo, zero), thi)
        for xx in range(PLANES):
            real = h[xx * 64 : xx * 64 + 32]
            imag = h[xx * 64 + 32 : xx * 64 + 64]
            at = xx * C * IPAD + b
            f_ref[pl.ds(at, C, stride=IPAD), :] = real[:, :128] - imag[:, 128:]
            f_ref[pl.ds(at + 16, C, stride=IPAD), :] = real[:, 128:] + imag[:, :128]

    def send(step):
        at = pl.ds(step * OSTEP, OSTEP)
        return pltpu.make_async_copy(o_ref.at[at], o_hbm.at[at], osems.at[step])

    def images(step, carry):
        ly = ly_ref[...]
        start = step * (OSTEP * IPAD)
        for j in range(0, OSTEP, 2):
            at = start + j * IPAD
            if UNROLL:
                at = pl.multiple_of(at, 8)
            block = f_ref[pl.ds(at, 72), :]
            pair = jnp.concatenate([block[:32], block[36:68]], axis=1)
            hi, lo = split(pair)
            res = mm(ly, jnp.concatenate([hi, lo, hi], axis=0)).astype(BF16)
            o_ref[step * OSTEP + j] = res[:, :128]
            o_ref[step * OSTEP + j + 1] = res[:, 128:]
        send(step).start()
        return carry

    loop(IMGS // OSTEP, images)
    for step in range(IMGS // OSTEP):
        send(step).wait()


def inverse(spread):
    return pl.pallas_call(
        inverse_kernel,
        out_shape=jax.ShapeDtypeStruct((IMGS, NY, NZ), BF16),
        in_specs=[pl.BlockSpec(memory_space=pltpu.VMEM)] * 4,
        out_specs=HBM,
        scratch_shapes=[
            pltpu.VMEM((IMGS, NY, NZ), BF16),
            pltpu.VMEM((IMGS * IPAD, 128), F32),
            pltpu.SemaphoreType.DMA((IMGS // OSTEP,)),
        ],
        compiler_params=pltpu.CompilerParams(vmem_limit_bytes=8 << 20),
        name="inv_local",
    )(spread, T["inv_z_hi"], T["inv_z_lo"], T["inv_y"])


def body(u_field, preact, cotangent, weights):
    shape = (IMGS, NY, NZ)
    partial = forward(u_field.reshape(shape), preact.reshape(shape), cotangent.reshape(shape))
    moved = lax.all_to_all(partial, "slab", split_axis=0, concat_axis=0, tiled=True)
    mine = lax.axis_index("dp")
    own, *away, back = middle(mine.reshape(1), moved.reshape(SLABS * 8, 128), weights)
    parts = [own]
    for other, piece in enumerate(away, 1):
        parts.append(lax.ppermute(piece, "dp", [(n, n ^ other) for n in range(4)]))
    spread = lax.all_to_all(back, "slab", split_axis=0, concat_axis=0, tiled=True)
    grad_weights = weight_grad(parts)
    field_grad = inverse(spread)
    return grad_weights, field_grad.reshape(1, PLANES, C, NY, NZ)


def solution(mesh):
    placed = (
        P("dp", "slab", None, None, None),
        P("dp", "slab", None, None, None),
        P("dp", "slab", None, None, None),
        P(None, "slab", None),
    )
    return jax.shard_map(
        body,
        mesh=mesh,
        in_specs=placed,
        out_specs=(P("dp", "slab", None), P("dp", "slab", None, None, None)),
        check_vma=False,
    )
```

```python
import itertools
import math

import jax
import jax.numpy as jnp
import numpy as np
from jax import lax
from jax.experimental import pallas as pl
from jax.experimental.pallas import tpu as pltpu
from jax.sharding import PartitionSpec as P

C = 32
NX = 128
NY = 128
NZ = 128
MX = 16
MY = 16
MZ = 16
SLABS = 64
PLANES = NX // SLABS
IMGS = PLANES * C
OWN = MY * MZ // SLABS
F32 = jnp.float32
BF16 = jnp.bfloat16
CUTS = (0, 24, 64)
OSTEP = 8
PAD = 132
IPAD = 36


def np_twiddles(length, freqs):
    product = (np.arange(length, dtype=np.int64)[:, None] * freqs[None, :]) % length
    angle = product.astype(np.float32) * np.float32(2.0 * math.pi / length)
    return np.cos(angle).astype(np.float32), np.sin(angle).astype(np.float32)


def signed(count):
    index = np.arange(count)
    return np.where(index < count // 2, index, index - count)


def split_np(table):
    high = table.astype(jnp.bfloat16)
    low = (table - high.astype(np.float32)).astype(jnp.bfloat16)
    return high, low


def make_tables():
    cx, sx = np_twiddles(NX, signed(MX))
    cy, sy = np_twiddles(NY, signed(MY))
    cz, sz = np_twiddles(NZ, np.arange(MZ))
    t = {}
    rows = np.concatenate([cy.T, sy.T], 0)
    t["fwd_y"] = np.concatenate(split_np(rows), 1)
    low_c = cz.astype(jnp.bfloat16).astype(np.float32)
    low_s = (-sz).astype(jnp.bfloat16).astype(np.float32)
    real = np.concatenate([low_c, low_s], 0).T
    imag = np.concatenate([low_s, -low_c], 0).T
    wz = np.stack([real.reshape(4, 4, 2 * NZ), imag.reshape(4, 4, 2 * NZ)], 1)
    t["fwd_z"] = wz.reshape(2 * MZ, 2 * NZ).astype(jnp.bfloat16)
    mode_scale = np.where(np.arange(MZ) == 0, 0.5, 1.0) / (NX * NY * NZ)
    per_row = np.broadcast_to(mode_scale.reshape(4, 1, 4), (4, 2, 4)).reshape(2 * MZ, 1)
    is_g = (np.arange(128) // C) % 2 == 1
    t["scale"] = np.where(is_g[None, :], per_row, 1.0).astype(np.float32)
    cxs, sxs = cx.reshape(SLABS, PLANES, MX), sx.reshape(SLABS, PLANES, MX)
    lx = np.zeros((PLANES, 2, MX, 2, SLABS), np.float32)
    for xx in range(PLANES):
        lx[xx, 0, :, 0] = cxs[:, xx].T
        lx[xx, 0, :, 1] = sxs[:, xx].T
        lx[xx, 1, :, 0] = -sxs[:, xx].T
        lx[xx, 1, :, 1] = cxs[:, xx].T
    t["fwd_x"] = np.concatenate(split_np(lx.reshape(PLANES * 2 * MX, 2 * SLABS)), 0)
    rep = np.zeros((128, 2, 4, C), np.float32)
    for part in range(2):
        for ch in range(C):
            rep[part * 64 + 32 + ch, part, :, ch] = 1.0
    t["rep_g"] = rep.reshape(128, 256).astype(jnp.bfloat16)
    rep = np.zeros((2, 2, 8, 4, 2, 4, C), np.float32)
    for part in range(2):
        for r in range(4):
            rep[part, 0, :, r, part, r, :] = 1.0
    t["rep_u"] = rep.reshape(128, 256).astype(jnp.bfloat16)
    red = np.zeros((2, 4, C, 4, 8, 4), np.float32)
    for r in range(4):
        red[0, r, :, 0, :, r] = 1.0
        red[1, r, :, 1, :, r] = 1.0
        red[1, r, :, 2, :, r] = -1.0
        red[0, r, :, 3, :, r] = 1.0
    t["red"] = red.reshape(256, 128).astype(jnp.bfloat16)
    ld = np.stack([cxs, sxs], 2).reshape(SLABS, PLANES * 2 * MX)
    high, low = split_np(ld)
    t["inv_x"] = np.concatenate([high, high, low], 1)
    tz = np.concatenate([cz.T, sz.T], 1)
    tz = np.broadcast_to(tz[None], (MY, MZ, 2 * NZ)).reshape(MY * MZ, 2 * NZ)
    high, low = split_np(tz)
    odd = (np.arange(MY * MZ) // MZ % 2 == 1)[:, None]
    t["inv_z"] = np.where(odd, low, high)
    ly = np.concatenate([cy, -sy], 1)
    high, low = split_np(ly)
    t["inv_y"] = np.concatenate([high, high, low], 1)
    return t


T = make_tables()


def split(value):
    high = value.astype(BF16)
    return high, (value - high.astype(F32)).astype(BF16)


def mm(a, b):
    return jnp.dot(a, b, preferred_element_type=F32)


def mm_nt(a, b):
    return lax.dot_general(a, b, (((1,), (1,)), ((), ())), preferred_element_type=F32)


HBM = pl.BlockSpec(memory_space=pltpu.HBM)


def forward_kernel(
    u_hbm, p_hbm, c_hbm, ty_hbm, wz_hbm, sc_hbm, o_hbm, o_ref, u_ref, p_ref, c_ref, ty_ref, wz_ref, sc_ref, xc_ref, xs_ref, sems, tsems, osems
):
    def chunk(src, dst, row, step):
        at = pl.ds(CUTS[step], CUTS[step + 1] - CUTS[step])
        return pltpu.make_async_copy(src.at[at], dst.at[at], sems.at[row, step])

    table = pltpu.make_async_copy(ty_hbm, ty_ref, tsems.at[0])
    late = [
        pltpu.make_async_copy(wz_hbm, wz_ref, tsems.at[1]),
        pltpu.make_async_copy(sc_hbm, sc_ref, tsems.at[2]),
    ]
    for step in range((len(CUTS) - 1)):
        chunk(p_hbm, p_ref, 1, step).start()
        chunk(c_hbm, c_ref, 2, step).start()
        chunk(u_hbm, u_ref, 0, step).start()
        if step == 0:
            table.start()
    for one in late:
        one.start()
    table.wait()

    def arrived(step):
        for row, (src, dst) in enumerate(((u_hbm, u_ref), (p_hbm, p_ref), (c_hbm, c_ref))):
            chunk(src, dst, row, step).wait()

    def slope_of(k):
        if True:
            arg = p_ref[k].astype(F32) * math.sqrt(0.5)
            bell = jnp.exp2((arg * (-math.log2(math.e))) * arg) * (2.0 / math.sqrt(math.pi))
            slope = (lax.erf(arg) + 1.0) + arg * bell
            c_ref[k] = (c_ref[k].astype(F32) * slope).astype(BF16)

    ty = ty_ref[...]

    def image(k):
        if True:
            both = jnp.concatenate([u_ref[k], c_ref[k]], axis=1)
            part = mm(ty, jnp.concatenate([both, both], axis=0))
            base = (k // C) * 64 + k % C
            xc_ref[pl.ds(base, MY, stride=PAD), :] = part[:16, :128]
            xs_ref[pl.ds(base, MY, stride=PAD), :] = part[16:, :128]
            xc_ref[pl.ds(base + 32, MY, stride=PAD), :] = part[:16, 128:]
            xs_ref[pl.ds(base + 32, MY, stride=PAD), :] = part[16:, 128:]

    for step in range(len(CUTS)):
        if step < len(CUTS) - 1:
            arrived(step)
        if step < len(CUTS) - 1:
            for k in range(CUTS[step], CUTS[step + 1]):
                slope_of(k)
                if k >= 2:
                    image(k - 2)
        else:
            image(62)
            image(63)
    for one in late:
        one.wait()
    wz = wz_ref[...]
    scale = sc_ref[...]

    def send(part):
        at = pl.ds(part * 16, 16)
        return pltpu.make_async_copy(o_ref.at[at], o_hbm.at[at], osems.at[part])

    for b in range(MY):
        rows = slice(b * PAD, b * PAD + 128)
        both = jnp.concatenate([xc_ref[rows, :].astype(BF16), xs_ref[rows, :].astype(BF16)], axis=1)
        res = mm_nt(wz, both)
        res = res * scale
        for q in range(4):
            o_ref[b * 4 + q] = res[q * 8 : (q + 1) * 8]
        if b % 4 == 3:
            send(b // 4).start()
    for part in range(4):
        send(part).wait()


def forward(u, pre, cot):
    big = pltpu.VMEM((IMGS, NY, NZ), BF16)
    flat = pltpu.VMEM((MY * PAD, 128), F32)
    return pl.pallas_call(
        forward_kernel,
        out_shape=jax.ShapeDtypeStruct((SLABS, 8, 128), F32),
        in_specs=[HBM] * 6,
        out_specs=HBM,
        scratch_shapes=[
            pltpu.VMEM((SLABS, 8, 128), F32),
            big,
            big,
            big,
            pltpu.VMEM((32, 256), BF16),
            pltpu.VMEM((32, 256), BF16),
            pltpu.VMEM((32, 128), F32),
            flat,
            flat,
            pltpu.SemaphoreType.DMA((3, (len(CUTS) - 1))),
            pltpu.SemaphoreType.DMA((3,)),
            pltpu.SemaphoreType.DMA((4,)),
        ],
        name="fwd_local",
    )(u, pre, cot, T["fwd_y"], T["fwd_z"], T["scale"])


def middle_kernel(
    mine_ref, m_ref, w_ref, lx_ref, rg_ref, red_ref, ld_ref, own0_ref, own1_ref, own2_ref, own3_ref, d_ref, wf_ref, own_ref, q_ref
):
    for a in range(MX):
        wf_ref[pl.ds(4 * a, 4), :] = w_ref[a].astype(F32)
    lx = lx_ref[...]
    lane = lax.broadcasted_iota(jnp.int32, (MX, 128), 1)
    left = lane < 64
    for cr in range(OWN):
        rhs = jnp.concatenate(
            [m_ref[pl.ds(cr, SLABS, stride=8), :], m_ref[pl.ds(4 + cr, SLABS, stride=8), :]], axis=0
        )
        hi, lo = split(rhs)
        res = mm(lx, hi)
        res = res[:64] + res[64:] + mm(lx[:64], lo)
        summed = res[:32] + pltpu.roll(res[32:], 64, 1)
        own_ref[pl.ds(cr, MX, stride=OWN), :] = jnp.where(
            left, summed[:16], pltpu.roll(summed[16:], 64, 1)
        )
    mine = mine_ref[0]
    for other, ref in enumerate((own0_ref, own1_ref, own2_ref, own3_ref)):
        ref[...] = own_ref[pl.ds(pl.multiple_of((mine ^ other) * 16, 16), 16), :]
    hi, lo = split(own_ref[...])
    rg = rg_ref[...]
    grep = mm(hi, rg) + mm(lo, rg)
    g_real, g_imag = grep[:, :128], grep[:, 128:]
    acc = jnp.zeros((MX * OWN, 128), F32)
    slot = (lax.broadcasted_iota(jnp.int32, (MX * OWN, 128), 1) // 4) % 8
    red = red_ref[...]
    for t in range(8):
        w_real = wf_ref[:, t * 128 : (t + 1) * 128]
        w_imag = wf_ref[:, 1024 + t * 128 : 1024 + (t + 1) * 128]
        rhi, rlo = split(w_real * g_real + w_imag * g_imag)
        ihi, ilo = split(w_real * g_imag - w_imag * g_real)
        res = mm(jnp.concatenate([rhi, ihi], axis=1), red)
        res += mm(jnp.concatenate([rlo, ilo], axis=1), red)
        acc = jnp.where(slot == t, res, acc)
    q_ref[...] = acc
    ld = ld_ref[...]
    for cr in range(OWN):
        q = q_ref[pl.ds(cr, MX, stride=OWN), :]
        r = pltpu.roll(q, 64, 1)
        zero = jnp.zeros_like(q)
        rhs = jnp.concatenate(
            [
                jnp.where(left, q, zero),
                jnp.where(left, r, zero),
                jnp.where(left, zero, r),
                jnp.where(left, zero, q),
            ],
            axis=0,
        )
        hi, lo = split(rhs)
        d_ref[pl.ds(cr, SLABS, stride=OWN), :] = mm(ld, jnp.concatenate([hi, lo, hi], axis=0))


def middle(mine, moved, weights):
    return pl.pallas_call(
        middle_kernel,
        out_shape=(jax.ShapeDtypeStruct((16, 128), F32),) * 4
        + (jax.ShapeDtypeStruct((SLABS * OWN, 128), F32),),
        in_specs=[pl.BlockSpec(memory_space=pltpu.SMEM)] + [pl.BlockSpec(memory_space=pltpu.VMEM)] * 6,
        scratch_shapes=[
            pltpu.VMEM((MX * OWN, 2048), F32),
            pltpu.VMEM((MX * OWN, 128), F32),
            pltpu.VMEM((MX * OWN, 128), F32),
        ],
        compiler_params=pltpu.CompilerParams(vmem_limit_bytes=8 << 20),
        name="middle",
    )(mine, moved, weights, T["fwd_x"], T["rep_g"], T["red"], T["inv_x"])


def weight_grad_kernel(s0_ref, s1_ref, s2_ref, s3_ref, rg_ref, ru_ref, o_ref):
    full = jnp.concatenate([s0_ref[...], s1_ref[...], s2_ref[...], s3_ref[...]], axis=0)
    hi, lo = split(full)
    rg = rg_ref[...]
    ru = ru_ref[...]
    grep = mm(hi, rg) + mm(lo, rg)
    g_real, g_imag = grep[:, :128], grep[:, 128:]
    slot = (lax.broadcasted_iota(jnp.int32, (64, 128), 1) // 4) % 8
    for t in range(8):
        hit, lot = split(jnp.where(slot == t, full, jnp.zeros_like(full)))
        urep = mm(hit, ru) + mm(lot, ru)
        u_real, u_imag = urep[:, :128], urep[:, 128:]
        real = g_real * u_real + g_imag * u_imag
        imag = g_imag * u_real - g_real * u_imag
        real = real[:16] + real[16:32] + real[32:48] + real[48:]
        imag = imag[:16] + imag[16:32] + imag[32:48] + imag[48:]
        for a in range(4):
            o_ref[a, :, t * 128 : (t + 1) * 128] = real[a * 4 : (a + 1) * 4]
            o_ref[a, :, 1024 + t * 128 : 1024 + (t + 1) * 128] = imag[a * 4 : (a + 1) * 4]


def weight_grad(parts):
    return pl.pallas_call(
        weight_grad_kernel,
        out_shape=jax.ShapeDtypeStruct((4, OWN, 2 * C * C), F32),
        compiler_params=pltpu.CompilerParams(vmem_limit_bytes=4 << 20),
        name="weight_grad",
    )(*parts, T["rep_g"], T["rep_u"])


def inverse_kernel(d_ref, tz_ref, ly_ref, o_hbm, o_ref, f_ref, osems):
    full = d_ref[...].astype(BF16)
    packed = []
    for odd in range(2):
        blocks = []
        for b in range(MY):
            at = (b // 2 * 2 + odd) * MZ
            blocks.append(full[at : at + MZ])
        packed.append(jnp.concatenate(blocks, axis=0).T)
    tz = tz_ref[...]
    group = lax.broadcasted_iota(jnp.int32, (128, 256), 1) // (2 * MZ)
    for b in range(MY):
        part = packed[b % 2]
        h = mm(jnp.where(group == b // 2, part, jnp.zeros_like(part)), tz)
        for xx in range(PLANES):
            real = h[xx * 64 : xx * 64 + 32]
            imag = h[xx * 64 + 32 : xx * 64 + 64]
            at = xx * C * IPAD + b
            f_ref[pl.ds(at, C, stride=IPAD), :] = real[:, :128] - imag[:, 128:]
            f_ref[pl.ds(at + 16, C, stride=IPAD), :] = real[:, 128:] + imag[:, :128]

    def send(step):
        at = pl.ds(step * OSTEP, OSTEP)
        return pltpu.make_async_copy(o_ref.at[at], o_hbm.at[at], osems.at[step])

    ly = ly_ref[...]
    for step in range(IMGS // OSTEP):
        for k in range(step * OSTEP, (step + 1) * OSTEP, 2):
            at = k * IPAD
            block = f_ref[pl.ds(at, 72), :]
            pair = jnp.concatenate([block[:32], block[36:68]], axis=1)
            hi, lo = split(pair)
            res = mm(ly, jnp.concatenate([hi, lo, hi], axis=0)).astype(BF16)
            o_ref[k] = res[:, :128]
            o_ref[k + 1] = res[:, 128:]
        send(step).start()
    for step in range(IMGS // OSTEP):
        send(step).wait()


def inverse(spread):
    return pl.pallas_call(
        inverse_kernel,
        out_shape=jax.ShapeDtypeStruct((IMGS, NY, NZ), BF16),
        in_specs=[pl.BlockSpec(memory_space=pltpu.VMEM)] * 3,
        out_specs=HBM,
        scratch_shapes=[
            pltpu.VMEM((IMGS, NY, NZ), BF16),
            pltpu.VMEM((IMGS * IPAD, 128), F32),
            pltpu.SemaphoreType.DMA((IMGS // OSTEP,)),
        ],
        compiler_params=pltpu.CompilerParams(vmem_limit_bytes=8 << 20),
        name="inv_local",
    )(spread, T["inv_z"], T["inv_y"])


def body(u_field, preact, cotangent, weights):
    shape = (IMGS, NY, NZ)
    partial = forward(u_field.reshape(shape), preact.reshape(shape), cotangent.reshape(shape))
    moved = lax.all_to_all(partial, "slab", split_axis=0, concat_axis=0, tiled=True)
    mine = lax.axis_index("dp")
    own, *away, back = middle(mine.reshape(1), moved.reshape(SLABS * 8, 128), weights)
    parts = [own]
    for other, piece in enumerate(away, 1):
        parts.append(lax.ppermute(piece, "dp", [(n, n ^ other) for n in range(4)]))
    spread = lax.all_to_all(back, "slab", split_axis=0, concat_axis=0, tiled=True)
    field_grad = inverse(spread)
    parts, field_grad = lax.optimization_barrier((parts, field_grad))
    grad_weights = weight_grad(parts)
    return grad_weights, field_grad.reshape(1, PLANES, C, NY, NZ)


def solution(mesh):
    placed = (
        P("dp", "slab", None, None, None),
        P("dp", "slab", None, None, None),
        P("dp", "slab", None, None, None),
        P(None, "slab", None),
    )
    return jax.shard_map(
        body,
        mesh=mesh,
        in_specs=placed,
        out_specs=(P("dp", "slab", None), P("dp", "slab", None, None, None)),
        check_vma=False,
    )
```

```python
import itertools
import math

import jax
import jax.numpy as jnp
import numpy as np
from jax import lax
from jax.experimental import pallas as pl
from jax.experimental.pallas import tpu as pltpu
from jax.sharding import PartitionSpec as P

C = 32
NX = 128
NY = 128
NZ = 128
MX = 16
MY = 16
MZ = 16
SLABS = 64
PLANES = NX // SLABS
IMGS = PLANES * C
OWN = MY * MZ // SLABS
F32 = jnp.float32
BF16 = jnp.bfloat16
AHEAD = 2
OTHERS = (0, 2, 3, 1)
CUTS = (0, 16, 40, 64)
OSTEP = 8
PAD = 132
IPAD = 36


def np_twiddles(length, freqs):
    product = (np.arange(length, dtype=np.int64)[:, None] * freqs[None, :]) % length
    angle = product.astype(np.float32) * np.float32(2.0 * math.pi / length)
    return np.cos(angle).astype(np.float32), np.sin(angle).astype(np.float32)


def signed(count):
    index = np.arange(count)
    return np.where(index < count // 2, index, index - count)


def split_np(table):
    high = table.astype(jnp.bfloat16)
    low = (table - high.astype(np.float32)).astype(jnp.bfloat16)
    return high, low


def make_tables():
    cx, sx = np_twiddles(NX, signed(MX))
    cy, sy = np_twiddles(NY, signed(MY))
    cz, sz = np_twiddles(NZ, np.arange(MZ))
    t = {}
    rows = np.concatenate([cy.T, sy.T], 0)
    t["fwd_y"] = np.concatenate(split_np(rows), 1)
    low_c = cz.astype(jnp.bfloat16).astype(np.float32)
    low_s = (-sz).astype(jnp.bfloat16).astype(np.float32)
    real = np.concatenate([low_c, low_s], 0).T
    imag = np.concatenate([low_s, -low_c], 0).T
    wz = np.stack([real.reshape(4, 4, 2 * NZ), imag.reshape(4, 4, 2 * NZ)], 1)
    t["fwd_z"] = wz.reshape(2 * MZ, 2 * NZ).astype(jnp.bfloat16)
    mode_scale = np.where(np.arange(MZ) == 0, 0.5, 1.0) / (NX * NY * NZ)
    per_row = np.broadcast_to(mode_scale.reshape(4, 1, 4), (4, 2, 4)).reshape(2 * MZ, 1)
    is_g = (np.arange(128) // C) % 2 == 1
    t["scale"] = np.where(is_g[None, :], per_row, 1.0).astype(np.float32)
    cxs, sxs = cx.reshape(SLABS, PLANES, MX), sx.reshape(SLABS, PLANES, MX)
    lx = np.zeros((PLANES, 2, MX, 2, SLABS), np.float32)
    for xx in range(PLANES):
        lx[xx, 0, :, 0] = cxs[:, xx].T
        lx[xx, 0, :, 1] = sxs[:, xx].T
        lx[xx, 1, :, 0] = -sxs[:, xx].T
        lx[xx, 1, :, 1] = cxs[:, xx].T
    t["fwd_x"] = np.concatenate(split_np(lx.reshape(PLANES * 2 * MX, 2 * SLABS)), 0)
    rep = np.zeros((128, 2, 4, C), np.float32)
    for part in range(2):
        for ch in range(C):
            rep[part * 64 + 32 + ch, part, :, ch] = 1.0
    t["rep_g"] = rep.reshape(128, 256).astype(jnp.bfloat16)
    rep = np.zeros((2, 2, 8, 4, 2, 4, C), np.float32)
    for part in range(2):
        for r in range(4):
            rep[part, 0, :, r, part, r, :] = 1.0
    t["rep_u"] = rep.reshape(128, 256).astype(jnp.bfloat16)
    red = np.zeros((2, 4, C, 4, 8, 4), np.float32)
    for r in range(4):
        red[0, r, :, 0, :, r] = 1.0
        red[1, r, :, 1, :, r] = 1.0
        red[1, r, :, 2, :, r] = -1.0
        red[0, r, :, 3, :, r] = 1.0
    t["red"] = red.reshape(256, 128).astype(jnp.bfloat16)
    ld = np.stack([cxs, sxs], 2).reshape(SLABS, PLANES * 2 * MX)
    high, low = split_np(ld)
    t["inv_x"] = np.concatenate([high, high, low], 1)
    tz = np.concatenate([cz.T, sz.T], 1)
    tz = np.broadcast_to(tz[None], (MY, MZ, 2 * NZ)).reshape(MY * MZ, 2 * NZ)
    high, low = split_np(tz)
    odd = (np.arange(MY * MZ) // MZ % 2 == 1)[:, None]
    t["inv_z"] = np.where(odd, low, high)
    ly = np.concatenate([cy, -sy], 1)
    high, low = split_np(ly)
    t["inv_y"] = np.concatenate([high, high, low], 1)
    return t


T = make_tables()


def split(value):
    high = value.astype(BF16)
    return high, (value - high.astype(F32)).astype(BF16)


def mm(a, b):
    return jnp.dot(a, b, preferred_element_type=F32)


def mm_nt(a, b):
    return lax.dot_general(a, b, (((1,), (1,)), ((), ())), preferred_element_type=F32)


HBM = pl.BlockSpec(memory_space=pltpu.HBM)


def forward_kernel(
    u_hbm, p_hbm, c_hbm, ty_hbm, wz_hbm, sc_hbm, o_hbm, o_ref, u_ref, p_ref, c_ref, ty_ref, wz_ref, sc_ref, xc_ref, xs_ref, sems, tsems, osems
):
    def chunk(src, dst, row, step):
        at = pl.ds(CUTS[step], CUTS[step + 1] - CUTS[step])
        return pltpu.make_async_copy(src.at[at], dst.at[at], sems.at[row, step])

    table = pltpu.make_async_copy(ty_hbm, ty_ref, tsems.at[0])
    late = [
        pltpu.make_async_copy(wz_hbm, wz_ref, tsems.at[1]),
        pltpu.make_async_copy(sc_hbm, sc_ref, tsems.at[2]),
    ]
    def fetch(step):
        chunk(p_hbm, p_ref, 1, step).start()
        chunk(c_hbm, c_ref, 2, step).start()
        chunk(u_hbm, u_ref, 0, step).start()

    fetch(0)
    table.start()
    for step in range(1, AHEAD):
        fetch(step)
    for one in late:
        one.start()
    table.wait()

    def arrived(step):
        for row, (src, dst) in enumerate(((u_hbm, u_ref), (p_hbm, p_ref), (c_hbm, c_ref))):
            chunk(src, dst, row, step).wait()

    def slope_of(k):
        if True:
            arg = p_ref[k].astype(F32) * math.sqrt(0.5)
            bell = jnp.exp2((arg * (-math.log2(math.e))) * arg) * (2.0 / math.sqrt(math.pi))
            slope = (lax.erf(arg) + 1.0) + arg * bell
            c_ref[k] = (c_ref[k].astype(F32) * slope).astype(BF16)

    ty = ty_ref[...]

    def image(k):
        if True:
            both = jnp.concatenate([u_ref[k], c_ref[k]], axis=1)
            part = mm(ty, jnp.concatenate([both, both], axis=0))
            base = (k // C) * 64 + k % C
            xc_ref[pl.ds(base, MY, stride=PAD), :] = part[:16, :128]
            xs_ref[pl.ds(base, MY, stride=PAD), :] = part[16:, :128]
            xc_ref[pl.ds(base + 32, MY, stride=PAD), :] = part[:16, 128:]
            xs_ref[pl.ds(base + 32, MY, stride=PAD), :] = part[16:, 128:]

    for step in range(len(CUTS)):
        if step < len(CUTS) - 1:
            arrived(step)
            if step + AHEAD < len(CUTS) - 1:
                fetch(step + AHEAD)
        if step < len(CUTS) - 1:
            for k in range(CUTS[step], CUTS[step + 1]):
                slope_of(k)
                if k >= 2:
                    image(k - 2)
        else:
            image(62)
            image(63)
    for one in late:
        one.wait()
    wz = wz_ref[...]
    scale = sc_ref[...]

    def send(part):
        at = pl.ds(part * 16, 16)
        return pltpu.make_async_copy(o_ref.at[at], o_hbm.at[at], osems.at[part])

    for b in range(MY):
        rows = slice(b * PAD, b * PAD + 128)
        both = jnp.concatenate([xc_ref[rows, :].astype(BF16), xs_ref[rows, :].astype(BF16)], axis=1)
        res = mm_nt(wz, both)
        res = res * scale
        for q in range(4):
            o_ref[b * 4 + q] = res[q * 8 : (q + 1) * 8]
        if b % 4 == 3:
            send(b // 4).start()
    for part in range(4):
        send(part).wait()


def forward(u, pre, cot):
    big = pltpu.VMEM((IMGS, NY, NZ), BF16)
    flat = pltpu.VMEM((MY * PAD, 128), F32)
    return pl.pallas_call(
        forward_kernel,
        out_shape=jax.ShapeDtypeStruct((SLABS, 8, 128), F32),
        in_specs=[HBM] * 6,
        out_specs=HBM,
        scratch_shapes=[
            pltpu.VMEM((SLABS, 8, 128), F32),
            big,
            big,
            big,
            pltpu.VMEM((32, 256), BF16),
            pltpu.VMEM((32, 256), BF16),
            pltpu.VMEM((32, 128), F32),
            flat,
            flat,
            pltpu.SemaphoreType.DMA((3, (len(CUTS) - 1))),
            pltpu.SemaphoreType.DMA((3,)),
            pltpu.SemaphoreType.DMA((4,)),
        ],
        name="fwd_local",
    )(u, pre, cot, T["fwd_y"], T["fwd_z"], T["scale"])


def widen_kernel(w_ref, o_ref):
    for a in range(MX):
        o_ref[pl.ds(4 * a, 4), :] = w_ref[a].astype(F32)


def widen(weights):
    return pl.pallas_call(
        widen_kernel,
        out_shape=jax.ShapeDtypeStruct((MX * OWN, 2 * C * C), F32),
        in_specs=[pl.BlockSpec(memory_space=pltpu.VMEM)],
        out_specs=pl.BlockSpec(memory_space=pltpu.VMEM),
        compiler_params=pltpu.CompilerParams(vmem_limit_bytes=4 << 20),
        name="widen",
    )(weights)


def middle_kernel(
    mine_ref, m_ref, wf_ref, lx_ref, rg_ref, red_ref, ld_ref, own0_ref, own1_ref, own2_ref, own3_ref, d_ref, own_ref, q_ref
):
    lx = lx_ref[...]
    lane = lax.broadcasted_iota(jnp.int32, (MX, 128), 1)
    left = lane < 64
    for cr in range(OWN):
        rhs = jnp.concatenate(
            [m_ref[pl.ds(cr, SLABS, stride=8), :], m_ref[pl.ds(4 + cr, SLABS, stride=8), :]], axis=0
        )
        hi, lo = split(rhs)
        res = mm(lx, hi)
        res = res[:64] + res[64:] + mm(lx[:64], lo)
        summed = res[:32] + pltpu.roll(res[32:], 64, 1)
        own_ref[pl.ds(cr, MX, stride=OWN), :] = jnp.where(
            left, summed[:16], pltpu.roll(summed[16:], 64, 1)
        )
    mine = mine_ref[0]
    for other, ref in zip(OTHERS, (own0_ref, own1_ref, own2_ref, own3_ref)):
        ref[...] = own_ref[pl.ds(pl.multiple_of((mine ^ other) * 16, 16), 16), :]
    hi, lo = split(own_ref[...])
    rg = rg_ref[...]
    grep = mm(hi, rg) + mm(lo, rg)
    g_real, g_imag = grep[:, :128], grep[:, 128:]
    acc = jnp.zeros((MX * OWN, 128), F32)
    slot = (lax.broadcasted_iota(jnp.int32, (MX * OWN, 128), 1) // 4) % 8
    red = red_ref[...]
    for t in range(8):
        w_real = wf_ref[:, t * 128 : (t + 1) * 128]
        w_imag = wf_ref[:, 1024 + t * 128 : 1024 + (t + 1) * 128]
        rhi, rlo = split(w_real * g_real + w_imag * g_imag)
        ihi, ilo = split(w_real * g_imag - w_imag * g_real)
        res = mm(jnp.concatenate([rhi, ihi], axis=1), red)
        res += mm(jnp.concatenate([rlo, ilo], axis=1), red)
        acc = jnp.where(slot == t, res, acc)
    q_ref[...] = acc
    ld = ld_ref[...]
    for cr in range(OWN):
        q = q_ref[pl.ds(cr, MX, stride=OWN), :]
        r = pltpu.roll(q, 64, 1)
        zero = jnp.zeros_like(q)
        rhs = jnp.concatenate(
            [
                jnp.where(left, q, zero),
                jnp.where(left, r, zero),
                jnp.where(left, zero, r),
                jnp.where(left, zero, q),
            ],
            axis=0,
        )
        hi, lo = split(rhs)
        d_ref[pl.ds(cr, SLABS, stride=OWN), :] = mm(ld, jnp.concatenate([hi, lo, hi], axis=0))


def middle(mine, moved, weights):
    return pl.pallas_call(
        middle_kernel,
        out_shape=(jax.ShapeDtypeStruct((16, 128), F32),) * 4
        + (jax.ShapeDtypeStruct((SLABS * OWN, 128), F32),),
        in_specs=[pl.BlockSpec(memory_space=pltpu.SMEM)] + [pl.BlockSpec(memory_space=pltpu.VMEM)] * 6,
        scratch_shapes=[
            pltpu.VMEM((MX * OWN, 128), F32),
            pltpu.VMEM((MX * OWN, 128), F32),
        ],
        compiler_params=pltpu.CompilerParams(vmem_limit_bytes=8 << 20),
        name="middle",
    )(mine, moved, weights, T["fwd_x"], T["rep_g"], T["red"], T["inv_x"])


def weight_grad(parts, rg_ref, ru_ref, o_ref):
    full = jnp.concatenate([part[...] for part in parts], axis=0)
    hi, lo = split(full)
    rg = rg_ref[...]
    ru = ru_ref[...]
    grep = mm(hi, rg) + mm(lo, rg)
    g_real, g_imag = grep[:, :128], grep[:, 128:]
    slot = (lax.broadcasted_iota(jnp.int32, (64, 128), 1) // 4) % 8
    for t in range(8):
        hit, lot = split(jnp.where(slot == t, full, jnp.zeros_like(full)))
        urep = mm(hit, ru) + mm(lot, ru)
        u_real, u_imag = urep[:, :128], urep[:, 128:]
        real = g_real * u_real + g_imag * u_imag
        imag = g_imag * u_real - g_real * u_imag
        real = real[:16] + real[16:32] + real[32:48] + real[48:]
        imag = imag[:16] + imag[16:32] + imag[32:48] + imag[48:]
        for a in range(4):
            o_ref[a, :, t * 128 : (t + 1) * 128] = real[a * 4 : (a + 1) * 4]
            o_ref[a, :, 1024 + t * 128 : 1024 + (t + 1) * 128] = imag[a * 4 : (a + 1) * 4]


def inverse_kernel(
    d_ref, tz_ref, ly_ref, s0_ref, s1_ref, s2_ref, s3_ref, rg_ref, ru_ref, o_hbm, gw_hbm, o_ref, gw_ref, f_ref, osems, gsem
):
    full = d_ref[...].astype(BF16)
    packed = []
    for odd in range(2):
        blocks = []
        for b in range(MY):
            at = (b // 2 * 2 + odd) * MZ
            blocks.append(full[at : at + MZ])
        packed.append(jnp.concatenate(blocks, axis=0).T)
    tz = tz_ref[...]
    group = lax.broadcasted_iota(jnp.int32, (128, 256), 1) // (2 * MZ)
    for b in range(MY):
        part = packed[b % 2]
        h = mm(jnp.where(group == b // 2, part, jnp.zeros_like(part)), tz)
        for xx in range(PLANES):
            real = h[xx * 64 : xx * 64 + 32]
            imag = h[xx * 64 + 32 : xx * 64 + 64]
            at = xx * C * IPAD + b
            f_ref[pl.ds(at, C, stride=IPAD), :] = real[:, :128] - imag[:, 128:]
            f_ref[pl.ds(at + 16, C, stride=IPAD), :] = real[:, 128:] + imag[:, :128]

    def send(step):
        at = pl.ds(step * OSTEP, OSTEP)
        return pltpu.make_async_copy(o_ref.at[at], o_hbm.at[at], osems.at[step])

    weight_grad((s0_ref, s1_ref, s2_ref, s3_ref), rg_ref, ru_ref, gw_ref)
    store = pltpu.make_async_copy(gw_ref, gw_hbm, gsem)
    store.start()
    ly = ly_ref[...]
    for step in range(IMGS // OSTEP):
        for k in range(step * OSTEP, (step + 1) * OSTEP, 2):
            at = k * IPAD
            block = f_ref[pl.ds(at, 72), :]
            pair = jnp.concatenate([block[:32], block[36:68]], axis=1)
            hi, lo = split(pair)
            res = mm(ly, jnp.concatenate([hi, lo, hi], axis=0)).astype(BF16)
            o_ref[k] = res[:, :128]
            o_ref[k + 1] = res[:, 128:]
        send(step).start()
    store.wait()
    for step in range(IMGS // OSTEP):
        send(step).wait()


def inverse(spread, parts):
    return pl.pallas_call(
        inverse_kernel,
        out_shape=(
            jax.ShapeDtypeStruct((IMGS, NY, NZ), BF16),
            jax.ShapeDtypeStruct((4, OWN, 2 * C * C), F32),
        ),
        in_specs=[pl.BlockSpec(memory_space=pltpu.VMEM)] * 9,
        out_specs=(HBM, HBM),
        scratch_shapes=[
            pltpu.VMEM((IMGS, NY, NZ), BF16),
            pltpu.VMEM((4, OWN, 2 * C * C), F32),
            pltpu.VMEM((IMGS * IPAD, 128), F32),
            pltpu.SemaphoreType.DMA((IMGS // OSTEP,)),
            pltpu.SemaphoreType.DMA,
        ],
        compiler_params=pltpu.CompilerParams(vmem_limit_bytes=8 << 20),
        name="inv_local",
    )(spread, T["inv_z"], T["inv_y"], *parts, T["rep_g"], T["rep_u"])


def body(u_field, preact, cotangent, weights):
    shape = (IMGS, NY, NZ)
    partial = forward(u_field.reshape(shape), preact.reshape(shape), cotangent.reshape(shape))
    partial, weights = lax.optimization_barrier((partial, weights))
    moved = lax.all_to_all(partial, "slab", split_axis=0, concat_axis=0, tiled=True)
    wide = widen(weights)
    mine = lax.axis_index("dp")
    *pieces, back = middle(mine.reshape(1), moved.reshape(SLABS * 8, 128), wide)
    for at, other in enumerate(OTHERS):
        if other:
            pieces[at] = lax.ppermute(pieces[at], "dp", [(n, n ^ other) for n in range(4)])
    spread = lax.all_to_all(back, "slab", split_axis=0, concat_axis=0, tiled=True)
    field_grad, grad_weights = inverse(spread, pieces)
    return grad_weights, field_grad.reshape(1, PLANES, C, NY, NZ)


def solution(mesh):
    placed = (
        P("dp", "slab", None, None, None),
        P("dp", "slab", None, None, None),
        P("dp", "slab", None, None, None),
        P(None, "slab", None),
    )
    return jax.shard_map(
        body,
        mesh=mesh,
        in_specs=placed,
        out_specs=(P("dp", "slab", None), P("dp", "slab", None, None, None)),
        check_vma=False,
    )
```

```python
import itertools
import math

import jax
import jax.numpy as jnp
import numpy as np
from jax import lax
from jax.experimental import pallas as pl
from jax.experimental.pallas import tpu as pltpu
from jax.sharding import PartitionSpec as P

C = 32
NX = 128
NY = 128
NZ = 128
MX = 16
MY = 16
MZ = 16
SLABS = 64
PLANES = NX // SLABS
IMGS = PLANES * C
OWN = MY * MZ // SLABS
F32 = jnp.float32
BF16 = jnp.bfloat16
AHEAD = 2
OTHERS = (0, 2, 3, 1)
TURN = 52
ORDER = [[n ^ TURN for n in range(SLABS)]]
CUTS = (0, 16, 40, 64)
OSTEP = 8
ZB = 2
PAD = 132
IPAD = 36


def np_twiddles(length, freqs):
    product = (np.arange(length, dtype=np.int64)[:, None] * freqs[None, :]) % length
    angle = product.astype(np.float32) * np.float32(2.0 * math.pi / length)
    return np.cos(angle).astype(np.float32), np.sin(angle).astype(np.float32)


def signed(count):
    index = np.arange(count)
    return np.where(index < count // 2, index, index - count)


def split_np(table):
    high = table.astype(jnp.bfloat16)
    low = (table - high.astype(np.float32)).astype(jnp.bfloat16)
    return high, low


def make_tables():
    cx, sx = np_twiddles(NX, signed(MX))
    cy, sy = np_twiddles(NY, signed(MY))
    cz, sz = np_twiddles(NZ, np.arange(MZ))
    t = {}
    rows = np.concatenate([cy.T, sy.T], 0)
    t["fwd_y"] = np.concatenate(split_np(rows), 1)
    low_c = cz.astype(jnp.bfloat16).astype(np.float32)
    low_s = (-sz).astype(jnp.bfloat16).astype(np.float32)
    real = np.concatenate([low_c, low_s], 0).T
    imag = np.concatenate([low_s, -low_c], 0).T
    wz = np.stack([real.reshape(4, 4, 2 * NZ), imag.reshape(4, 4, 2 * NZ)], 1)
    t["fwd_z"] = wz.reshape(2 * MZ, 2 * NZ).astype(jnp.bfloat16)
    mode_scale = np.where(np.arange(MZ) == 0, 0.5, 1.0) / (NX * NY * NZ)
    per_row = np.broadcast_to(mode_scale.reshape(4, 1, 4), (4, 2, 4)).reshape(2 * MZ, 1)
    is_g = (np.arange(128) // C) % 2 == 1
    t["scale"] = np.where(is_g[None, :], per_row, 1.0).astype(np.float32)
    cxs, sxs = cx.reshape(SLABS, PLANES, MX)[ORDER[0]], sx.reshape(SLABS, PLANES, MX)[ORDER[0]]
    lx = np.zeros((PLANES, 2, MX, 2, SLABS), np.float32)
    for xx in range(PLANES):
        lx[xx, 0, :, 0] = cxs[:, xx].T
        lx[xx, 0, :, 1] = sxs[:, xx].T
        lx[xx, 1, :, 0] = -sxs[:, xx].T
        lx[xx, 1, :, 1] = cxs[:, xx].T
    t["fwd_x"] = np.concatenate(split_np(lx.reshape(PLANES * 2 * MX, 2 * SLABS)), 0)
    rep = np.zeros((128, 2, 4, C), np.float32)
    for part in range(2):
        for ch in range(C):
            rep[part * 64 + 32 + ch, part, :, ch] = 1.0
    t["rep_g"] = rep.reshape(128, 256).astype(jnp.bfloat16)
    rep = np.zeros((2, 2, 8, 4, 2, 4, C), np.float32)
    for part in range(2):
        for r in range(4):
            rep[part, 0, :, r, part, r, :] = 1.0
    t["rep_u"] = rep.reshape(128, 256).astype(jnp.bfloat16)
    red = np.zeros((2, 4, C, 4, 8, 4), np.float32)
    for r in range(4):
        red[0, r, :, 0, :, r] = 1.0
        red[1, r, :, 1, :, r] = 1.0
        red[1, r, :, 2, :, r] = -1.0
        red[0, r, :, 3, :, r] = 1.0
    t["red"] = red.reshape(256, 128).astype(jnp.bfloat16)
    ld = np.stack([cxs, sxs], 2).reshape(SLABS, PLANES * 2 * MX)
    high, low = split_np(ld)
    t["inv_x"] = np.concatenate([high, high, low], 1)
    tz = np.stack([np.concatenate([cz.T, sz.T], 1), np.concatenate([-sz.T, cz.T], 1)])
    tz = np.broadcast_to(tz[:, None], (2, 8, MZ, 2 * NZ)).reshape(256, 2 * NZ)
    high, low = split_np(tz)
    odd = (np.arange(256) // MZ % 2 == 1)[:, None]
    t["inv_z"] = np.where(odd, low, high)
    ly = np.concatenate([cy, -sy], 1)
    high, low = split_np(ly)
    t["inv_y"] = np.concatenate([high, high, low], 1)
    return t


T = make_tables()


def split(value):
    high = value.astype(BF16)
    return high, (value - high.astype(F32)).astype(BF16)


def mm(a, b):
    return jnp.dot(a, b, preferred_element_type=F32)


def mm_nt(a, b):
    return lax.dot_general(a, b, (((1,), (1,)), ((), ())), preferred_element_type=F32)


HBM = pl.BlockSpec(memory_space=pltpu.HBM)


def forward_kernel(
    u_hbm, p_hbm, c_hbm, ty_hbm, wz_hbm, sc_hbm, o_hbm, o_ref, u_ref, p_ref, c_ref, ty_ref, wz_ref, sc_ref, xc_ref, xs_ref, sems, tsems, osems
):
    def chunk(src, dst, row, step):
        at = pl.ds(CUTS[step], CUTS[step + 1] - CUTS[step])
        return pltpu.make_async_copy(src.at[at], dst.at[at], sems.at[row, step])

    table = pltpu.make_async_copy(ty_hbm, ty_ref, tsems.at[0])
    late = [
        pltpu.make_async_copy(wz_hbm, wz_ref, tsems.at[1]),
        pltpu.make_async_copy(sc_hbm, sc_ref, tsems.at[2]),
    ]
    def fetch(step):
        chunk(p_hbm, p_ref, 1, step).start()
        chunk(c_hbm, c_ref, 2, step).start()
        chunk(u_hbm, u_ref, 0, step).start()

    fetch(0)
    table.start()
    for step in range(1, AHEAD):
        fetch(step)
    for one in late:
        one.start()
    table.wait()

    def arrived(step):
        for row, (src, dst) in enumerate(((u_hbm, u_ref), (p_hbm, p_ref), (c_hbm, c_ref))):
            chunk(src, dst, row, step).wait()

    def slope_of(k):
        if True:
            arg = p_ref[k].astype(F32) * math.sqrt(0.5)
            bell = jnp.exp2((arg * (-math.log2(math.e))) * arg) * (2.0 / math.sqrt(math.pi))
            slope = (lax.erf(arg) + 1.0) + arg * bell
            c_ref[k] = (c_ref[k].astype(F32) * slope).astype(BF16)

    ty = ty_ref[...]

    def image(k):
        if True:
            both = jnp.concatenate([u_ref[k], c_ref[k]], axis=1)
            part = mm(ty, jnp.concatenate([both, both], axis=0))
            base = (k // C) * 64 + k % C
            xc_ref[pl.ds(base, MY, stride=PAD), :] = part[:16, :128]
            xs_ref[pl.ds(base, MY, stride=PAD), :] = part[16:, :128]
            xc_ref[pl.ds(base + 32, MY, stride=PAD), :] = part[:16, 128:]
            xs_ref[pl.ds(base + 32, MY, stride=PAD), :] = part[16:, 128:]

    for step in range(len(CUTS)):
        if step < len(CUTS) - 1:
            arrived(step)
            if step + AHEAD < len(CUTS) - 1:
                fetch(step + AHEAD)
        if step < len(CUTS) - 1:
            for k in range(CUTS[step], CUTS[step + 1]):
                slope_of(k)
                if k >= 2:
                    image(k - 2)
        else:
            image(62)
            image(63)
    for one in late:
        one.wait()
    wz = wz_ref[...]
    scale = sc_ref[...]

    def send(part):
        at = pl.ds(part * 16, 16)
        return pltpu.make_async_copy(o_ref.at[at], o_hbm.at[at], osems.at[part])

    for b in range(MY):
        rows = slice(b * PAD, b * PAD + 128)
        both = jnp.concatenate([xc_ref[rows, :].astype(BF16), xs_ref[rows, :].astype(BF16)], axis=1)
        res = mm_nt(wz, both)
        res = res * scale
        for q in range(4):
            o_ref[(b * 4 + q) ^ TURN] = res[q * 8 : (q + 1) * 8]
        if b % 4 == 3:
            send(b // 4 ^ TURN // 16).start()
    for part in range(4):
        send(part).wait()


def forward(u, pre, cot):
    big = pltpu.VMEM((IMGS, NY, NZ), BF16)
    flat = pltpu.VMEM((MY * PAD, 128), F32)
    return pl.pallas_call(
        forward_kernel,
        out_shape=jax.ShapeDtypeStruct((SLABS, 8, 128), F32),
        in_specs=[HBM] * 6,
        out_specs=HBM,
        scratch_shapes=[
            pltpu.VMEM((SLABS, 8, 128), F32),
            big,
            big,
            big,
            pltpu.VMEM((32, 256), BF16),
            pltpu.VMEM((32, 256), BF16),
            pltpu.VMEM((32, 128), F32),
            flat,
            flat,
            pltpu.SemaphoreType.DMA((3, (len(CUTS) - 1))),
            pltpu.SemaphoreType.DMA((3,)),
            pltpu.SemaphoreType.DMA((4,)),
        ],
        name="fwd_local",
    )(u, pre, cot, T["fwd_y"], T["fwd_z"], T["scale"])


def widen_kernel(w_ref, o_ref):
    for a in range(MX):
        o_ref[pl.ds(4 * a, 4), :] = w_ref[a].astype(F32)


def widen(weights):
    return pl.pallas_call(
        widen_kernel,
        out_shape=jax.ShapeDtypeStruct((MX * OWN, 2 * C * C), F32),
        in_specs=[pl.BlockSpec(memory_space=pltpu.VMEM)],
        out_specs=pl.BlockSpec(memory_space=pltpu.VMEM),
        compiler_params=pltpu.CompilerParams(vmem_limit_bytes=4 << 20),
        name="widen",
    )(weights)


def middle_kernel(
    mine_ref, m_ref, wf_ref, lx_ref, rg_ref, red_ref, ld_ref, own0_ref, own1_ref, own2_ref, own3_ref, d_ref, own_ref, q_ref
):
    lx = lx_ref[...]
    lane = lax.broadcasted_iota(jnp.int32, (MX, 128), 1)
    left = lane < 64
    for cr in range(OWN):
        rhs = jnp.concatenate(
            [m_ref[pl.ds(cr, SLABS, stride=8), :], m_ref[pl.ds(4 + cr, SLABS, stride=8), :]], axis=0
        )
        hi, lo = split(rhs)
        res = mm(lx, hi)
        res = res[:64] + res[64:] + mm(lx[:64], lo)
        summed = res[:32] + pltpu.roll(res[32:], 64, 1)
        own_ref[pl.ds(cr, MX, stride=OWN), :] = jnp.where(
            left, summed[:16], pltpu.roll(summed[16:], 64, 1)
        )
    mine = mine_ref[...]
    quarter = [own_ref[c * 16 : (c + 1) * 16, :] for c in range(4)]
    for other, ref in zip(OTHERS, (own0_ref, own1_ref, own2_ref, own3_ref)):
        piece = quarter[3 ^ other]
        for c in range(3):
            piece = jnp.where(mine == c, quarter[c ^ other], piece)
        ref[...] = piece
    hi, lo = split(own_ref[...])
    rg = rg_ref[...]
    grep = mm(hi, rg) + mm(lo, rg)
    g_real, g_imag = grep[:, :128], grep[:, 128:]
    acc = jnp.zeros((MX * OWN, 128), F32)
    slot = (lax.broadcasted_iota(jnp.int32, (MX * OWN, 128), 1) // 4) % 8
    red = red_ref[...]
    for t in range(8):
        w_real = wf_ref[:, t * 128 : (t + 1) * 128]
        w_imag = wf_ref[:, 1024 + t * 128 : 1024 + (t + 1) * 128]
        rhi, rlo = split(w_real * g_real + w_imag * g_imag)
        ihi, ilo = split(w_real * g_imag - w_imag * g_real)
        res = mm(jnp.concatenate([rhi, ihi], axis=1), red)
        res += mm(jnp.concatenate([rlo, ilo], axis=1), red)
        acc = jnp.where(slot == t, res, acc)
    q_ref[...] = acc
    ld = ld_ref[...]
    for cr in range(OWN):
        q = q_ref[pl.ds(cr, MX, stride=OWN), :]
        r = pltpu.roll(q, 64, 1)
        zero = jnp.zeros_like(q)
        rhs = jnp.concatenate(
            [
                jnp.where(left, q, zero),
                jnp.where(left, r, zero),
                jnp.where(left, zero, r),
                jnp.where(left, zero, q),
            ],
            axis=0,
        )
        hi, lo = split(rhs)
        d_ref[pl.ds(cr, SLABS, stride=OWN), :] = mm(ld, jnp.concatenate([hi, lo, hi], axis=0))


def middle(mine, moved, weights):
    return pl.pallas_call(
        middle_kernel,
        out_shape=(jax.ShapeDtypeStruct((16, 128), F32),) * 4
        + (jax.ShapeDtypeStruct((SLABS * OWN, 128), F32),),
        in_specs=[pl.BlockSpec(memory_space=pltpu.VMEM)] * 7,
        scratch_shapes=[
            pltpu.VMEM((MX * OWN, 128), F32),
            pltpu.VMEM((MX * OWN, 128), F32),
        ],
        compiler_params=pltpu.CompilerParams(vmem_limit_bytes=8 << 20),
        name="middle",
    )(mine, moved, weights, T["fwd_x"], T["rep_g"], T["red"], T["inv_x"])


def weight_grad(parts, rg_ref, ru_ref, o_ref):
    full = jnp.concatenate([part[...] for part in parts], axis=0)
    both = jnp.concatenate(split(full), axis=1)
    rg = rg_ref[...]
    ru = ru_ref[...]
    rg = jnp.concatenate([rg, rg], axis=0)
    ru = jnp.concatenate([ru, ru], axis=0)
    grep = mm(both, rg)
    g_real, g_imag = grep[:, :128], grep[:, 128:]
    slot = (lax.broadcasted_iota(jnp.int32, (64, 256), 1) // 4) % 8
    for t in range(8):
        urep = mm(jnp.where(slot == t, both, jnp.zeros_like(both)), ru)
        u_real, u_imag = urep[:, :128], urep[:, 128:]
        real = g_real * u_real + g_imag * u_imag
        imag = g_imag * u_real - g_real * u_imag
        real = real[:16] + real[16:32] + real[32:48] + real[48:]
        imag = imag[:16] + imag[16:32] + imag[32:48] + imag[48:]
        for a in range(4):
            o_ref[a, :, t * 128 : (t + 1) * 128] = real[a * 4 : (a + 1) * 4]
            o_ref[a, :, 1024 + t * 128 : 1024 + (t + 1) * 128] = imag[a * 4 : (a + 1) * 4]


def inverse_kernel(
    d_ref, tz_ref, ly_ref, s0_ref, s1_ref, s2_ref, s3_ref, rg_ref, ru_ref, o_hbm, gw_hbm, o_ref, gw_ref, f_ref, osems, gsem
):
    full = d_ref[...].astype(BF16)
    packed = []
    for odd in range(2):
        blocks = []
        for b in range(MY):
            at = ((b // 2 * 2 + odd) ^ TURN // 4) * MZ
            blocks.append(full[at : at + MZ])
        flat = jnp.concatenate(blocks, axis=0).T
        real = jnp.concatenate([flat[0:32], flat[64:96]], axis=0)
        imag = jnp.concatenate([flat[32:64], flat[96:128]], axis=0)
        for half in (slice(0, 128), slice(128, 256)):
            packed.append(jnp.concatenate([real[:, half], imag[:, half]], axis=1))
    tz = tz_ref[...]
    group = lax.broadcasted_iota(jnp.int32, (64, 256), 1) % 128 // (2 * MZ)
    for first in range(0, MY, ZB):
        rows = []
        for b in range(first, first + ZB):
            part = packed[b % 2 * 2 + b // 8]
            rows.append(jnp.where(group == b % 8 // 2, part, jnp.zeros_like(part)))
        res = mm(jnp.concatenate(rows, axis=0), tz)
        for b in range(first, first + ZB):
            h = res[(b - first) * 64 : (b - first + 1) * 64]
            for xx in range(PLANES):
                at = xx * C * IPAD + b
                f_ref[pl.ds(at, C, stride=IPAD), :] = h[xx * 32 : xx * 32 + 32, :128]
                f_ref[pl.ds(at + 16, C, stride=IPAD), :] = h[xx * 32 : xx * 32 + 32, 128:]

    def send(step):
        at = pl.ds(step * OSTEP, OSTEP)
        return pltpu.make_async_copy(o_ref.at[at], o_hbm.at[at], osems.at[step])

    weight_grad((s0_ref, s1_ref, s2_ref, s3_ref), rg_ref, ru_ref, gw_ref)
    store = pltpu.make_async_copy(gw_ref, gw_hbm, gsem)
    store.start()
    ly = ly_ref[...]
    for step in range(IMGS // OSTEP):
        for k in range(step * OSTEP, (step + 1) * OSTEP, 2):
            at = k * IPAD
            block = f_ref[pl.ds(at, 72), :]
            pair = jnp.concatenate([block[:32], block[36:68]], axis=1)
            hi, lo = split(pair)
            res = mm(ly, jnp.concatenate([hi, lo, hi], axis=0)).astype(BF16)
            o_ref[k] = res[:, :128]
            o_ref[k + 1] = res[:, 128:]
        send(step).start()
    store.wait()
    for step in range(IMGS // OSTEP):
        send(step).wait()


def inverse(spread, parts):
    return pl.pallas_call(
        inverse_kernel,
        out_shape=(
            jax.ShapeDtypeStruct((IMGS, NY, NZ), BF16),
            jax.ShapeDtypeStruct((4, OWN, 2 * C * C), F32),
        ),
        in_specs=[pl.BlockSpec(memory_space=pltpu.VMEM)] * 9,
        out_specs=(HBM, HBM),
        scratch_shapes=[
            pltpu.VMEM((IMGS, NY, NZ), BF16),
            pltpu.VMEM((4, OWN, 2 * C * C), F32),
            pltpu.VMEM((IMGS * IPAD, 128), F32),
            pltpu.SemaphoreType.DMA((IMGS // OSTEP,)),
            pltpu.SemaphoreType.DMA,
        ],
        compiler_params=pltpu.CompilerParams(vmem_limit_bytes=8 << 20),
        name="inv_local",
    )(spread, T["inv_z"], T["inv_y"], *parts, T["rep_g"], T["rep_u"])


def body(u_field, preact, cotangent, weights):
    shape = (IMGS, NY, NZ)
    partial = forward(u_field.reshape(shape), preact.reshape(shape), cotangent.reshape(shape))
    partial, weights = lax.optimization_barrier((partial, weights))
    mine = jnp.full((16, 128), lax.axis_index("dp"), jnp.int32)
    moved = lax.all_to_all(partial, "slab", split_axis=0, concat_axis=0, axis_index_groups=ORDER, tiled=True)
    wide = widen(weights)
    *pieces, back = middle(mine, moved.reshape(SLABS * 8, 128), wide)
    for at, other in enumerate(OTHERS):
        if other:
            pieces[at] = lax.ppermute(pieces[at], "dp", [(n, n ^ other) for n in range(4)])
    spread = lax.all_to_all(back, "slab", split_axis=0, concat_axis=0, axis_index_groups=ORDER, tiled=True)
    field_grad, grad_weights = inverse(spread, pieces)
    return grad_weights, field_grad.reshape(1, PLANES, C, NY, NZ)


def solution(mesh):
    placed = (
        P("dp", "slab", None, None, None),
        P("dp", "slab", None, None, None),
        P("dp", "slab", None, None, None),
        P(None, "slab", None),
    )
    return jax.shard_map(
        body,
        mesh=mesh,
        in_specs=placed,
        out_specs=(P("dp", "slab", None), P("dp", "slab", None, None, None)),
        check_vma=False,
    )
```

```python
import itertools
import math

import jax
import jax.numpy as jnp
import numpy as np
from jax import lax
from jax.experimental import pallas as pl
from jax.experimental.pallas import tpu as pltpu
from jax.sharding import PartitionSpec as P

C = 32
NX = 128
NY = 128
NZ = 128
MX = 16
MY = 16
MZ = 16
SLABS = 64
PLANES = NX // SLABS
IMGS = PLANES * C
OWN = MY * MZ // SLABS
F32 = jnp.float32
BF16 = jnp.bfloat16
AHEAD = 2
TURN = 52
BACK = 36
ORDER = [[n ^ TURN for n in range(SLABS)]]
BACK_ORDER = [[n ^ BACK for n in range(SLABS)]]
CUTS = (0, 16, 40, 64)
OSTEP = 8
ZB = 2
PAD = 132
IPAD = 36


def np_twiddles(length, freqs):
    product = (np.arange(length, dtype=np.int64)[:, None] * freqs[None, :]) % length
    angle = product.astype(np.float32) * np.float32(2.0 * math.pi / length)
    return np.cos(angle).astype(np.float32), np.sin(angle).astype(np.float32)


def signed(count):
    index = np.arange(count)
    return np.where(index < count // 2, index, index - count)


def split_np(table):
    high = table.astype(jnp.bfloat16)
    low = (table - high.astype(np.float32)).astype(jnp.bfloat16)
    return high, low


def make_tables():
    cx, sx = np_twiddles(NX, signed(MX))
    cy, sy = np_twiddles(NY, signed(MY))
    cz, sz = np_twiddles(NZ, np.arange(MZ))
    t = {}
    rows = np.concatenate([cy.T, sy.T], 0)
    t["fwd_y"] = np.concatenate(split_np(rows), 1)
    low_c = cz.astype(jnp.bfloat16).astype(np.float32)
    low_s = (-sz).astype(jnp.bfloat16).astype(np.float32)
    real = np.concatenate([low_c, low_s], 0).T
    imag = np.concatenate([low_s, -low_c], 0).T
    wz = np.stack([real.reshape(4, 4, 2 * NZ), imag.reshape(4, 4, 2 * NZ)], 1)
    t["fwd_z"] = wz.reshape(2 * MZ, 2 * NZ).astype(jnp.bfloat16)
    mode_scale = np.where(np.arange(MZ) == 0, 0.5, 1.0) / (NX * NY * NZ)
    per_row = np.broadcast_to(mode_scale.reshape(4, 1, 4), (4, 2, 4)).reshape(2 * MZ, 1)
    is_g = (np.arange(128) // C) % 2 == 1
    t["scale"] = np.where(is_g[None, :], per_row, 1.0).astype(np.float32)
    cxs, sxs = cx.reshape(SLABS, PLANES, MX)[ORDER[0]], sx.reshape(SLABS, PLANES, MX)[ORDER[0]]
    lx = np.zeros((PLANES, 2, MX, 2, SLABS), np.float32)
    for xx in range(PLANES):
        lx[xx, 0, :, 0] = cxs[:, xx].T
        lx[xx, 0, :, 1] = sxs[:, xx].T
        lx[xx, 1, :, 0] = -sxs[:, xx].T
        lx[xx, 1, :, 1] = cxs[:, xx].T
    t["fwd_x"] = np.concatenate(split_np(lx.reshape(PLANES * 2 * MX, 2 * SLABS)), 0)
    rep = np.zeros((128, 2, 4, C), np.float32)
    for part in range(2):
        for ch in range(C):
            rep[part * 64 + 32 + ch, part, :, ch] = 1.0
    t["rep_g"] = rep.reshape(128, 256).astype(jnp.bfloat16)
    rep = np.zeros((2, 2, 8, 4, 2, 4, C), np.float32)
    for part in range(2):
        for r in range(4):
            rep[part, 0, :, r, part, r, :] = 1.0
    t["rep_u"] = rep.reshape(128, 256).astype(jnp.bfloat16)
    red = np.zeros((2, 4, C, 4, 8, 4), np.float32)
    for r in range(4):
        red[0, r, :, 0, :, r] = 1.0
        red[1, r, :, 1, :, r] = 1.0
        red[1, r, :, 2, :, r] = -1.0
        red[0, r, :, 3, :, r] = 1.0
    t["red"] = red.reshape(256, 128).astype(jnp.bfloat16)
    cxb, sxb = cx.reshape(SLABS, PLANES, MX)[BACK_ORDER[0]], sx.reshape(SLABS, PLANES, MX)[BACK_ORDER[0]]
    ld = np.stack([cxb, sxb], 2).reshape(SLABS, PLANES * 2 * MX)
    high, low = split_np(ld)
    t["inv_x"] = np.concatenate([high, high, low], 1)
    tz = np.stack([np.concatenate([cz.T, sz.T], 1), np.concatenate([-sz.T, cz.T], 1)])
    tz = np.broadcast_to(tz[:, None], (2, 8, MZ, 2 * NZ)).reshape(256, 2 * NZ)
    high, low = split_np(tz)
    odd = (np.arange(256) // MZ % 2 == 1)[:, None]
    t["inv_z"] = np.where(odd, low, high)
    ly = np.concatenate([cy, -sy], 1)
    high, low = split_np(ly)
    t["inv_y"] = np.concatenate([high, high, low], 1)
    return t


T = make_tables()


def split(value):
    high = value.astype(BF16)
    return high, (value - high.astype(F32)).astype(BF16)


def mm(a, b):
    return jnp.dot(a, b, preferred_element_type=F32)


def mm_nt(a, b):
    return lax.dot_general(a, b, (((1,), (1,)), ((), ())), preferred_element_type=F32)


HBM = pl.BlockSpec(memory_space=pltpu.HBM)


def forward_kernel(
    u_hbm, p_hbm, c_hbm, ty_hbm, wz_hbm, sc_hbm, o_hbm, o_ref, u_ref, p_ref, c_ref, ty_ref, wz_ref, sc_ref, xc_ref, xs_ref, sems, tsems, osems
):
    def chunk(src, dst, row, step):
        at = pl.ds(CUTS[step], CUTS[step + 1] - CUTS[step])
        return pltpu.make_async_copy(src.at[at], dst.at[at], sems.at[row, step])

    table = pltpu.make_async_copy(ty_hbm, ty_ref, tsems.at[0])
    late = [
        pltpu.make_async_copy(wz_hbm, wz_ref, tsems.at[1]),
        pltpu.make_async_copy(sc_hbm, sc_ref, tsems.at[2]),
    ]
    def fetch(step):
        chunk(p_hbm, p_ref, 1, step).start()
        chunk(c_hbm, c_ref, 2, step).start()
        chunk(u_hbm, u_ref, 0, step).start()

    fetch(0)
    table.start()
    for step in range(1, AHEAD):
        fetch(step)
    for one in late:
        one.start()
    table.wait()

    def arrived(step):
        for row, (src, dst) in enumerate(((u_hbm, u_ref), (p_hbm, p_ref), (c_hbm, c_ref))):
            chunk(src, dst, row, step).wait()

    def slope_of(k):
        if True:
            arg = p_ref[k].astype(F32) * math.sqrt(0.5)
            bell = jnp.exp2((arg * (-math.log2(math.e))) * arg) * (2.0 / math.sqrt(math.pi))
            slope = (lax.erf(arg) + 1.0) + arg * bell
            c_ref[k] = (c_ref[k].astype(F32) * slope).astype(BF16)

    ty = ty_ref[...]

    def image(k):
        if True:
            both = jnp.concatenate([u_ref[k], c_ref[k]], axis=1)
            part = mm(ty, jnp.concatenate([both, both], axis=0))
            base = (k // C) * 64 + k % C
            xc_ref[pl.ds(base, MY, stride=PAD), :] = part[:16, :128]
            xs_ref[pl.ds(base, MY, stride=PAD), :] = part[16:, :128]
            xc_ref[pl.ds(base + 32, MY, stride=PAD), :] = part[:16, 128:]
            xs_ref[pl.ds(base + 32, MY, stride=PAD), :] = part[16:, 128:]

    for step in range(len(CUTS)):
        if step < len(CUTS) - 1:
            arrived(step)
            if step + AHEAD < len(CUTS) - 1:
                fetch(step + AHEAD)
        if step < len(CUTS) - 1:
            for k in range(CUTS[step], CUTS[step + 1]):
                slope_of(k)
                if k >= 2:
                    image(k - 2)
        else:
            image(62)
            image(63)
    for one in late:
        one.wait()
    wz = wz_ref[...]
    scale = sc_ref[...]

    def send(part):
        at = pl.ds(part * 16, 16)
        return pltpu.make_async_copy(o_ref.at[at], o_hbm.at[at], osems.at[part])

    for b in range(MY):
        rows = slice(b * PAD, b * PAD + 128)
        both = jnp.concatenate([xc_ref[rows, :].astype(BF16), xs_ref[rows, :].astype(BF16)], axis=1)
        res = mm_nt(wz, both)
        res = res * scale
        for q in range(4):
            o_ref[(b * 4 + q) ^ TURN] = res[q * 8 : (q + 1) * 8]
        if b % 4 == 3:
            send(b // 4 ^ TURN // 16).start()
    for part in range(4):
        send(part).wait()


def forward(u, pre, cot):
    big = pltpu.VMEM((IMGS, NY, NZ), BF16)
    flat = pltpu.VMEM((MY * PAD, 128), F32)
    return pl.pallas_call(
        forward_kernel,
        out_shape=jax.ShapeDtypeStruct((SLABS, 8, 128), F32),
        in_specs=[HBM] * 6,
        out_specs=HBM,
        scratch_shapes=[
            pltpu.VMEM((SLABS, 8, 128), F32),
            big,
            big,
            big,
            pltpu.VMEM((32, 256), BF16),
            pltpu.VMEM((32, 256), BF16),
            pltpu.VMEM((32, 128), F32),
            flat,
            flat,
            pltpu.SemaphoreType.DMA((3, (len(CUTS) - 1))),
            pltpu.SemaphoreType.DMA((3,)),
            pltpu.SemaphoreType.DMA((4,)),
        ],
        name="fwd_local",
    )(u, pre, cot, T["fwd_y"], T["fwd_z"], T["scale"])


def widen_kernel(w_ref, o_ref):
    for a in range(MX):
        o_ref[pl.ds(4 * a, 4), :] = w_ref[a].astype(F32)


def widen(weights):
    return pl.pallas_call(
        widen_kernel,
        out_shape=jax.ShapeDtypeStruct((MX * OWN, 2 * C * C), F32),
        in_specs=[pl.BlockSpec(memory_space=pltpu.VMEM)],
        out_specs=pl.BlockSpec(memory_space=pltpu.VMEM),
        compiler_params=pltpu.CompilerParams(vmem_limit_bytes=4 << 20),
        name="widen",
    )(weights)


def middle_kernel(
    mine_ref, m_ref, wf_ref, lx_ref, rg_ref, red_ref, ld_ref, own0_ref, own13_ref, own2_ref, d_ref, own_ref, q_ref
):
    lx = lx_ref[...]
    lane = lax.broadcasted_iota(jnp.int32, (MX, 128), 1)
    left = lane < 64
    for cr in range(OWN):
        rhs = jnp.concatenate(
            [m_ref[pl.ds(cr, SLABS, stride=8), :], m_ref[pl.ds(4 + cr, SLABS, stride=8), :]], axis=0
        )
        hi, lo = split(rhs)
        res = mm(lx, hi)
        res = res[:64] + res[64:] + mm(lx[:64], lo)
        summed = res[:32] + pltpu.roll(res[32:], 64, 1)
        own_ref[pl.ds(cr, MX, stride=OWN), :] = jnp.where(
            left, summed[:16], pltpu.roll(summed[16:], 64, 1)
        )
    mine = mine_ref[...]
    quarter = [own_ref[c * 16 : (c + 1) * 16, :] for c in range(4)]
    for other, ref in enumerate((own0_ref, own13_ref.at[:16], own2_ref, own13_ref.at[16:])):
        piece = quarter[3 ^ other]
        for c in range(3):
            piece = jnp.where(mine == c, quarter[c ^ other], piece)
        ref[...] = piece
    hi, lo = split(own_ref[...])
    rg = rg_ref[...]
    grep = mm(hi, rg) + mm(lo, rg)
    g_real, g_imag = grep[:, :128], grep[:, 128:]
    acc = jnp.zeros((MX * OWN, 128), F32)
    slot = (lax.broadcasted_iota(jnp.int32, (MX * OWN, 128), 1) // 4) % 8
    red = red_ref[...]
    for t in range(8):
        w_real = wf_ref[:, t * 128 : (t + 1) * 128]
        w_imag = wf_ref[:, 1024 + t * 128 : 1024 + (t + 1) * 128]
        rhi, rlo = split(w_real * g_real + w_imag * g_imag)
        ihi, ilo = split(w_real * g_imag - w_imag * g_real)
        res = mm(jnp.concatenate([rhi, ihi], axis=1), red)
        res += mm(jnp.concatenate([rlo, ilo], axis=1), red)
        acc = jnp.where(slot == t, res, acc)
    q_ref[...] = acc
    ld = ld_ref[...]
    for cr in range(OWN):
        q = q_ref[pl.ds(cr, MX, stride=OWN), :]
        r = pltpu.roll(q, 64, 1)
        zero = jnp.zeros_like(q)
        rhs = jnp.concatenate(
            [
                jnp.where(left, q, zero),
                jnp.where(left, r, zero),
                jnp.where(left, zero, r),
                jnp.where(left, zero, q),
            ],
            axis=0,
        )
        hi, lo = split(rhs)
        d_ref[pl.ds(cr, SLABS, stride=OWN), :] = mm(ld, jnp.concatenate([hi, lo, hi], axis=0))


def middle(mine, moved, weights):
    return pl.pallas_call(
        middle_kernel,
        out_shape=tuple(
            jax.ShapeDtypeStruct((rows, 128), F32) for rows in (16, 32, 16, SLABS * OWN)
        ),
        in_specs=[pl.BlockSpec(memory_space=pltpu.VMEM)] * 7,
        scratch_shapes=[
            pltpu.VMEM((MX * OWN, 128), F32),
            pltpu.VMEM((MX * OWN, 128), F32),
        ],
        compiler_params=pltpu.CompilerParams(vmem_limit_bytes=8 << 20),
        name="middle",
    )(mine, moved, weights, T["fwd_x"], T["rep_g"], T["red"], T["inv_x"])


def weight_grad(parts, rg_ref, ru_ref, o_ref):
    full = jnp.concatenate([part[...] for part in parts], axis=0)
    both = jnp.concatenate(split(full), axis=1)
    rg = rg_ref[...]
    ru = ru_ref[...]
    rg = jnp.concatenate([rg, rg], axis=0)
    ru = jnp.concatenate([ru, ru], axis=0)
    grep = mm(both, rg)
    g_real, g_imag = grep[:, :128], grep[:, 128:]
    slot = (lax.broadcasted_iota(jnp.int32, (64, 256), 1) // 4) % 8
    for t in range(8):
        urep = mm(jnp.where(slot == t, both, jnp.zeros_like(both)), ru)
        u_real, u_imag = urep[:, :128], urep[:, 128:]
        real = g_real * u_real + g_imag * u_imag
        imag = g_imag * u_real - g_real * u_imag
        real = real[:16] + real[16:32] + real[32:48] + real[48:]
        imag = imag[:16] + imag[16:32] + imag[32:48] + imag[48:]
        for a in range(4):
            o_ref[a, :, t * 128 : (t + 1) * 128] = real[a * 4 : (a + 1) * 4]
            o_ref[a, :, 1024 + t * 128 : 1024 + (t + 1) * 128] = imag[a * 4 : (a + 1) * 4]


def inverse_kernel(
    d_ref, tz_ref, ly_ref, s0_ref, s1_ref, s23_ref, rg_ref, ru_ref, o_hbm, gw_hbm, o_ref, gw_ref, f_ref, osems, gsem
):
    full = d_ref[...].astype(BF16)
    packed = []
    for odd in range(2):
        blocks = []
        for b in range(MY):
            at = ((b // 2 * 2 + odd) ^ BACK // 4) * MZ
            blocks.append(full[at : at + MZ])
        flat = jnp.concatenate(blocks, axis=0).T
        real = jnp.concatenate([flat[0:32], flat[64:96]], axis=0)
        imag = jnp.concatenate([flat[32:64], flat[96:128]], axis=0)
        for half in (slice(0, 128), slice(128, 256)):
            packed.append(jnp.concatenate([real[:, half], imag[:, half]], axis=1))
    tz = tz_ref[...]
    group = lax.broadcasted_iota(jnp.int32, (64, 256), 1) % 128 // (2 * MZ)
    for first in range(0, MY, ZB):
        rows = []
        for b in range(first, first + ZB):
            part = packed[b % 2 * 2 + b // 8]
            rows.append(jnp.where(group == b % 8 // 2, part, jnp.zeros_like(part)))
        res = mm(jnp.concatenate(rows, axis=0), tz)
        for b in range(first, first + ZB):
            h = res[(b - first) * 64 : (b - first + 1) * 64]
            for xx in range(PLANES):
                at = xx * C * IPAD + b
                f_ref[pl.ds(at, C, stride=IPAD), :] = h[xx * 32 : xx * 32 + 32, :128]
                f_ref[pl.ds(at + 16, C, stride=IPAD), :] = h[xx * 32 : xx * 32 + 32, 128:]

    def send(step):
        at = pl.ds(step * OSTEP, OSTEP)
        return pltpu.make_async_copy(o_ref.at[at], o_hbm.at[at], osems.at[step])

    weight_grad((s0_ref, s1_ref.at[:16], s23_ref), rg_ref, ru_ref, gw_ref)
    store = pltpu.make_async_copy(gw_ref, gw_hbm, gsem)
    store.start()
    ly = ly_ref[...]
    for step in range(IMGS // OSTEP):
        for k in range(step * OSTEP, (step + 1) * OSTEP, 2):
            at = k * IPAD
            block = f_ref[pl.ds(at, 72), :]
            pair = jnp.concatenate([block[:32], block[36:68]], axis=1)
            hi, lo = split(pair)
            res = mm(ly, jnp.concatenate([hi, lo, hi], axis=0)).astype(BF16)
            o_ref[k] = res[:, :128]
            o_ref[k + 1] = res[:, 128:]
        send(step).start()
    store.wait()
    for step in range(IMGS // OSTEP):
        send(step).wait()


def inverse(spread, parts):
    return pl.pallas_call(
        inverse_kernel,
        out_shape=(
            jax.ShapeDtypeStruct((IMGS, NY, NZ), BF16),
            jax.ShapeDtypeStruct((4, OWN, 2 * C * C), F32),
        ),
        in_specs=[pl.BlockSpec(memory_space=pltpu.VMEM)] * 8,
        out_specs=(HBM, HBM),
        scratch_shapes=[
            pltpu.VMEM((IMGS, NY, NZ), BF16),
            pltpu.VMEM((4, OWN, 2 * C * C), F32),
            pltpu.VMEM((IMGS * IPAD, 128), F32),
            pltpu.SemaphoreType.DMA((IMGS // OSTEP,)),
            pltpu.SemaphoreType.DMA,
        ],
        compiler_params=pltpu.CompilerParams(vmem_limit_bytes=8 << 20),
        name="inv_local",
    )(spread, T["inv_z"], T["inv_y"], *parts, T["rep_g"], T["rep_u"])


def body(u_field, preact, cotangent, weights):
    shape = (IMGS, NY, NZ)
    partial = forward(u_field.reshape(shape), preact.reshape(shape), cotangent.reshape(shape))
    partial, weights = lax.optimization_barrier((partial, weights))
    mine = jnp.full((16, 128), lax.axis_index("dp"), jnp.int32)
    moved = lax.all_to_all(partial, "slab", split_axis=0, concat_axis=0, axis_index_groups=ORDER, tiled=True)
    wide = widen(weights)
    own, to_core, to_far, back = middle(mine, moved.reshape(SLABS * 8, 128), wide)
    near = lax.ppermute(to_core, "dp", [(n, n ^ 1) for n in range(4)])
    far = lax.ppermute(
        jnp.concatenate([to_far, near[16:]], axis=0), "dp", [(n, n ^ 2) for n in range(4)]
    )
    spread = lax.all_to_all(back, "slab", split_axis=0, concat_axis=0, axis_index_groups=BACK_ORDER, tiled=True)
    field_grad, grad_weights = inverse(spread, (own, near, far))
    return grad_weights, field_grad.reshape(1, PLANES, C, NY, NZ)


def solution(mesh):
    placed = (
        P("dp", "slab", None, None, None),
        P("dp", "slab", None, None, None),
        P("dp", "slab", None, None, None),
        P(None, "slab", None),
    )
    return jax.shard_map(
        body,
        mesh=mesh,
        in_specs=placed,
        out_specs=(P("dp", "slab", None), P("dp", "slab", None, None, None)),
        check_vma=False,
    )
```

```python
import itertools
import math

import jax
import jax.numpy as jnp
import numpy as np
from jax import lax
from jax.experimental import pallas as pl
from jax.experimental.pallas import tpu as pltpu
from jax.sharding import PartitionSpec as P

C = 32
NX = 128
NY = 128
NZ = 128
MX = 16
MY = 16
MZ = 16
SLABS = 64
PLANES = NX // SLABS
IMGS = PLANES * C
OWN = MY * MZ // SLABS
F32 = jnp.float32
BF16 = jnp.bfloat16
AHEAD = 2
OTHERS = (0, 2, 3, 1)
TURN = 53
BACK = 53
ORDER = [[n ^ TURN for n in range(SLABS)]]
BACK_ORDER = [[n ^ BACK for n in range(SLABS)]]
CUTS = (0, 16, 40, 64)
OSTEP = 8
ZB = 2
PAD = 132
IPAD = 36


def np_twiddles(length, freqs):
    product = (np.arange(length, dtype=np.int64)[:, None] * freqs[None, :]) % length
    angle = product.astype(np.float32) * np.float32(2.0 * math.pi / length)
    return np.cos(angle).astype(np.float32), np.sin(angle).astype(np.float32)


def signed(count):
    index = np.arange(count)
    return np.where(index < count // 2, index, index - count)


def split_np(table):
    high = table.astype(jnp.bfloat16)
    low = (table - high.astype(np.float32)).astype(jnp.bfloat16)
    return high, low


def make_tables():
    cx, sx = np_twiddles(NX, signed(MX))
    cy, sy = np_twiddles(NY, signed(MY))
    cz, sz = np_twiddles(NZ, np.arange(MZ))
    t = {}
    rows = np.concatenate([cy.T, sy.T], 0)
    t["fwd_y"] = np.concatenate(split_np(rows), 1)
    low_c = cz.astype(jnp.bfloat16).astype(np.float32)
    low_s = (-sz).astype(jnp.bfloat16).astype(np.float32)
    real = np.concatenate([low_c, low_s], 0).T
    imag = np.concatenate([low_s, -low_c], 0).T
    wz = np.stack([real.reshape(4, 4, 2 * NZ), imag.reshape(4, 4, 2 * NZ)], 1)
    t["fwd_z"] = wz.reshape(2 * MZ, 2 * NZ).astype(jnp.bfloat16)
    mode_scale = np.where(np.arange(MZ) == 0, 0.5, 1.0) / (NX * NY * NZ)
    per_row = np.broadcast_to(mode_scale.reshape(4, 1, 4), (4, 2, 4)).reshape(2 * MZ, 1)
    is_g = (np.arange(128) // C) % 2 == 1
    t["scale"] = np.where(is_g[None, :], per_row, 1.0).astype(np.float32)
    cxs, sxs = cx.reshape(SLABS, PLANES, MX)[ORDER[0]], sx.reshape(SLABS, PLANES, MX)[ORDER[0]]
    lx = np.zeros((PLANES, 2, MX, 2, SLABS), np.float32)
    for xx in range(PLANES):
        lx[xx, 0, :, 0] = cxs[:, xx].T
        lx[xx, 0, :, 1] = sxs[:, xx].T
        lx[xx, 1, :, 0] = -sxs[:, xx].T
        lx[xx, 1, :, 1] = cxs[:, xx].T
    t["fwd_x"] = np.concatenate(split_np(lx.reshape(PLANES * 2 * MX, 2 * SLABS)), 0)
    rep = np.zeros((128, 2, 4, C), np.float32)
    for part in range(2):
        for ch in range(C):
            rep[part * 64 + 32 + ch, part, :, ch] = 1.0
    t["rep_g"] = rep.reshape(128, 256).astype(jnp.bfloat16)
    rep = np.zeros((2, 2, 8, 4, 2, 4, C), np.float32)
    for part in range(2):
        for r in range(4):
            rep[part, 0, :, r, part, r, :] = 1.0
    t["rep_u"] = rep.reshape(128, 256).astype(jnp.bfloat16)
    red = np.zeros((2, 4, C, 4, 8, 4), np.float32)
    for r in range(4):
        red[0, r, :, 0, :, r] = 1.0
        red[1, r, :, 1, :, r] = 1.0
        red[1, r, :, 2, :, r] = -1.0
        red[0, r, :, 3, :, r] = 1.0
    t["red"] = red.reshape(256, 128).astype(jnp.bfloat16)
    cxb, sxb = cx.reshape(SLABS, PLANES, MX)[BACK_ORDER[0]], sx.reshape(SLABS, PLANES, MX)[BACK_ORDER[0]]
    ld = np.stack([cxb, sxb], 2).reshape(SLABS, PLANES * 2 * MX)
    high, low = split_np(ld)
    t["inv_x"] = np.concatenate([high, high, low], 1)
    czb, szb = ((v.T.reshape(4, 4, NZ)[np.arange(4) ^ BACK % 4]).reshape(MZ, NZ) for v in (cz, sz))
    tz = np.stack([np.concatenate([czb, szb], 1), np.concatenate([-szb, czb], 1)])
    tz = np.broadcast_to(tz[:, None], (2, 8, MZ, 2 * NZ)).reshape(256, 2 * NZ)
    high, low = split_np(tz)
    odd = (np.arange(256) // MZ % 2 == 1)[:, None]
    t["inv_z"] = np.where(odd, low, high)
    ly = np.concatenate([cy, -sy], 1)
    high, low = split_np(ly)
    t["inv_y"] = np.concatenate([high, high, low], 1)
    return t


T = make_tables()


def split(value):
    high = value.astype(BF16)
    return high, (value - high.astype(F32)).astype(BF16)


def mm(a, b):
    return jnp.dot(a, b, preferred_element_type=F32)


def mm_nt(a, b):
    return lax.dot_general(a, b, (((1,), (1,)), ((), ())), preferred_element_type=F32)


HBM = pl.BlockSpec(memory_space=pltpu.HBM)


def forward_kernel(
    u_hbm, p_hbm, c_hbm, ty_hbm, wz_hbm, sc_hbm, o_hbm, o_ref, u_ref, p_ref, c_ref, ty_ref, wz_ref, sc_ref, xc_ref, xs_ref, sems, tsems, osems
):
    def chunk(src, dst, row, step):
        at = pl.ds(CUTS[step], CUTS[step + 1] - CUTS[step])
        return pltpu.make_async_copy(src.at[at], dst.at[at], sems.at[row, step])

    table = pltpu.make_async_copy(ty_hbm, ty_ref, tsems.at[0])
    late = [
        pltpu.make_async_copy(wz_hbm, wz_ref, tsems.at[1]),
        pltpu.make_async_copy(sc_hbm, sc_ref, tsems.at[2]),
    ]
    def fetch(step):
        chunk(p_hbm, p_ref, 1, step).start()
        chunk(c_hbm, c_ref, 2, step).start()
        chunk(u_hbm, u_ref, 0, step).start()

    fetch(0)
    table.start()
    for step in range(1, AHEAD):
        fetch(step)
    for one in late:
        one.start()
    table.wait()

    def arrived(step):
        for row, (src, dst) in enumerate(((u_hbm, u_ref), (p_hbm, p_ref), (c_hbm, c_ref))):
            chunk(src, dst, row, step).wait()

    def slope_of(k):
        if True:
            arg = p_ref[k].astype(F32) * math.sqrt(0.5)
            bell = jnp.exp2((arg * (-math.log2(math.e))) * arg) * (2.0 / math.sqrt(math.pi))
            slope = (lax.erf(arg) + 1.0) + arg * bell
            c_ref[k] = (c_ref[k].astype(F32) * slope).astype(BF16)

    ty = ty_ref[...]

    def image(k):
        if True:
            both = jnp.concatenate([u_ref[k], c_ref[k]], axis=1)
            part = mm(ty, jnp.concatenate([both, both], axis=0))
            base = (k // C) * 64 + k % C
            xc_ref[pl.ds(base, MY, stride=PAD), :] = part[:16, :128]
            xs_ref[pl.ds(base, MY, stride=PAD), :] = part[16:, :128]
            xc_ref[pl.ds(base + 32, MY, stride=PAD), :] = part[:16, 128:]
            xs_ref[pl.ds(base + 32, MY, stride=PAD), :] = part[16:, 128:]

    for step in range(len(CUTS)):
        if step < len(CUTS) - 1:
            arrived(step)
            if step + AHEAD < len(CUTS) - 1:
                fetch(step + AHEAD)
        if step < len(CUTS) - 1:
            for k in range(CUTS[step], CUTS[step + 1]):
                slope_of(k)
                if k >= 2:
                    image(k - 2)
        else:
            image(62)
            image(63)
    for one in late:
        one.wait()
    wz = wz_ref[...]
    scale = sc_ref[...]

    def send(part):
        at = pl.ds(part * 16, 16)
        return pltpu.make_async_copy(o_ref.at[at], o_hbm.at[at], osems.at[part])

    for b in range(MY):
        rows = slice(b * PAD, b * PAD + 128)
        both = jnp.concatenate([xc_ref[rows, :].astype(BF16), xs_ref[rows, :].astype(BF16)], axis=1)
        res = mm_nt(wz, both)
        res = res * scale
        for q in range(4):
            o_ref[(b * 4 + q) ^ TURN] = res[q * 8 : (q + 1) * 8]
        if b % 4 == 3:
            send(b // 4 ^ TURN // 16).start()
    for part in range(4):
        send(part).wait()


def forward(u, pre, cot):
    big = pltpu.VMEM((IMGS, NY, NZ), BF16)
    flat = pltpu.VMEM((MY * PAD, 128), F32)
    return pl.pallas_call(
        forward_kernel,
        out_shape=jax.ShapeDtypeStruct((SLABS, 8, 128), F32),
        in_specs=[HBM] * 6,
        out_specs=HBM,
        scratch_shapes=[
            pltpu.VMEM((SLABS, 8, 128), F32),
            big,
            big,
            big,
            pltpu.VMEM((32, 256), BF16),
            pltpu.VMEM((32, 256), BF16),
            pltpu.VMEM((32, 128), F32),
            flat,
            flat,
            pltpu.SemaphoreType.DMA((3, (len(CUTS) - 1))),
            pltpu.SemaphoreType.DMA((3,)),
            pltpu.SemaphoreType.DMA((4,)),
        ],
        name="fwd_local",
    )(u, pre, cot, T["fwd_y"], T["fwd_z"], T["scale"])


def widen_kernel(w_ref, o_ref):
    for a in range(MX):
        o_ref[pl.ds(4 * a, 4), :] = w_ref[a].astype(F32)


def widen(weights):
    return pl.pallas_call(
        widen_kernel,
        out_shape=jax.ShapeDtypeStruct((MX * OWN, 2 * C * C), F32),
        in_specs=[pl.BlockSpec(memory_space=pltpu.VMEM)],
        out_specs=pl.BlockSpec(memory_space=pltpu.VMEM),
        compiler_params=pltpu.CompilerParams(vmem_limit_bytes=4 << 20),
        name="widen",
    )(weights)


def middle_kernel(
    mine_ref, m_ref, wf_ref, lx_ref, rg_ref, red_ref, ld_ref, own0_ref, own1_ref, own2_ref, own3_ref, d_ref, own_ref, q_ref
):
    lx = lx_ref[...]
    lane = lax.broadcasted_iota(jnp.int32, (MX, 128), 1)
    left = lane < 64
    for cr in range(OWN):
        rhs = jnp.concatenate(
            [m_ref[pl.ds(cr, SLABS, stride=8), :], m_ref[pl.ds(4 + cr, SLABS, stride=8), :]], axis=0
        )
        hi, lo = split(rhs)
        res = mm(lx, hi)
        res = res[:64] + res[64:] + mm(lx[:64], lo)
        summed = res[:32] + pltpu.roll(res[32:], 64, 1)
        own_ref[pl.ds(cr, MX, stride=OWN), :] = jnp.where(
            left, summed[:16], pltpu.roll(summed[16:], 64, 1)
        )
    mine = mine_ref[...]
    quarter = [own_ref[c * 16 : (c + 1) * 16, :] for c in range(4)]
    for other, ref in zip(OTHERS, (own0_ref, own1_ref, own2_ref, own3_ref)):
        piece = quarter[3 ^ other]
        for c in range(3):
            piece = jnp.where(mine == c, quarter[c ^ other], piece)
        ref[...] = piece
    hi, lo = split(own_ref[...])
    rg = rg_ref[...]
    grep = mm(hi, rg) + mm(lo, rg)
    g_real, g_imag = grep[:, :128], grep[:, 128:]
    acc = jnp.zeros((MX * OWN, 128), F32)
    slot = (lax.broadcasted_iota(jnp.int32, (MX * OWN, 128), 1) // 4) % 8
    red = red_ref[...]
    for t in range(8):
        w_real = wf_ref[:, t * 128 : (t + 1) * 128]
        w_imag = wf_ref[:, 1024 + t * 128 : 1024 + (t + 1) * 128]
        rhi, rlo = split(w_real * g_real + w_imag * g_imag)
        ihi, ilo = split(w_real * g_imag - w_imag * g_real)
        res = mm(jnp.concatenate([rhi, ihi], axis=1), red)
        res += mm(jnp.concatenate([rlo, ilo], axis=1), red)
        acc = jnp.where(slot == t, res, acc)
    q_ref[...] = acc
    ld = ld_ref[...]
    for cr in range(OWN):
        q = q_ref[pl.ds(cr, MX, stride=OWN), :]
        r = pltpu.roll(q, 64, 1)
        zero = jnp.zeros_like(q)
        rhs = jnp.concatenate(
            [
                jnp.where(left, q, zero),
                jnp.where(left, r, zero),
                jnp.where(left, zero, r),
                jnp.where(left, zero, q),
            ],
            axis=0,
        )
        hi, lo = split(rhs)
        d_ref[pl.ds(cr, SLABS, stride=OWN), :] = mm(ld, jnp.concatenate([hi, lo, hi], axis=0))


def middle(mine, moved, weights):
    return pl.pallas_call(
        middle_kernel,
        out_shape=(jax.ShapeDtypeStruct((16, 128), F32),) * 4
        + (jax.ShapeDtypeStruct((SLABS * OWN, 128), F32),),
        in_specs=[pl.BlockSpec(memory_space=pltpu.VMEM)] * 7,
        scratch_shapes=[
            pltpu.VMEM((MX * OWN, 128), F32),
            pltpu.VMEM((MX * OWN, 128), F32),
        ],
        compiler_params=pltpu.CompilerParams(vmem_limit_bytes=8 << 20),
        name="middle",
    )(mine, moved, weights, T["fwd_x"], T["rep_g"], T["red"], T["inv_x"])


def weight_grad_kernel(s0_ref, s1_ref, s2_ref, s3_ref, rg_ref, ru_ref, o_ref):
    parts = (s0_ref, s1_ref, s2_ref, s3_ref)
    full = jnp.concatenate([part[...] for part in parts], axis=0)
    both = jnp.concatenate(split(full), axis=1)
    rg = rg_ref[...]
    ru = ru_ref[...]
    rg = jnp.concatenate([rg, rg], axis=0)
    ru = jnp.concatenate([ru, ru], axis=0)
    grep = mm(both, rg)
    g_real, g_imag = grep[:, :128], grep[:, 128:]
    slot = (lax.broadcasted_iota(jnp.int32, (64, 256), 1) // 4) % 8
    for t in range(8):
        urep = mm(jnp.where(slot == t, both, jnp.zeros_like(both)), ru)
        u_real, u_imag = urep[:, :128], urep[:, 128:]
        real = g_real * u_real + g_imag * u_imag
        imag = g_imag * u_real - g_real * u_imag
        real = real[:16] + real[16:32] + real[32:48] + real[48:]
        imag = imag[:16] + imag[16:32] + imag[32:48] + imag[48:]
        for a in range(4):
            o_ref[a, :, t * 128 : (t + 1) * 128] = real[a * 4 : (a + 1) * 4]
            o_ref[a, :, 1024 + t * 128 : 1024 + (t + 1) * 128] = imag[a * 4 : (a + 1) * 4]


def weight_grad(parts):
    return pl.pallas_call(
        weight_grad_kernel,
        out_shape=jax.ShapeDtypeStruct((4, OWN, 2 * C * C), F32),
        compiler_params=pltpu.CompilerParams(vmem_limit_bytes=4 << 20),
        name="weight_grad",
    )(*parts, T["rep_g"], T["rep_u"])


def inverse_kernel(
    d_ref, tz_ref, ly_ref, o_hbm, o_ref, f_ref, osems
):
    full = d_ref[...].astype(BF16)
    packed = []
    for odd in range(2):
        blocks = []
        for b in range(MY):
            at = ((b // 2 * 2 + odd) ^ BACK // 4) * MZ
            blocks.append(full[at : at + MZ])
        flat = jnp.concatenate(blocks, axis=0).T
        real = jnp.concatenate([flat[0:32], flat[64:96]], axis=0)
        imag = jnp.concatenate([flat[32:64], flat[96:128]], axis=0)
        for half in (slice(0, 128), slice(128, 256)):
            packed.append(jnp.concatenate([real[:, half], imag[:, half]], axis=1))
    tz = tz_ref[...]
    group = lax.broadcasted_iota(jnp.int32, (64, 256), 1) % 128 // (2 * MZ)
    for first in range(0, MY, ZB):
        rows = []
        for b in range(first, first + ZB):
            part = packed[b % 2 * 2 + b // 8]
            rows.append(jnp.where(group == b % 8 // 2, part, jnp.zeros_like(part)))
        res = mm(jnp.concatenate(rows, axis=0), tz)
        for b in range(first, first + ZB):
            h = res[(b - first) * 64 : (b - first + 1) * 64]
            for xx in range(PLANES):
                at = xx * C * IPAD + b
                f_ref[pl.ds(at, C, stride=IPAD), :] = h[xx * 32 : xx * 32 + 32, :128]
                f_ref[pl.ds(at + 16, C, stride=IPAD), :] = h[xx * 32 : xx * 32 + 32, 128:]

    def send(step):
        at = pl.ds(step * OSTEP, OSTEP)
        return pltpu.make_async_copy(o_ref.at[at], o_hbm.at[at], osems.at[step])

    ly = ly_ref[...]
    for step in range(IMGS // OSTEP):
        for k in range(step * OSTEP, (step + 1) * OSTEP, 2):
            at = k * IPAD
            block = f_ref[pl.ds(at, 72), :]
            pair = jnp.concatenate([block[:32], block[36:68]], axis=1)
            hi, lo = split(pair)
            res = mm(ly, jnp.concatenate([hi, lo, hi], axis=0)).astype(BF16)
            o_ref[k] = res[:, :128]
            o_ref[k + 1] = res[:, 128:]
        send(step).start()
    for step in range(IMGS // OSTEP):
        send(step).wait()


def inverse(spread):
    return pl.pallas_call(
        inverse_kernel,
        out_shape=jax.ShapeDtypeStruct((IMGS, NY, NZ), BF16),
        in_specs=[pl.BlockSpec(memory_space=pltpu.VMEM)] * 3,
        out_specs=HBM,
        scratch_shapes=[
            pltpu.VMEM((IMGS, NY, NZ), BF16),
            pltpu.VMEM((IMGS * IPAD, 128), F32),
            pltpu.SemaphoreType.DMA((IMGS // OSTEP,)),
        ],
        compiler_params=pltpu.CompilerParams(vmem_limit_bytes=8 << 20),
        name="inv_local",
    )(spread, T["inv_z"], T["inv_y"])


def body(u_field, preact, cotangent, weights):
    shape = (IMGS, NY, NZ)
    partial = forward(u_field.reshape(shape), preact.reshape(shape), cotangent.reshape(shape))
    partial, weights = lax.optimization_barrier((partial, weights))
    mine = jnp.full((16, 128), lax.axis_index("dp"), jnp.int32)
    moved = lax.all_to_all(partial, "slab", split_axis=0, concat_axis=0, axis_index_groups=ORDER, tiled=True)
    wide = widen(weights)
    *pieces, back = middle(mine, moved.reshape(SLABS * 8, 128), wide)
    for at, other in enumerate(OTHERS):
        if other:
            pieces[at] = lax.ppermute(pieces[at], "dp", [(n, n ^ other) for n in range(4)])
    spread = lax.all_to_all(back, "slab", split_axis=0, concat_axis=0, axis_index_groups=BACK_ORDER, tiled=True)
    field_grad = inverse(spread)
    pieces, field_grad = lax.optimization_barrier((pieces, field_grad))
    grad_weights = weight_grad(pieces)
    return grad_weights, field_grad.reshape(1, PLANES, C, NY, NZ)


def solution(mesh):
    placed = (
        P("dp", "slab", None, None, None),
        P("dp", "slab", None, None, None),
        P("dp", "slab", None, None, None),
        P(None, "slab", None),
    )
    return jax.shard_map(
        body,
        mesh=mesh,
        in_specs=placed,
        out_specs=(P("dp", "slab", None), P("dp", "slab", None, None, None)),
        check_vma=False,
    )
```

```python
import itertools
import math

import jax
import jax.numpy as jnp
import numpy as np
from jax import lax
from jax.experimental import pallas as pl
from jax.experimental.pallas import tpu as pltpu
from jax.sharding import PartitionSpec as P

C = 32
NX = 128
NY = 128
NZ = 128
MX = 16
MY = 16
MZ = 16
SLABS = 64
PLANES = NX // SLABS
IMGS = PLANES * C
OWN = MY * MZ // SLABS
F32 = jnp.float32
BF16 = jnp.bfloat16
AHEAD = 2
OTHERS = (0, 2, 3, 1)
TURN = 52
BACK = 42
ORDER = [[n ^ TURN for n in range(SLABS)]]
BACK_ORDER = [[n ^ BACK for n in range(SLABS)]]
CUTS = (0, 16, 40, 64)
OSTEP = 8
ZB = 2
PAD = 132
IPAD = 36


def np_twiddles(length, freqs):
    product = (np.arange(length, dtype=np.int64)[:, None] * freqs[None, :]) % length
    angle = product.astype(np.float32) * np.float32(2.0 * math.pi / length)
    return np.cos(angle).astype(np.float32), np.sin(angle).astype(np.float32)


def signed(count):
    index = np.arange(count)
    return np.where(index < count // 2, index, index - count)


def split_np(table):
    high = table.astype(jnp.bfloat16)
    low = (table - high.astype(np.float32)).astype(jnp.bfloat16)
    return high, low


def make_tables():
    cx, sx = np_twiddles(NX, signed(MX))
    cy, sy = np_twiddles(NY, signed(MY))
    cz, sz = np_twiddles(NZ, np.arange(MZ))
    t = {}
    rows = np.concatenate([cy.T, sy.T], 0)
    t["fwd_y"] = np.concatenate(split_np(rows), 1)
    low_c = cz.astype(jnp.bfloat16).astype(np.float32)
    low_s = (-sz).astype(jnp.bfloat16).astype(np.float32)
    real = np.concatenate([low_c, low_s], 0).T
    imag = np.concatenate([low_s, -low_c], 0).T
    wz = np.stack([real.reshape(4, 4, 2 * NZ), imag.reshape(4, 4, 2 * NZ)], 1)
    t["fwd_z"] = wz.reshape(2 * MZ, 2 * NZ).astype(jnp.bfloat16)
    mode_scale = np.where(np.arange(MZ) == 0, 0.5, 1.0) / (NX * NY * NZ)
    per_row = np.broadcast_to(mode_scale.reshape(4, 1, 4), (4, 2, 4)).reshape(2 * MZ, 1)
    is_g = (np.arange(128) // C) % 2 == 1
    t["scale"] = np.where(is_g[None, :], per_row, 1.0).astype(np.float32)
    cxs, sxs = cx.reshape(SLABS, PLANES, MX)[ORDER[0]], sx.reshape(SLABS, PLANES, MX)[ORDER[0]]
    lx = np.zeros((PLANES, 2, MX, 2, SLABS), np.float32)
    for xx in range(PLANES):
        lx[xx, 0, :, 0] = cxs[:, xx].T
        lx[xx, 0, :, 1] = sxs[:, xx].T
        lx[xx, 1, :, 0] = -sxs[:, xx].T
        lx[xx, 1, :, 1] = cxs[:, xx].T
    t["fwd_x"] = np.concatenate(split_np(lx.reshape(PLANES * 2 * MX, 2 * SLABS)), 0)
    rep = np.zeros((128, 2, 4, C), np.float32)
    for part in range(2):
        for ch in range(C):
            rep[part * 64 + 32 + ch, part, :, ch] = 1.0
    t["rep_g"] = rep.reshape(128, 256).astype(jnp.bfloat16)
    rep = np.zeros((2, 2, 8, 4, 2, 4, C), np.float32)
    for part in range(2):
        for r in range(4):
            rep[part, 0, :, r, part, r, :] = 1.0
    t["rep_u"] = rep.reshape(128, 256).astype(jnp.bfloat16)
    red = np.zeros((2, 4, C, 4, 8, 4), np.float32)
    for r in range(4):
        red[0, r, :, 0, :, r] = 1.0
        red[1, r, :, 1, :, r] = 1.0
        red[1, r, :, 2, :, r] = -1.0
        red[0, r, :, 3, :, r] = 1.0
    t["red"] = red.reshape(256, 128).astype(jnp.bfloat16)
    cxb, sxb = cx.reshape(SLABS, PLANES, MX)[BACK_ORDER[0]], sx.reshape(SLABS, PLANES, MX)[BACK_ORDER[0]]
    ld = np.stack([cxb, sxb], 2).reshape(SLABS, PLANES * 2 * MX)
    high, low = split_np(ld)
    t["inv_x"] = np.concatenate([high, high, low], 1)
    czb, szb = ((v.T.reshape(4, 4, NZ)[np.arange(4) ^ BACK % 4]).reshape(MZ, NZ) for v in (cz, sz))
    tz = np.stack([np.concatenate([czb, szb], 1), np.concatenate([-szb, czb], 1)])
    tz = np.broadcast_to(tz[:, None], (2, 8, MZ, 2 * NZ)).reshape(256, 2 * NZ)
    high, low = split_np(tz)
    odd = (np.arange(256) // MZ % 2 == 1)[:, None]
    t["inv_z"] = np.where(odd, low, high)
    ly = np.concatenate([cy, -sy], 1)
    high, low = split_np(ly)
    t["inv_y"] = np.concatenate([high, high, low], 1)
    return t


T = make_tables()


def split(value):
    high = value.astype(BF16)
    return high, (value - high.astype(F32)).astype(BF16)


def mm(a, b):
    return jnp.dot(a, b, preferred_element_type=F32)


def mm_nt(a, b):
    return lax.dot_general(a, b, (((1,), (1,)), ((), ())), preferred_element_type=F32)


HBM = pl.BlockSpec(memory_space=pltpu.HBM)


def forward_kernel(
    u_hbm, p_hbm, c_hbm, ty_hbm, wz_hbm, sc_hbm, o_hbm, o_ref, u_ref, p_ref, c_ref, ty_ref, wz_ref, sc_ref, xc_ref, xs_ref, sems, tsems, osems
):
    def chunk(src, dst, row, step):
        at = pl.ds(CUTS[step], CUTS[step + 1] - CUTS[step])
        return pltpu.make_async_copy(src.at[at], dst.at[at], sems.at[row, step])

    table = pltpu.make_async_copy(ty_hbm, ty_ref, tsems.at[0])
    late = [
        pltpu.make_async_copy(wz_hbm, wz_ref, tsems.at[1]),
        pltpu.make_async_copy(sc_hbm, sc_ref, tsems.at[2]),
    ]
    def fetch(step):
        chunk(p_hbm, p_ref, 1, step).start()
        chunk(c_hbm, c_ref, 2, step).start()
        chunk(u_hbm, u_ref, 0, step).start()

    fetch(0)
    table.start()
    for step in range(1, AHEAD):
        fetch(step)
    for one in late:
        one.start()
    table.wait()

    def arrived(step):
        for row, (src, dst) in enumerate(((u_hbm, u_ref), (p_hbm, p_ref), (c_hbm, c_ref))):
            chunk(src, dst, row, step).wait()

    def slope_of(k):
        if True:
            arg = p_ref[k].astype(F32) * math.sqrt(0.5)
            bell = jnp.exp2((arg * (-math.log2(math.e))) * arg) * (2.0 / math.sqrt(math.pi))
            slope = (lax.erf(arg) + 1.0) + arg * bell
            c_ref[k] = (c_ref[k].astype(F32) * slope).astype(BF16)

    ty = ty_ref[...]

    def image(k):
        if True:
            both = jnp.concatenate([u_ref[k], c_ref[k]], axis=1)
            part = mm(ty, jnp.concatenate([both, both], axis=0))
            base = (k // C) * 64 + k % C
            xc_ref[pl.ds(base, MY, stride=PAD), :] = part[:16, :128]
            xs_ref[pl.ds(base, MY, stride=PAD), :] = part[16:, :128]
            xc_ref[pl.ds(base + 32, MY, stride=PAD), :] = part[:16, 128:]
            xs_ref[pl.ds(base + 32, MY, stride=PAD), :] = part[16:, 128:]

    for step in range(len(CUTS)):
        if step < len(CUTS) - 1:
            arrived(step)
            if step + AHEAD < len(CUTS) - 1:
                fetch(step + AHEAD)
        if step < len(CUTS) - 1:
            for k in range(CUTS[step], CUTS[step + 1]):
                slope_of(k)
                if k >= 2:
                    image(k - 2)
        else:
            image(62)
            image(63)
    for one in late:
        one.wait()
    wz = wz_ref[...]
    scale = sc_ref[...]

    def send(part):
        at = pl.ds(part * 16, 16)
        return pltpu.make_async_copy(o_ref.at[at], o_hbm.at[at], osems.at[part])

    for b in range(MY):
        rows = slice(b * PAD, b * PAD + 128)
        both = jnp.concatenate([xc_ref[rows, :].astype(BF16), xs_ref[rows, :].astype(BF16)], axis=1)
        res = mm_nt(wz, both)
        res = res * scale
        for q in range(4):
            o_ref[(b * 4 + q) ^ TURN] = res[q * 8 : (q + 1) * 8]
        if b % 4 == 3:
            send(b // 4 ^ TURN // 16).start()
    for part in range(4):
        send(part).wait()


def forward(u, pre, cot):
    big = pltpu.VMEM((IMGS, NY, NZ), BF16)
    flat = pltpu.VMEM((MY * PAD, 128), F32)
    return pl.pallas_call(
        forward_kernel,
        out_shape=jax.ShapeDtypeStruct((SLABS, 8, 128), F32),
        in_specs=[HBM] * 6,
        out_specs=HBM,
        scratch_shapes=[
            pltpu.VMEM((SLABS, 8, 128), F32),
            big,
            big,
            big,
            pltpu.VMEM((32, 256), BF16),
            pltpu.VMEM((32, 256), BF16),
            pltpu.VMEM((32, 128), F32),
            flat,
            flat,
            pltpu.SemaphoreType.DMA((3, (len(CUTS) - 1))),
            pltpu.SemaphoreType.DMA((3,)),
            pltpu.SemaphoreType.DMA((4,)),
        ],
        name="fwd_local",
    )(u, pre, cot, T["fwd_y"], T["fwd_z"], T["scale"])


def widen_kernel(w_ref, o_ref):
    for a in range(MX):
        o_ref[pl.ds(4 * a, 4), :] = w_ref[a].astype(F32)


def widen(weights):
    return pl.pallas_call(
        widen_kernel,
        out_shape=jax.ShapeDtypeStruct((MX * OWN, 2 * C * C), F32),
        in_specs=[pl.BlockSpec(memory_space=pltpu.VMEM)],
        out_specs=pl.BlockSpec(memory_space=pltpu.VMEM),
        compiler_params=pltpu.CompilerParams(vmem_limit_bytes=4 << 20),
        name="widen",
    )(weights)


def middle_kernel(
    mine_ref, m_ref, wf_ref, lx_ref, rg_ref, red_ref, ld_ref, own0_ref, own1_ref, own2_ref, own3_ref, d_ref, own_ref, q_ref
):
    lx = lx_ref[...]
    lane = lax.broadcasted_iota(jnp.int32, (MX, 128), 1)
    left = lane < 64
    for cr in range(OWN):
        rhs = jnp.concatenate(
            [m_ref[pl.ds(cr, SLABS, stride=8), :], m_ref[pl.ds(4 + cr, SLABS, stride=8), :]], axis=0
        )
        hi, lo = split(rhs)
        res = mm(lx, hi)
        res = res[:64] + res[64:] + mm(lx[:64], lo)
        summed = res[:32] + pltpu.roll(res[32:], 64, 1)
        own_ref[pl.ds(cr, MX, stride=OWN), :] = jnp.where(
            left, summed[:16], pltpu.roll(summed[16:], 64, 1)
        )
    mine = mine_ref[...]
    quarter = [own_ref[c * 16 : (c + 1) * 16, :] for c in range(4)]
    for other, ref in zip(OTHERS, (own0_ref, own1_ref, own2_ref, own3_ref)):
        piece = quarter[3 ^ other]
        for c in range(3):
            piece = jnp.where(mine == c, quarter[c ^ other], piece)
        ref[...] = piece
    hi, lo = split(own_ref[...])
    rg = rg_ref[...]
    grep = mm(hi, rg) + mm(lo, rg)
    g_real, g_imag = grep[:, :128], grep[:, 128:]
    acc = jnp.zeros((MX * OWN, 128), F32)
    slot = (lax.broadcasted_iota(jnp.int32, (MX * OWN, 128), 1) // 4) % 8
    red = red_ref[...]
    for t in range(8):
        w_real = wf_ref[:, t * 128 : (t + 1) * 128]
        w_imag = wf_ref[:, 1024 + t * 128 : 1024 + (t + 1) * 128]
        rhi, rlo = split(w_real * g_real + w_imag * g_imag)
        ihi, ilo = split(w_real * g_imag - w_imag * g_real)
        res = mm(jnp.concatenate([rhi, ihi], axis=1), red)
        res += mm(jnp.concatenate([rlo, ilo], axis=1), red)
        acc = jnp.where(slot == t, res, acc)
    q_ref[...] = acc
    ld = ld_ref[...]
    for cr in range(OWN):
        q = q_ref[pl.ds(cr, MX, stride=OWN), :]
        r = pltpu.roll(q, 64, 1)
        zero = jnp.zeros_like(q)
        rhs = jnp.concatenate(
            [
                jnp.where(left, q, zero),
                jnp.where(left, r, zero),
                jnp.where(left, zero, r),
                jnp.where(left, zero, q),
            ],
            axis=0,
        )
        hi, lo = split(rhs)
        d_ref[pl.ds(cr, SLABS, stride=OWN), :] = mm(ld, jnp.concatenate([hi, lo, hi], axis=0))


def middle(mine, moved, weights):
    return pl.pallas_call(
        middle_kernel,
        out_shape=(jax.ShapeDtypeStruct((16, 128), F32),) * 4
        + (jax.ShapeDtypeStruct((SLABS * OWN, 128), F32),),
        in_specs=[pl.BlockSpec(memory_space=pltpu.VMEM)] * 7,
        scratch_shapes=[
            pltpu.VMEM((MX * OWN, 128), F32),
            pltpu.VMEM((MX * OWN, 128), F32),
        ],
        compiler_params=pltpu.CompilerParams(vmem_limit_bytes=8 << 20),
        name="middle",
    )(mine, moved, weights, T["fwd_x"], T["rep_g"], T["red"], T["inv_x"])


def weight_grad(parts, rg_ref, ru_ref, o_ref):
    full = jnp.concatenate([part[...] for part in parts], axis=0)
    both = jnp.concatenate(split(full), axis=1)
    rg = rg_ref[...]
    ru = ru_ref[...]
    rg = jnp.concatenate([rg, rg], axis=0)
    ru = jnp.concatenate([ru, ru], axis=0)
    grep = mm(both, rg)
    g_real, g_imag = grep[:, :128], grep[:, 128:]
    slot = (lax.broadcasted_iota(jnp.int32, (64, 256), 1) // 4) % 8
    for t in range(8):
        urep = mm(jnp.where(slot == t, both, jnp.zeros_like(both)), ru)
        u_real, u_imag = urep[:, :128], urep[:, 128:]
        real = g_real * u_real + g_imag * u_imag
        imag = g_imag * u_real - g_real * u_imag
        real = real[:16] + real[16:32] + real[32:48] + real[48:]
        imag = imag[:16] + imag[16:32] + imag[32:48] + imag[48:]
        for a in range(4):
            o_ref[a, :, t * 128 : (t + 1) * 128] = real[a * 4 : (a + 1) * 4]
            o_ref[a, :, 1024 + t * 128 : 1024 + (t + 1) * 128] = imag[a * 4 : (a + 1) * 4]


def inverse_kernel(
    d_ref, tz_ref, ly_ref, s0_ref, s1_ref, s2_ref, s3_ref, rg_ref, ru_ref, o_hbm, gw_hbm, o_ref, gw_ref, f_ref, osems, gsem
):
    full = d_ref[...].astype(BF16)
    packed = []
    for odd in range(2):
        blocks = []
        for b in range(MY):
            at = ((b // 2 * 2 + odd) ^ BACK // 4) * MZ
            blocks.append(full[at : at + MZ])
        flat = jnp.concatenate(blocks, axis=0).T
        real = jnp.concatenate([flat[0:32], flat[64:96]], axis=0)
        imag = jnp.concatenate([flat[32:64], flat[96:128]], axis=0)
        for half in (slice(0, 128), slice(128, 256)):
            packed.append(jnp.concatenate([real[:, half], imag[:, half]], axis=1))
    tz = tz_ref[...]
    group = lax.broadcasted_iota(jnp.int32, (64, 256), 1) % 128 // (2 * MZ)
    for first in range(0, MY, ZB):
        rows = []
        for b in range(first, first + ZB):
            part = packed[b % 2 * 2 + b // 8]
            rows.append(jnp.where(group == b % 8 // 2, part, jnp.zeros_like(part)))
        res = mm(jnp.concatenate(rows, axis=0), tz)
        for b in range(first, first + ZB):
            h = res[(b - first) * 64 : (b - first + 1) * 64]
            for xx in range(PLANES):
                at = xx * C * IPAD + b
                f_ref[pl.ds(at, C, stride=IPAD), :] = h[xx * 32 : xx * 32 + 32, :128]
                f_ref[pl.ds(at + 16, C, stride=IPAD), :] = h[xx * 32 : xx * 32 + 32, 128:]

    def send(step):
        at = pl.ds(step * OSTEP, OSTEP)
        return pltpu.make_async_copy(o_ref.at[at], o_hbm.at[at], osems.at[step])

    weight_grad((s0_ref, s1_ref, s2_ref, s3_ref), rg_ref, ru_ref, gw_ref)
    store = pltpu.make_async_copy(gw_ref, gw_hbm, gsem)
    store.start()
    ly = ly_ref[...]
    for step in range(IMGS // OSTEP):
        for k in range(step * OSTEP, (step + 1) * OSTEP, 2):
            at = k * IPAD
            block = f_ref[pl.ds(at, 72), :]
            pair = jnp.concatenate([block[:32], block[36:68]], axis=1)
            hi, lo = split(pair)
            res = mm(ly, jnp.concatenate([hi, lo, hi], axis=0)).astype(BF16)
            o_ref[k] = res[:, :128]
            o_ref[k + 1] = res[:, 128:]
        send(step).start()
    store.wait()
    for step in range(IMGS // OSTEP):
        send(step).wait()


def inverse(spread, parts):
    return pl.pallas_call(
        inverse_kernel,
        out_shape=(
            jax.ShapeDtypeStruct((IMGS, NY, NZ), BF16),
            jax.ShapeDtypeStruct((4, OWN, 2 * C * C), F32),
        ),
        in_specs=[pl.BlockSpec(memory_space=pltpu.VMEM)] * 9,
        out_specs=(HBM, HBM),
        scratch_shapes=[
            pltpu.VMEM((IMGS, NY, NZ), BF16),
            pltpu.VMEM((4, OWN, 2 * C * C), F32),
            pltpu.VMEM((IMGS * IPAD, 128), F32),
            pltpu.SemaphoreType.DMA((IMGS // OSTEP,)),
            pltpu.SemaphoreType.DMA,
        ],
        compiler_params=pltpu.CompilerParams(vmem_limit_bytes=8 << 20),
        name="inv_local",
    )(spread, T["inv_z"], T["inv_y"], *parts, T["rep_g"], T["rep_u"])


def body(u_field, preact, cotangent, weights):
    shape = (IMGS, NY, NZ)
    partial = forward(u_field.reshape(shape), preact.reshape(shape), cotangent.reshape(shape))
    partial, weights = lax.optimization_barrier((partial, weights))
    mine = jnp.full((16, 128), lax.axis_index("dp"), jnp.int32)
    moved = lax.all_to_all(partial, "slab", split_axis=0, concat_axis=0, axis_index_groups=ORDER, tiled=True)
    wide = widen(weights)
    *pieces, back = middle(mine, moved.reshape(SLABS * 8, 128), wide)
    for at, other in enumerate(OTHERS):
        if other:
            pieces[at] = lax.ppermute(pieces[at], "dp", [(n, n ^ other) for n in range(4)])
    spread = lax.all_to_all(back, "slab", split_axis=0, concat_axis=0, axis_index_groups=BACK_ORDER, tiled=True)
    field_grad, grad_weights = inverse(spread, pieces)
    return grad_weights, field_grad.reshape(1, PLANES, C, NY, NZ)


def solution(mesh):
    placed = (
        P("dp", "slab", None, None, None),
        P("dp", "slab", None, None, None),
        P("dp", "slab", None, None, None),
        P(None, "slab", None),
    )
    return jax.shard_map(
        body,
        mesh=mesh,
        in_specs=placed,
        out_specs=(P("dp", "slab", None), P("dp", "slab", None, None, None)),
        check_vma=False,
    )
```

```python
import itertools
import math

import jax
import jax.numpy as jnp
import numpy as np
from jax import lax
from jax.experimental import pallas as pl
from jax.experimental.pallas import tpu as pltpu
from jax.sharding import PartitionSpec as P

C = 32
NX = 128
NY = 128
NZ = 128
MX = 16
MY = 16
MZ = 16
SLABS = 64
PLANES = NX // SLABS
IMGS = PLANES * C
OWN = MY * MZ // SLABS
F32 = jnp.float32
BF16 = jnp.bfloat16
AHEAD = 2
OTHERS = (0, 2, 3, 1)
TURN = 52
BACK = 52
ORDER = [[n ^ TURN for n in range(SLABS)]]
BACK_ORDER = [[n ^ BACK for n in range(SLABS)]]
CUTS = (0, 16, 40, 64)
OSTEP = 8
ZB = 2
PAD = 132
IPAD = 36


def np_twiddles(length, freqs):
    product = (np.arange(length, dtype=np.int64)[:, None] * freqs[None, :]) % length
    angle = product.astype(np.float32) * np.float32(2.0 * math.pi / length)
    return np.cos(angle).astype(np.float32), np.sin(angle).astype(np.float32)


def signed(count):
    index = np.arange(count)
    return np.where(index < count // 2, index, index - count)


def split_np(table):
    high = table.astype(jnp.bfloat16)
    low = (table - high.astype(np.float32)).astype(jnp.bfloat16)
    return high, low


def make_tables():
    cx, sx = np_twiddles(NX, signed(MX))
    cy, sy = np_twiddles(NY, signed(MY))
    cz, sz = np_twiddles(NZ, np.arange(MZ))
    t = {}
    rows = np.concatenate([cy.T, sy.T], 0)
    t["fwd_y"] = np.concatenate(split_np(rows), 1)
    low_c = cz.astype(jnp.bfloat16).astype(np.float32)
    low_s = (-sz).astype(jnp.bfloat16).astype(np.float32)
    real = np.concatenate([low_c, low_s], 0).T
    imag = np.concatenate([low_s, -low_c], 0).T
    wz = np.stack([real.reshape(4, 4, 2 * NZ), imag.reshape(4, 4, 2 * NZ)], 1)
    t["fwd_z"] = wz.reshape(2 * MZ, 2 * NZ).astype(jnp.bfloat16)
    mode_scale = np.where(np.arange(MZ) == 0, 0.5, 1.0) / (NX * NY * NZ)
    per_row = np.broadcast_to(mode_scale.reshape(4, 1, 4), (4, 2, 4)).reshape(2 * MZ, 1)
    is_g = (np.arange(128) // C) % 2 == 1
    t["scale"] = np.where(is_g[None, :], per_row, 1.0).astype(np.float32)
    cxs, sxs = cx.reshape(SLABS, PLANES, MX)[ORDER[0]], sx.reshape(SLABS, PLANES, MX)[ORDER[0]]
    lx = np.zeros((PLANES, 2, MX, 2, SLABS), np.float32)
    for xx in range(PLANES):
        lx[xx, 0, :, 0] = cxs[:, xx].T
        lx[xx, 0, :, 1] = sxs[:, xx].T
        lx[xx, 1, :, 0] = -sxs[:, xx].T
        lx[xx, 1, :, 1] = cxs[:, xx].T
    t["fwd_x"] = np.concatenate(split_np(lx.reshape(PLANES * 2 * MX, 2 * SLABS)), 0)
    rep = np.zeros((128, 2, 4, C), np.float32)
    for part in range(2):
        for ch in range(C):
            rep[part * 64 + 32 + ch, part, :, ch] = 1.0
    t["rep_g"] = rep.reshape(128, 256).astype(jnp.bfloat16)
    rep = np.zeros((2, 2, 8, 4, 2, 4, C), np.float32)
    for part in range(2):
        for r in range(4):
            rep[part, 0, :, r, part, r, :] = 1.0
    t["rep_u"] = rep.reshape(128, 256).astype(jnp.bfloat16)
    red = np.zeros((2, 4, C, 4, 8, 4), np.float32)
    for r in range(4):
        red[0, r, :, 0, :, r] = 1.0
        red[1, r, :, 1, :, r] = 1.0
        red[1, r, :, 2, :, r] = -1.0
        red[0, r, :, 3, :, r] = 1.0
    t["red"] = red.reshape(256, 128).astype(jnp.bfloat16)
    cxb, sxb = cx.reshape(SLABS, PLANES, MX)[BACK_ORDER[0]], sx.reshape(SLABS, PLANES, MX)[BACK_ORDER[0]]
    ld = np.stack([cxb, sxb], 2).reshape(SLABS, PLANES * 2 * MX)
    high, low = split_np(ld)
    t["inv_x"] = np.concatenate([high, high, low], 1)
    czb, szb = ((v.T.reshape(4, 4, NZ)[np.arange(4) ^ BACK % 4]).reshape(MZ, NZ) for v in (cz, sz))
    tz = np.stack([np.concatenate([czb, szb], 1), np.concatenate([-szb, czb], 1)])
    tz = np.broadcast_to(tz[:, None], (2, 8, MZ, 2 * NZ)).reshape(256, 2 * NZ)
    high, low = split_np(tz)
    odd = (np.arange(256) // MZ % 2 == 1)[:, None]
    t["inv_z"] = np.where(odd, low, high)
    ly = np.concatenate([cy, -sy], 1)
    high, low = split_np(ly)
    t["inv_y"] = np.concatenate([high, high, low], 1)
    return t


T = make_tables()


def split(value):
    high = value.astype(BF16)
    return high, (value - high.astype(F32)).astype(BF16)


def mm(a, b):
    return jnp.dot(a, b, preferred_element_type=F32)


def mm_nt(a, b):
    return lax.dot_general(a, b, (((1,), (1,)), ((), ())), preferred_element_type=F32)


HBM = pl.BlockSpec(memory_space=pltpu.HBM)


def forward_kernel(
    u_hbm, p_hbm, c_hbm, ty_hbm, wz_hbm, sc_hbm, o_hbm, o_ref, u_ref, p_ref, c_ref, ty_ref, wz_ref, sc_ref, xc_ref, xs_ref, sems, tsems, osems
):
    def chunk(src, dst, row, step):
        at = pl.ds(CUTS[step], CUTS[step + 1] - CUTS[step])
        return pltpu.make_async_copy(src.at[at], dst.at[at], sems.at[row, step])

    table = pltpu.make_async_copy(ty_hbm, ty_ref, tsems.at[0])
    late = [
        pltpu.make_async_copy(wz_hbm, wz_ref, tsems.at[1]),
        pltpu.make_async_copy(sc_hbm, sc_ref, tsems.at[2]),
    ]
    def fetch(step):
        chunk(p_hbm, p_ref, 1, step).start()
        chunk(c_hbm, c_ref, 2, step).start()
        chunk(u_hbm, u_ref, 0, step).start()

    fetch(0)
    table.start()
    for step in range(1, AHEAD):
        fetch(step)
    for one in late:
        one.start()
    table.wait()

    def arrived(step):
        for row, (src, dst) in enumerate(((u_hbm, u_ref), (p_hbm, p_ref), (c_hbm, c_ref))):
            chunk(src, dst, row, step).wait()

    def slope_of(k):
        if True:
            arg = p_ref[k].astype(F32) * math.sqrt(0.5)
            bell = jnp.exp2((arg * (-math.log2(math.e))) * arg) * (2.0 / math.sqrt(math.pi))
            slope = (lax.erf(arg) + 1.0) + arg * bell
            c_ref[k] = (c_ref[k].astype(F32) * slope).astype(BF16)

    ty = ty_ref[...]

    def image(k):
        if True:
            both = jnp.concatenate([u_ref[k], c_ref[k]], axis=1)
            part = mm(ty, jnp.concatenate([both, both], axis=0))
            base = (k // C) * 64 + k % C
            xc_ref[pl.ds(base, MY, stride=PAD), :] = part[:16, :128]
            xs_ref[pl.ds(base, MY, stride=PAD), :] = part[16:, :128]
            xc_ref[pl.ds(base + 32, MY, stride=PAD), :] = part[:16, 128:]
            xs_ref[pl.ds(base + 32, MY, stride=PAD), :] = part[16:, 128:]

    for step in range(len(CUTS)):
        if step < len(CUTS) - 1:
            arrived(step)
            if step + AHEAD < len(CUTS) - 1:
                fetch(step + AHEAD)
        if step < len(CUTS) - 1:
            for k in range(CUTS[step], CUTS[step + 1]):
                slope_of(k)
                if k >= 2:
                    image(k - 2)
        else:
            image(62)
            image(63)
    for one in late:
        one.wait()
    wz = wz_ref[...]
    scale = sc_ref[...]

    def send(part):
        at = pl.ds(part * 16, 16)
        return pltpu.make_async_copy(o_ref.at[at], o_hbm.at[at], osems.at[part])

    for b in range(MY):
        rows = slice(b * PAD, b * PAD + 128)
        both = jnp.concatenate([xc_ref[rows, :].astype(BF16), xs_ref[rows, :].astype(BF16)], axis=1)
        res = mm_nt(wz, both)
        res = res * scale
        for q in range(4):
            o_ref[(b * 4 + q) ^ TURN] = res[q * 8 : (q + 1) * 8]
        if b % 4 == 3:
            send(b // 4 ^ TURN // 16).start()
    for part in range(4):
        send(part).wait()


def forward(u, pre, cot):
    big = pltpu.VMEM((IMGS, NY, NZ), BF16)
    flat = pltpu.VMEM((MY * PAD, 128), F32)
    return pl.pallas_call(
        forward_kernel,
        out_shape=jax.ShapeDtypeStruct((SLABS, 8, 128), F32),
        in_specs=[HBM] * 6,
        out_specs=HBM,
        scratch_shapes=[
            pltpu.VMEM((SLABS, 8, 128), F32),
            big,
            big,
            big,
            pltpu.VMEM((32, 256), BF16),
            pltpu.VMEM((32, 256), BF16),
            pltpu.VMEM((32, 128), F32),
            flat,
            flat,
            pltpu.SemaphoreType.DMA((3, (len(CUTS) - 1))),
            pltpu.SemaphoreType.DMA((3,)),
            pltpu.SemaphoreType.DMA((4,)),
        ],
        name="fwd_local",
    )(u, pre, cot, T["fwd_y"], T["fwd_z"], T["scale"])


def widen_kernel(w_ref, o_ref):
    for a in range(MX):
        o_ref[pl.ds(4 * a, 4), :] = w_ref[a].astype(F32)


def widen(weights):
    return pl.pallas_call(
        widen_kernel,
        out_shape=jax.ShapeDtypeStruct((MX * OWN, 2 * C * C), F32),
        in_specs=[pl.BlockSpec(memory_space=pltpu.VMEM)],
        out_specs=pl.BlockSpec(memory_space=pltpu.VMEM),
        compiler_params=pltpu.CompilerParams(vmem_limit_bytes=4 << 20),
        name="widen",
    )(weights)


def middle_kernel(
    mine_ref, m_ref, wf_ref, lx_ref, rg_ref, red_ref, ld_ref, own0_ref, own1_ref, own2_ref, own3_ref, d_ref, own_ref, q_ref
):
    lx = lx_ref[...]
    lane = lax.broadcasted_iota(jnp.int32, (MX, 128), 1)
    left = lane < 64
    for cr in range(OWN):
        rhs = jnp.concatenate(
            [m_ref[pl.ds(cr, SLABS, stride=8), :], m_ref[pl.ds(4 + cr, SLABS, stride=8), :]], axis=0
        )
        hi, lo = split(rhs)
        res = mm(lx, hi)
        res = res[:64] + res[64:] + mm(lx[:64], lo)
        summed = res[:32] + pltpu.roll(res[32:], 64, 1)
        own_ref[pl.ds(cr, MX, stride=OWN), :] = jnp.where(
            left, summed[:16], pltpu.roll(summed[16:], 64, 1)
        )
    mine = mine_ref[...]
    quarter = [own_ref[c * 16 : (c + 1) * 16, :] for c in range(4)]
    for other, ref in zip(OTHERS, (own0_ref, own1_ref, own2_ref, own3_ref)):
        piece = quarter[3 ^ other]
        for c in range(3):
            piece = jnp.where(mine == c, quarter[c ^ other], piece)
        ref[...] = piece
    hi, lo = split(own_ref[...])
    rg = rg_ref[...]
    grep = mm(hi, rg) + mm(lo, rg)
    g_real, g_imag = grep[:, :128], grep[:, 128:]
    acc = jnp.zeros((MX * OWN, 128), F32)
    slot = (lax.broadcasted_iota(jnp.int32, (MX * OWN, 128), 1) // 4) % 8
    red = red_ref[...]
    for t in range(8):
        w_real = wf_ref[:, t * 128 : (t + 1) * 128]
        w_imag = wf_ref[:, 1024 + t * 128 : 1024 + (t + 1) * 128]
        rhi, rlo = split(w_real * g_real + w_imag * g_imag)
        ihi, ilo = split(w_real * g_imag - w_imag * g_real)
        res = mm(jnp.concatenate([rhi, ihi], axis=1), red)
        res += mm(jnp.concatenate([rlo, ilo], axis=1), red)
        acc = jnp.where(slot == t, res, acc)
    q_ref[...] = acc
    ld = ld_ref[...]
    for cr in range(OWN):
        q = q_ref[pl.ds(cr, MX, stride=OWN), :]
        r = pltpu.roll(q, 64, 1)
        zero = jnp.zeros_like(q)
        rhs = jnp.concatenate(
            [
                jnp.where(left, q, zero),
                jnp.where(left, r, zero),
                jnp.where(left, zero, r),
                jnp.where(left, zero, q),
            ],
            axis=0,
        )
        hi, lo = split(rhs)
        d_ref[pl.ds(cr, SLABS, stride=OWN), :] = mm(ld, jnp.concatenate([hi, lo, hi], axis=0))


def middle(mine, moved, weights):
    return pl.pallas_call(
        middle_kernel,
        out_shape=(jax.ShapeDtypeStruct((16, 128), F32),) * 4
        + (jax.ShapeDtypeStruct((SLABS * OWN, 128), F32),),
        in_specs=[pl.BlockSpec(memory_space=pltpu.VMEM)] * 7,
        scratch_shapes=[
            pltpu.VMEM((MX * OWN, 128), F32),
            pltpu.VMEM((MX * OWN, 128), F32),
        ],
        compiler_params=pltpu.CompilerParams(vmem_limit_bytes=8 << 20),
        name="middle",
    )(mine, moved, weights, T["fwd_x"], T["rep_g"], T["red"], T["inv_x"])


def weight_grad_kernel(s0_ref, s1_ref, s2_ref, s3_ref, rg_ref, ru_ref, o_ref):
    parts = (s0_ref, s1_ref, s2_ref, s3_ref)
    full = jnp.concatenate([part[...] for part in parts], axis=0)
    both = jnp.concatenate(split(full), axis=1)
    rg = rg_ref[...]
    ru = ru_ref[...]
    rg = jnp.concatenate([rg, rg], axis=0)
    ru = jnp.concatenate([ru, ru], axis=0)
    grep = mm(both, rg)
    g_real, g_imag = grep[:, :128], grep[:, 128:]
    slot = (lax.broadcasted_iota(jnp.int32, (64, 256), 1) // 4) % 8
    for t in range(8):
        urep = mm(jnp.where(slot == t, both, jnp.zeros_like(both)), ru)
        u_real, u_imag = urep[:, :128], urep[:, 128:]
        real = g_real * u_real + g_imag * u_imag
        imag = g_imag * u_real - g_real * u_imag
        real = real[:16] + real[16:32] + real[32:48] + real[48:]
        imag = imag[:16] + imag[16:32] + imag[32:48] + imag[48:]
        for a in range(4):
            o_ref[a, :, t * 128 : (t + 1) * 128] = real[a * 4 : (a + 1) * 4]
            o_ref[a, :, 1024 + t * 128 : 1024 + (t + 1) * 128] = imag[a * 4 : (a + 1) * 4]


def weight_grad(parts):
    return pl.pallas_call(
        weight_grad_kernel,
        out_shape=jax.ShapeDtypeStruct((4, OWN, 2 * C * C), F32),
        compiler_params=pltpu.CompilerParams(vmem_limit_bytes=4 << 20),
        name="weight_grad",
    )(*parts, T["rep_g"], T["rep_u"])


def inverse_kernel(
    d_ref, tz_ref, ly_ref, o_hbm, o_ref, f_ref, osems
):
    full = d_ref[...].astype(BF16)
    packed = []
    for odd in range(2):
        blocks = []
        for b in range(MY):
            at = ((b // 2 * 2 + odd) ^ BACK // 4) * MZ
            blocks.append(full[at : at + MZ])
        flat = jnp.concatenate(blocks, axis=0).T
        real = jnp.concatenate([flat[0:32], flat[64:96]], axis=0)
        imag = jnp.concatenate([flat[32:64], flat[96:128]], axis=0)
        for half in (slice(0, 128), slice(128, 256)):
            packed.append(jnp.concatenate([real[:, half], imag[:, half]], axis=1))
    tz = tz_ref[...]
    group = lax.broadcasted_iota(jnp.int32, (64, 256), 1) % 128 // (2 * MZ)
    for first in range(0, MY, ZB):
        rows = []
        for b in range(first, first + ZB):
            part = packed[b % 2 * 2 + b // 8]
            rows.append(jnp.where(group == b % 8 // 2, part, jnp.zeros_like(part)))
        res = mm(jnp.concatenate(rows, axis=0), tz)
        for b in range(first, first + ZB):
            h = res[(b - first) * 64 : (b - first + 1) * 64]
            for xx in range(PLANES):
                at = xx * C * IPAD + b
                f_ref[pl.ds(at, C, stride=IPAD), :] = h[xx * 32 : xx * 32 + 32, :128]
                f_ref[pl.ds(at + 16, C, stride=IPAD), :] = h[xx * 32 : xx * 32 + 32, 128:]

    def send(step):
        at = pl.ds(step * OSTEP, OSTEP)
        return pltpu.make_async_copy(o_ref.at[at], o_hbm.at[at], osems.at[step])

    ly = ly_ref[...]
    for step in range(IMGS // OSTEP):
        for k in range(step * OSTEP, (step + 1) * OSTEP, 2):
            at = k * IPAD
            block = f_ref[pl.ds(at, 72), :]
            pair = jnp.concatenate([block[:32], block[36:68]], axis=1)
            hi, lo = split(pair)
            res = mm(ly, jnp.concatenate([hi, lo, hi], axis=0)).astype(BF16)
            o_ref[k] = res[:, :128]
            o_ref[k + 1] = res[:, 128:]
        send(step).start()
    for step in range(IMGS // OSTEP):
        send(step).wait()


def inverse(spread):
    return pl.pallas_call(
        inverse_kernel,
        out_shape=jax.ShapeDtypeStruct((IMGS, NY, NZ), BF16),
        in_specs=[pl.BlockSpec(memory_space=pltpu.VMEM)] * 3,
        out_specs=HBM,
        scratch_shapes=[
            pltpu.VMEM((IMGS, NY, NZ), BF16),
            pltpu.VMEM((IMGS * IPAD, 128), F32),
            pltpu.SemaphoreType.DMA((IMGS // OSTEP,)),
        ],
        compiler_params=pltpu.CompilerParams(vmem_limit_bytes=8 << 20),
        name="inv_local",
    )(spread, T["inv_z"], T["inv_y"])


def body(u_field, preact, cotangent, weights):
    shape = (IMGS, NY, NZ)
    partial = forward(u_field.reshape(shape), preact.reshape(shape), cotangent.reshape(shape))
    partial, weights = lax.optimization_barrier((partial, weights))
    mine = jnp.full((16, 128), lax.axis_index("dp"), jnp.int32)
    moved = lax.all_to_all(partial, "slab", split_axis=0, concat_axis=0, axis_index_groups=ORDER, tiled=True)
    wide = widen(weights)
    *pieces, back = middle(mine, moved.reshape(SLABS * 8, 128), wide)
    for at, other in enumerate(OTHERS):
        if other:
            pieces[at] = lax.ppermute(pieces[at], "dp", [(n, n ^ other) for n in range(4)])
    spread = lax.all_to_all(back, "slab", split_axis=0, concat_axis=0, axis_index_groups=BACK_ORDER, tiled=True)
    field_grad = inverse(spread)
    pieces, field_grad = lax.optimization_barrier((pieces, field_grad))
    grad_weights = weight_grad(pieces)
    return grad_weights, field_grad.reshape(1, PLANES, C, NY, NZ)


def solution(mesh):
    placed = (
        P("dp", "slab", None, None, None),
        P("dp", "slab", None, None, None),
        P("dp", "slab", None, None, None),
        P(None, "slab", None),
    )
    return jax.shard_map(
        body,
        mesh=mesh,
        in_specs=placed,
        out_specs=(P("dp", "slab", None), P("dp", "slab", None, None, None)),
        check_vma=False,
    )
```

```python
import itertools
import math

import jax
import jax.numpy as jnp
import numpy as np
from jax import lax
from jax.experimental import pallas as pl
from jax.experimental.pallas import tpu as pltpu
from jax.sharding import PartitionSpec as P

C = 32
NX = 128
NY = 128
NZ = 128
MX = 16
MY = 16
MZ = 16
SLABS = 64
PLANES = NX // SLABS
IMGS = PLANES * C
OWN = MY * MZ // SLABS
F32 = jnp.float32
BF16 = jnp.bfloat16
AHEAD = 2
TURN = 52
BACK = 52
ORDER = [[n ^ TURN for n in range(SLABS)]]
BACK_ORDER = [[n ^ BACK for n in range(SLABS)]]
CUTS = (0, 16, 40, 64)
OSTEP = 8
ZB = 2
PAD = 132
IPAD = 36


def np_twiddles(length, freqs):
    product = (np.arange(length, dtype=np.int64)[:, None] * freqs[None, :]) % length
    angle = product.astype(np.float32) * np.float32(2.0 * math.pi / length)
    return np.cos(angle).astype(np.float32), np.sin(angle).astype(np.float32)


def signed(count):
    index = np.arange(count)
    return np.where(index < count // 2, index, index - count)


def split_np(table):
    high = table.astype(jnp.bfloat16)
    low = (table - high.astype(np.float32)).astype(jnp.bfloat16)
    return high, low


def make_tables():
    cx, sx = np_twiddles(NX, signed(MX))
    cy, sy = np_twiddles(NY, signed(MY))
    cz, sz = np_twiddles(NZ, np.arange(MZ))
    t = {}
    rows = np.concatenate([cy.T, sy.T], 0)
    t["fwd_y"] = np.concatenate(split_np(rows), 1)
    low_c = cz.astype(jnp.bfloat16).astype(np.float32)
    low_s = (-sz).astype(jnp.bfloat16).astype(np.float32)
    real = np.concatenate([low_c, low_s], 0).T
    imag = np.concatenate([low_s, -low_c], 0).T
    wz = np.stack([real.reshape(4, 4, 2 * NZ), imag.reshape(4, 4, 2 * NZ)], 1)
    t["fwd_z"] = wz.reshape(2 * MZ, 2 * NZ).astype(jnp.bfloat16)
    mode_scale = np.where(np.arange(MZ) == 0, 0.5, 1.0) / (NX * NY * NZ)
    per_row = np.broadcast_to(mode_scale.reshape(4, 1, 4), (4, 2, 4)).reshape(2 * MZ, 1)
    is_g = (np.arange(128) // C) % 2 == 1
    t["scale"] = np.where(is_g[None, :], per_row, 1.0).astype(np.float32)
    cxs, sxs = cx.reshape(SLABS, PLANES, MX)[ORDER[0]], sx.reshape(SLABS, PLANES, MX)[ORDER[0]]
    lx = np.zeros((PLANES, 2, MX, 2, SLABS), np.float32)
    for xx in range(PLANES):
        lx[xx, 0, :, 0] = cxs[:, xx].T
        lx[xx, 0, :, 1] = sxs[:, xx].T
        lx[xx, 1, :, 0] = -sxs[:, xx].T
        lx[xx, 1, :, 1] = cxs[:, xx].T
    t["fwd_x"] = np.concatenate(split_np(lx.reshape(PLANES * 2 * MX, 2 * SLABS)), 0)
    rep = np.zeros((128, 2, 4, C), np.float32)
    for part in range(2):
        for ch in range(C):
            rep[part * 64 + 32 + ch, part, :, ch] = 1.0
    t["rep_g"] = rep.reshape(128, 256).astype(jnp.bfloat16)
    rep = np.zeros((2, 2, 8, 4, 2, 4, C), np.float32)
    for part in range(2):
        for r in range(4):
            rep[part, 0, :, r, part, r, :] = 1.0
    t["rep_u"] = rep.reshape(128, 256).astype(jnp.bfloat16)
    red = np.zeros((2, 4, C, 4, 8, 4), np.float32)
    for r in range(4):
        red[0, r, :, 0, :, r] = 1.0
        red[1, r, :, 1, :, r] = 1.0
        red[1, r, :, 2, :, r] = -1.0
        red[0, r, :, 3, :, r] = 1.0
    t["red"] = red.reshape(256, 128).astype(jnp.bfloat16)
    cxb, sxb = cx.reshape(SLABS, PLANES, MX)[BACK_ORDER[0]], sx.reshape(SLABS, PLANES, MX)[BACK_ORDER[0]]
    ld = np.stack([cxb, sxb], 2).reshape(SLABS, PLANES * 2 * MX)
    high, low = split_np(ld)
    t["inv_x"] = np.concatenate([high, high, low], 1)
    czb, szb = ((v.T.reshape(4, 4, NZ)[np.arange(4) ^ BACK % 4]).reshape(MZ, NZ) for v in (cz, sz))
    tz = np.stack([np.concatenate([czb, szb], 1), np.concatenate([-szb, czb], 1)])
    tz = np.broadcast_to(tz[:, None], (2, 8, MZ, 2 * NZ)).reshape(256, 2 * NZ)
    high, low = split_np(tz)
    odd = (np.arange(256) // MZ % 2 == 1)[:, None]
    t["inv_z"] = np.where(odd, low, high)
    ly = np.concatenate([cy, -sy], 1)
    high, low = split_np(ly)
    t["inv_y"] = np.concatenate([high, high, low], 1)
    return t


T = make_tables()


def split(value):
    high = value.astype(BF16)
    return high, (value - high.astype(F32)).astype(BF16)


def mm(a, b):
    return jnp.dot(a, b, preferred_element_type=F32)


def mm_nt(a, b):
    return lax.dot_general(a, b, (((1,), (1,)), ((), ())), preferred_element_type=F32)


HBM = pl.BlockSpec(memory_space=pltpu.HBM)


def forward_kernel(
    u_hbm, p_hbm, c_hbm, ty_hbm, wz_hbm, sc_hbm, o_hbm, o_ref, u_ref, p_ref, c_ref, ty_ref, wz_ref, sc_ref, xc_ref, xs_ref, sems, tsems, osems
):
    def chunk(src, dst, row, step):
        at = pl.ds(CUTS[step], CUTS[step + 1] - CUTS[step])
        return pltpu.make_async_copy(src.at[at], dst.at[at], sems.at[row, step])

    table = pltpu.make_async_copy(ty_hbm, ty_ref, tsems.at[0])
    late = [
        pltpu.make_async_copy(wz_hbm, wz_ref, tsems.at[1]),
        pltpu.make_async_copy(sc_hbm, sc_ref, tsems.at[2]),
    ]
    def fetch(step):
        chunk(p_hbm, p_ref, 1, step).start()
        chunk(c_hbm, c_ref, 2, step).start()
        chunk(u_hbm, u_ref, 0, step).start()

    fetch(0)
    table.start()
    for step in range(1, AHEAD):
        fetch(step)
    for one in late:
        one.start()
    table.wait()

    def arrived(step):
        for row, (src, dst) in enumerate(((u_hbm, u_ref), (p_hbm, p_ref), (c_hbm, c_ref))):
            chunk(src, dst, row, step).wait()

    def slope_of(k):
        if True:
            arg = p_ref[k].astype(F32) * math.sqrt(0.5)
            bell = jnp.exp2((arg * (-math.log2(math.e))) * arg) * (2.0 / math.sqrt(math.pi))
            slope = (lax.erf(arg) + 1.0) + arg * bell
            c_ref[k] = (c_ref[k].astype(F32) * slope).astype(BF16)

    ty = ty_ref[...]

    def image(k):
        if True:
            both = jnp.concatenate([u_ref[k], c_ref[k]], axis=1)
            part = mm(ty, jnp.concatenate([both, both], axis=0))
            base = (k // C) * 64 + k % C
            xc_ref[pl.ds(base, MY, stride=PAD), :] = part[:16, :128]
            xs_ref[pl.ds(base, MY, stride=PAD), :] = part[16:, :128]
            xc_ref[pl.ds(base + 32, MY, stride=PAD), :] = part[:16, 128:]
            xs_ref[pl.ds(base + 32, MY, stride=PAD), :] = part[16:, 128:]

    for step in range(len(CUTS)):
        if step < len(CUTS) - 1:
            arrived(step)
            if step + AHEAD < len(CUTS) - 1:
                fetch(step + AHEAD)
        if step < len(CUTS) - 1:
            for k in range(CUTS[step], CUTS[step + 1]):
                slope_of(k)
                if k >= 2:
                    image(k - 2)
        else:
            image(62)
            image(63)
    for one in late:
        one.wait()
    wz = wz_ref[...]
    scale = sc_ref[...]

    def send(part):
        at = pl.ds(part * 16, 16)
        return pltpu.make_async_copy(o_ref.at[at], o_hbm.at[at], osems.at[part])

    for b in range(MY):
        rows = slice(b * PAD, b * PAD + 128)
        both = jnp.concatenate([xc_ref[rows, :].astype(BF16), xs_ref[rows, :].astype(BF16)], axis=1)
        res = mm_nt(wz, both)
        res = res * scale
        for q in range(4):
            o_ref[(b * 4 + q) ^ TURN] = res[q * 8 : (q + 1) * 8]
        if b % 4 == 3:
            send(b // 4 ^ TURN // 16).start()
    for part in range(4):
        send(part).wait()


def forward(u, pre, cot):
    big = pltpu.VMEM((IMGS, NY, NZ), BF16)
    flat = pltpu.VMEM((MY * PAD, 128), F32)
    return pl.pallas_call(
        forward_kernel,
        out_shape=jax.ShapeDtypeStruct((SLABS, 8, 128), F32),
        in_specs=[HBM] * 6,
        out_specs=HBM,
        scratch_shapes=[
            pltpu.VMEM((SLABS, 8, 128), F32),
            big,
            big,
            big,
            pltpu.VMEM((32, 256), BF16),
            pltpu.VMEM((32, 256), BF16),
            pltpu.VMEM((32, 128), F32),
            flat,
            flat,
            pltpu.SemaphoreType.DMA((3, (len(CUTS) - 1))),
            pltpu.SemaphoreType.DMA((3,)),
            pltpu.SemaphoreType.DMA((4,)),
        ],
        name="fwd_local",
    )(u, pre, cot, T["fwd_y"], T["fwd_z"], T["scale"])


def widen_kernel(w_ref, o_ref):
    for a in range(MX):
        o_ref[pl.ds(4 * a, 4), :] = w_ref[a].astype(F32)


def widen(weights):
    return pl.pallas_call(
        widen_kernel,
        out_shape=jax.ShapeDtypeStruct((MX * OWN, 2 * C * C), F32),
        in_specs=[pl.BlockSpec(memory_space=pltpu.VMEM)],
        out_specs=pl.BlockSpec(memory_space=pltpu.VMEM),
        compiler_params=pltpu.CompilerParams(vmem_limit_bytes=4 << 20),
        name="widen",
    )(weights)


def middle_kernel(
    mine_ref, m_ref, wf_ref, lx_ref, rg_ref, red_ref, ld_ref, own0_ref, own13_ref, own2_ref, d_ref, own_ref, q_ref
):
    lx = lx_ref[...]
    lane = lax.broadcasted_iota(jnp.int32, (MX, 128), 1)
    left = lane < 64
    for cr in range(OWN):
        rhs = jnp.concatenate(
            [m_ref[pl.ds(cr, SLABS, stride=8), :], m_ref[pl.ds(4 + cr, SLABS, stride=8), :]], axis=0
        )
        hi, lo = split(rhs)
        res = mm(lx, hi)
        res = res[:64] + res[64:] + mm(lx[:64], lo)
        summed = res[:32] + pltpu.roll(res[32:], 64, 1)
        own_ref[pl.ds(cr, MX, stride=OWN), :] = jnp.where(
            left, summed[:16], pltpu.roll(summed[16:], 64, 1)
        )
    mine = mine_ref[...]
    quarter = [own_ref[c * 16 : (c + 1) * 16, :] for c in range(4)]
    for other, ref in enumerate((own0_ref, own13_ref.at[:16], own2_ref, own13_ref.at[16:])):
        piece = quarter[3 ^ other]
        for c in range(3):
            piece = jnp.where(mine == c, quarter[c ^ other], piece)
        ref[...] = piece
    hi, lo = split(own_ref[...])
    rg = rg_ref[...]
    grep = mm(hi, rg) + mm(lo, rg)
    g_real, g_imag = grep[:, :128], grep[:, 128:]
    acc = jnp.zeros((MX * OWN, 128), F32)
    slot = (lax.broadcasted_iota(jnp.int32, (MX * OWN, 128), 1) // 4) % 8
    red = red_ref[...]
    for t in range(8):
        w_real = wf_ref[:, t * 128 : (t + 1) * 128]
        w_imag = wf_ref[:, 1024 + t * 128 : 1024 + (t + 1) * 128]
        rhi, rlo = split(w_real * g_real + w_imag * g_imag)
        ihi, ilo = split(w_real * g_imag - w_imag * g_real)
        res = mm(jnp.concatenate([rhi, ihi], axis=1), red)
        res += mm(jnp.concatenate([rlo, ilo], axis=1), red)
        acc = jnp.where(slot == t, res, acc)
    q_ref[...] = acc
    ld = ld_ref[...]
    for cr in range(OWN):
        q = q_ref[pl.ds(cr, MX, stride=OWN), :]
        r = pltpu.roll(q, 64, 1)
        zero = jnp.zeros_like(q)
        rhs = jnp.concatenate(
            [
                jnp.where(left, q, zero),
                jnp.where(left, r, zero),
                jnp.where(left, zero, r),
                jnp.where(left, zero, q),
            ],
            axis=0,
        )
        hi, lo = split(rhs)
        d_ref[pl.ds(cr, SLABS, stride=OWN), :] = mm(ld, jnp.concatenate([hi, lo, hi], axis=0))


def middle(mine, moved, weights):
    return pl.pallas_call(
        middle_kernel,
        out_shape=tuple(
            jax.ShapeDtypeStruct((rows, 128), F32) for rows in (16, 32, 16, SLABS * OWN)
        ),
        in_specs=[pl.BlockSpec(memory_space=pltpu.VMEM)] * 7,
        scratch_shapes=[
            pltpu.VMEM((MX * OWN, 128), F32),
            pltpu.VMEM((MX * OWN, 128), F32),
        ],
        compiler_params=pltpu.CompilerParams(vmem_limit_bytes=8 << 20),
        name="middle",
    )(mine, moved, weights, T["fwd_x"], T["rep_g"], T["red"], T["inv_x"])


def weight_grad_kernel(s0_ref, s1_ref, s23_ref, rg_ref, ru_ref, o_ref):
    parts = (s0_ref, s1_ref.at[:16], s23_ref)
    full = jnp.concatenate([part[...] for part in parts], axis=0)
    both = jnp.concatenate(split(full), axis=1)
    rg = rg_ref[...]
    ru = ru_ref[...]
    rg = jnp.concatenate([rg, rg], axis=0)
    ru = jnp.concatenate([ru, ru], axis=0)
    grep = mm(both, rg)
    g_real, g_imag = grep[:, :128], grep[:, 128:]
    slot = (lax.broadcasted_iota(jnp.int32, (64, 256), 1) // 4) % 8
    for t in range(8):
        urep = mm(jnp.where(slot == t, both, jnp.zeros_like(both)), ru)
        u_real, u_imag = urep[:, :128], urep[:, 128:]
        real = g_real * u_real + g_imag * u_imag
        imag = g_imag * u_real - g_real * u_imag
        real = real[:16] + real[16:32] + real[32:48] + real[48:]
        imag = imag[:16] + imag[16:32] + imag[32:48] + imag[48:]
        for a in range(4):
            o_ref[a, :, t * 128 : (t + 1) * 128] = real[a * 4 : (a + 1) * 4]
            o_ref[a, :, 1024 + t * 128 : 1024 + (t + 1) * 128] = imag[a * 4 : (a + 1) * 4]


def weight_grad(parts):
    return pl.pallas_call(
        weight_grad_kernel,
        out_shape=jax.ShapeDtypeStruct((4, OWN, 2 * C * C), F32),
        compiler_params=pltpu.CompilerParams(vmem_limit_bytes=4 << 20),
        name="weight_grad",
    )(*parts, T["rep_g"], T["rep_u"])


def inverse_kernel(
    d_ref, tz_ref, ly_ref, o_hbm, o_ref, f_ref, osems
):
    full = d_ref[...].astype(BF16)
    packed = []
    for odd in range(2):
        blocks = []
        for b in range(MY):
            at = ((b // 2 * 2 + odd) ^ BACK // 4) * MZ
            blocks.append(full[at : at + MZ])
        flat = jnp.concatenate(blocks, axis=0).T
        real = jnp.concatenate([flat[0:32], flat[64:96]], axis=0)
        imag = jnp.concatenate([flat[32:64], flat[96:128]], axis=0)
        for half in (slice(0, 128), slice(128, 256)):
            packed.append(jnp.concatenate([real[:, half], imag[:, half]], axis=1))
    tz = tz_ref[...]
    group = lax.broadcasted_iota(jnp.int32, (64, 256), 1) % 128 // (2 * MZ)
    for first in range(0, MY, ZB):
        rows = []
        for b in range(first, first + ZB):
            part = packed[b % 2 * 2 + b // 8]
            rows.append(jnp.where(group == b % 8 // 2, part, jnp.zeros_like(part)))
        res = mm(jnp.concatenate(rows, axis=0), tz)
        for b in range(first, first + ZB):
            h = res[(b - first) * 64 : (b - first + 1) * 64]
            for xx in range(PLANES):
                at = xx * C * IPAD + b
                f_ref[pl.ds(at, C, stride=IPAD), :] = h[xx * 32 : xx * 32 + 32, :128]
                f_ref[pl.ds(at + 16, C, stride=IPAD), :] = h[xx * 32 : xx * 32 + 32, 128:]

    def send(step):
        at = pl.ds(step * OSTEP, OSTEP)
        return pltpu.make_async_copy(o_ref.at[at], o_hbm.at[at], osems.at[step])

    ly = ly_ref[...]
    for step in range(IMGS // OSTEP):
        for k in range(step * OSTEP, (step + 1) * OSTEP, 2):
            at = k * IPAD
            block = f_ref[pl.ds(at, 72), :]
            pair = jnp.concatenate([block[:32], block[36:68]], axis=1)
            hi, lo = split(pair)
            res = mm(ly, jnp.concatenate([hi, lo, hi], axis=0)).astype(BF16)
            o_ref[k] = res[:, :128]
            o_ref[k + 1] = res[:, 128:]
        send(step).start()
    for step in range(IMGS // OSTEP):
        send(step).wait()


def inverse(spread):
    return pl.pallas_call(
        inverse_kernel,
        out_shape=jax.ShapeDtypeStruct((IMGS, NY, NZ), BF16),
        in_specs=[pl.BlockSpec(memory_space=pltpu.VMEM)] * 3,
        out_specs=HBM,
        scratch_shapes=[
            pltpu.VMEM((IMGS, NY, NZ), BF16),
            pltpu.VMEM((IMGS * IPAD, 128), F32),
            pltpu.SemaphoreType.DMA((IMGS // OSTEP,)),
        ],
        compiler_params=pltpu.CompilerParams(vmem_limit_bytes=8 << 20),
        name="inv_local",
    )(spread, T["inv_z"], T["inv_y"])


def body(u_field, preact, cotangent, weights):
    shape = (IMGS, NY, NZ)
    partial = forward(u_field.reshape(shape), preact.reshape(shape), cotangent.reshape(shape))
    partial, weights = lax.optimization_barrier((partial, weights))
    mine = jnp.full((16, 128), lax.axis_index("dp"), jnp.int32)
    moved = lax.all_to_all(partial, "slab", split_axis=0, concat_axis=0, axis_index_groups=ORDER, tiled=True)
    wide = widen(weights)
    own, to_core, to_far, back = middle(mine, moved.reshape(SLABS * 8, 128), wide)
    near = lax.ppermute(to_core, "dp", [(n, n ^ 1) for n in range(4)])
    far = lax.ppermute(
        jnp.concatenate([to_far, near[16:]], axis=0), "dp", [(n, n ^ 2) for n in range(4)]
    )
    spread = lax.all_to_all(back, "slab", split_axis=0, concat_axis=0, axis_index_groups=BACK_ORDER, tiled=True)
    field_grad = inverse(spread)
    far, field_grad = lax.optimization_barrier((far, field_grad))
    grad_weights = weight_grad((own, near, far))
    return grad_weights, field_grad.reshape(1, PLANES, C, NY, NZ)


def solution(mesh):
    placed = (
        P("dp", "slab", None, None, None),
        P("dp", "slab", None, None, None),
        P("dp", "slab", None, None, None),
        P(None, "slab", None),
    )
    return jax.shard_map(
        body,
        mesh=mesh,
        in_specs=placed,
        out_specs=(P("dp", "slab", None), P("dp", "slab", None, None, None)),
        check_vma=False,
    )
```

```python
import itertools
import math

import jax
import jax.numpy as jnp
import numpy as np
from jax import lax
from jax.experimental import pallas as pl
from jax.experimental.pallas import tpu as pltpu
from jax.sharding import PartitionSpec as P

C = 32
NX = 128
NY = 128
NZ = 128
MX = 16
MY = 16
MZ = 16
SLABS = 64
PLANES = NX // SLABS
IMGS = PLANES * C
OWN = MY * MZ // SLABS
F32 = jnp.float32
BF16 = jnp.bfloat16
AHEAD = 2
TURN = 52
BACK = 52
ORDER = [[n ^ TURN for n in range(SLABS)]]
BACK_ORDER = [[n ^ BACK for n in range(SLABS)]]
CUTS = (0, 16, 40, 64)
OSTEP = 8
ZB = 2
PAD = 132
IPAD = 36


def np_twiddles(length, freqs):
    product = (np.arange(length, dtype=np.int64)[:, None] * freqs[None, :]) % length
    angle = product.astype(np.float32) * np.float32(2.0 * math.pi / length)
    return np.cos(angle).astype(np.float32), np.sin(angle).astype(np.float32)


def signed(count):
    index = np.arange(count)
    return np.where(index < count // 2, index, index - count)


def split_np(table):
    high = table.astype(jnp.bfloat16)
    low = (table - high.astype(np.float32)).astype(jnp.bfloat16)
    return high, low


def make_tables():
    cx, sx = np_twiddles(NX, signed(MX))
    cy, sy = np_twiddles(NY, signed(MY))
    cz, sz = np_twiddles(NZ, np.arange(MZ))
    t = {}
    rows = np.concatenate([cy.T, sy.T], 0)
    t["fwd_y"] = np.concatenate(split_np(rows), 1)
    low_c = cz.astype(jnp.bfloat16).astype(np.float32)
    low_s = (-sz).astype(jnp.bfloat16).astype(np.float32)
    real = np.concatenate([low_c, low_s], 0).T
    imag = np.concatenate([low_s, -low_c], 0).T
    wz = np.stack([real.reshape(4, 4, 2 * NZ), imag.reshape(4, 4, 2 * NZ)], 1)
    t["fwd_z"] = wz.reshape(2 * MZ, 2 * NZ).astype(jnp.bfloat16)
    mode_scale = np.where(np.arange(MZ) == 0, 0.5, 1.0) / (NX * NY * NZ)
    per_row = np.broadcast_to(mode_scale.reshape(4, 1, 4), (4, 2, 4)).reshape(2 * MZ, 1)
    is_g = (np.arange(128) // C) % 2 == 1
    t["scale"] = np.where(is_g[None, :], per_row, 1.0).astype(np.float32)
    cxs, sxs = cx.reshape(SLABS, PLANES, MX)[ORDER[0]], sx.reshape(SLABS, PLANES, MX)[ORDER[0]]
    lx = np.zeros((PLANES, 2, MX, 2, SLABS), np.float32)
    for xx in range(PLANES):
        lx[xx, 0, :, 0] = cxs[:, xx].T
        lx[xx, 0, :, 1] = sxs[:, xx].T
        lx[xx, 1, :, 0] = -sxs[:, xx].T
        lx[xx, 1, :, 1] = cxs[:, xx].T
    t["fwd_x"] = np.concatenate(split_np(lx.reshape(PLANES * 2 * MX, 2 * SLABS)), 0)
    rep = np.zeros((128, 2, 4, C), np.float32)
    for part in range(2):
        for ch in range(C):
            rep[part * 64 + 32 + ch, part, :, ch] = 1.0
    t["rep_g"] = rep.reshape(128, 256).astype(jnp.bfloat16)
    rep = np.zeros((2, 2, 8, 4, 2, 4, C), np.float32)
    for part in range(2):
        for r in range(4):
            rep[part, 0, :, r, part, r, :] = 1.0
    t["rep_u"] = rep.reshape(128, 256).astype(jnp.bfloat16)
    red = np.zeros((2, 4, C, 4, 8, 4), np.float32)
    for r in range(4):
        red[0, r, :, 0, :, r] = 1.0
        red[1, r, :, 1, :, r] = 1.0
        red[1, r, :, 2, :, r] = -1.0
        red[0, r, :, 3, :, r] = 1.0
    t["red"] = red.reshape(256, 128).astype(jnp.bfloat16)
    cxb, sxb = cx.reshape(SLABS, PLANES, MX)[BACK_ORDER[0]], sx.reshape(SLABS, PLANES, MX)[BACK_ORDER[0]]
    ld = np.stack([cxb, sxb], 2).reshape(SLABS, PLANES * 2 * MX)
    high, low = split_np(ld)
    t["inv_x"] = np.concatenate([high, high, low], 1)
    czb, szb = ((v.T.reshape(4, 4, NZ)[np.arange(4) ^ BACK % 4]).reshape(MZ, NZ) for v in (cz, sz))
    tz = np.stack([np.concatenate([czb, szb], 1), np.concatenate([-szb, czb], 1)])
    tz = np.broadcast_to(tz[:, None], (2, 8, MZ, 2 * NZ)).reshape(256, 2 * NZ)
    high, low = split_np(tz)
    odd = (np.arange(256) // MZ % 2 == 1)[:, None]
    t["inv_z"] = np.where(odd, low, high)
    ly = np.concatenate([cy, -sy], 1)
    high, low = split_np(ly)
    t["inv_y"] = np.concatenate([high, high, low], 1)
    return t


T = make_tables()


def split(value):
    high = value.astype(BF16)
    return high, (value - high.astype(F32)).astype(BF16)


def mm(a, b):
    return jnp.dot(a, b, preferred_element_type=F32)


def mm_nt(a, b):
    return lax.dot_general(a, b, (((1,), (1,)), ((), ())), preferred_element_type=F32)


HBM = pl.BlockSpec(memory_space=pltpu.HBM)


def forward_kernel(
    u_hbm, p_hbm, c_hbm, ty_hbm, wz_hbm, sc_hbm, o_hbm, o_ref, u_ref, p_ref, c_ref, ty_ref, wz_ref, sc_ref, xc_ref, xs_ref, sems, tsems, osems
):
    def chunk(src, dst, row, step):
        at = pl.ds(CUTS[step], CUTS[step + 1] - CUTS[step])
        return pltpu.make_async_copy(src.at[at], dst.at[at], sems.at[row, step])

    table = pltpu.make_async_copy(ty_hbm, ty_ref, tsems.at[0])
    late = [
        pltpu.make_async_copy(wz_hbm, wz_ref, tsems.at[1]),
        pltpu.make_async_copy(sc_hbm, sc_ref, tsems.at[2]),
    ]
    def fetch(step):
        chunk(p_hbm, p_ref, 1, step).start()
        chunk(c_hbm, c_ref, 2, step).start()
        chunk(u_hbm, u_ref, 0, step).start()

    fetch(0)
    table.start()
    for step in range(1, AHEAD):
        fetch(step)
    for one in late:
        one.start()
    table.wait()

    def arrived(step):
        for row, (src, dst) in enumerate(((u_hbm, u_ref), (p_hbm, p_ref), (c_hbm, c_ref))):
            chunk(src, dst, row, step).wait()

    def slope_of(k):
        if True:
            arg = p_ref[k].astype(F32) * math.sqrt(0.5)
            bell = jnp.exp2((arg * (-math.log2(math.e))) * arg) * (2.0 / math.sqrt(math.pi))
            slope = (lax.erf(arg) + 1.0) + arg * bell
            c_ref[k] = (c_ref[k].astype(F32) * slope).astype(BF16)

    ty = ty_ref[...]

    def image(k):
        if True:
            both = jnp.concatenate([u_ref[k], c_ref[k]], axis=1)
            part = mm(ty, jnp.concatenate([both, both], axis=0))
            base = (k // C) * 64 + k % C
            xc_ref[pl.ds(base, MY, stride=PAD), :] = part[:16, :128]
            xs_ref[pl.ds(base, MY, stride=PAD), :] = part[16:, :128]
            xc_ref[pl.ds(base + 32, MY, stride=PAD), :] = part[:16, 128:]
            xs_ref[pl.ds(base + 32, MY, stride=PAD), :] = part[16:, 128:]

    for step in range(len(CUTS)):
        if step < len(CUTS) - 1:
            arrived(step)
            if step + AHEAD < len(CUTS) - 1:
                fetch(step + AHEAD)
        if step < len(CUTS) - 1:
            for k in range(CUTS[step], CUTS[step + 1]):
                slope_of(k)
                if k >= 2:
                    image(k - 2)
        else:
            image(62)
            image(63)
    for one in late:
        one.wait()
    wz = wz_ref[...]
    scale = sc_ref[...]

    def send(part):
        at = pl.ds(part * 16, 16)
        return pltpu.make_async_copy(o_ref.at[at], o_hbm.at[at], osems.at[part])

    for b in range(MY):
        rows = slice(b * PAD, b * PAD + 128)
        both = jnp.concatenate([xc_ref[rows, :].astype(BF16), xs_ref[rows, :].astype(BF16)], axis=1)
        res = mm_nt(wz, both)
        res = res * scale
        for q in range(4):
            o_ref[(b * 4 + q) ^ TURN] = res[q * 8 : (q + 1) * 8]
        if b % 4 == 3:
            send(b // 4 ^ TURN // 16).start()
    for part in range(4):
        send(part).wait()


def forward(u, pre, cot):
    big = pltpu.VMEM((IMGS, NY, NZ), BF16)
    flat = pltpu.VMEM((MY * PAD, 128), F32)
    return pl.pallas_call(
        forward_kernel,
        out_shape=jax.ShapeDtypeStruct((SLABS, 8, 128), F32),
        in_specs=[HBM] * 6,
        out_specs=HBM,
        scratch_shapes=[
            pltpu.VMEM((SLABS, 8, 128), F32),
            big,
            big,
            big,
            pltpu.VMEM((32, 256), BF16),
            pltpu.VMEM((32, 256), BF16),
            pltpu.VMEM((32, 128), F32),
            flat,
            flat,
            pltpu.SemaphoreType.DMA((3, (len(CUTS) - 1))),
            pltpu.SemaphoreType.DMA((3,)),
            pltpu.SemaphoreType.DMA((4,)),
        ],
        name="fwd_local",
    )(u, pre, cot, T["fwd_y"], T["fwd_z"], T["scale"])


def widen_kernel(w_ref, o_ref):
    for a in range(MX):
        o_ref[pl.ds(4 * a, 4), :] = w_ref[a].astype(F32)


def widen(weights):
    return pl.pallas_call(
        widen_kernel,
        out_shape=jax.ShapeDtypeStruct((MX * OWN, 2 * C * C), F32),
        in_specs=[pl.BlockSpec(memory_space=pltpu.VMEM)],
        out_specs=pl.BlockSpec(memory_space=pltpu.VMEM),
        compiler_params=pltpu.CompilerParams(vmem_limit_bytes=4 << 20),
        name="widen",
    )(weights)


def middle_kernel(
    mine_ref, m_ref, wf_ref, lx_ref, rg_ref, red_ref, ld_ref, own0_ref, own23_ref, own1_ref, d_ref, own_ref, q_ref
):
    lx = lx_ref[...]
    lane = lax.broadcasted_iota(jnp.int32, (MX, 128), 1)
    left = lane < 64
    for cr in range(OWN):
        rhs = jnp.concatenate(
            [m_ref[pl.ds(cr, SLABS, stride=8), :], m_ref[pl.ds(4 + cr, SLABS, stride=8), :]], axis=0
        )
        hi, lo = split(rhs)
        res = mm(lx, hi)
        res = res[:64] + res[64:] + mm(lx[:64], lo)
        summed = res[:32] + pltpu.roll(res[32:], 64, 1)
        own_ref[pl.ds(cr, MX, stride=OWN), :] = jnp.where(
            left, summed[:16], pltpu.roll(summed[16:], 64, 1)
        )
    mine = mine_ref[...]
    quarter = [own_ref[c * 16 : (c + 1) * 16, :] for c in range(4)]
    for other, ref in enumerate((own0_ref, own1_ref, own23_ref.at[:16], own23_ref.at[16:])):
        piece = quarter[3 ^ other]
        for c in range(3):
            piece = jnp.where(mine == c, quarter[c ^ other], piece)
        ref[...] = piece
    hi, lo = split(own_ref[...])
    rg = rg_ref[...]
    grep = mm(hi, rg) + mm(lo, rg)
    g_real, g_imag = grep[:, :128], grep[:, 128:]
    acc = jnp.zeros((MX * OWN, 128), F32)
    slot = (lax.broadcasted_iota(jnp.int32, (MX * OWN, 128), 1) // 4) % 8
    red = red_ref[...]
    for t in range(8):
        w_real = wf_ref[:, t * 128 : (t + 1) * 128]
        w_imag = wf_ref[:, 1024 + t * 128 : 1024 + (t + 1) * 128]
        rhi, rlo = split(w_real * g_real + w_imag * g_imag)
        ihi, ilo = split(w_real * g_imag - w_imag * g_real)
        res = mm(jnp.concatenate([rhi, ihi], axis=1), red)
        res += mm(jnp.concatenate([rlo, ilo], axis=1), red)
        acc = jnp.where(slot == t, res, acc)
    q_ref[...] = acc
    ld = ld_ref[...]
    for cr in range(OWN):
        q = q_ref[pl.ds(cr, MX, stride=OWN), :]
        r = pltpu.roll(q, 64, 1)
        zero = jnp.zeros_like(q)
        rhs = jnp.concatenate(
            [
                jnp.where(left, q, zero),
                jnp.where(left, r, zero),
                jnp.where(left, zero, r),
                jnp.where(left, zero, q),
            ],
            axis=0,
        )
        hi, lo = split(rhs)
        d_ref[pl.ds(cr, SLABS, stride=OWN), :] = mm(ld, jnp.concatenate([hi, lo, hi], axis=0))


def middle(mine, moved, weights):
    return pl.pallas_call(
        middle_kernel,
        out_shape=tuple(
            jax.ShapeDtypeStruct((rows, 128), F32) for rows in (16, 32, 16, SLABS * OWN)
        ),
        in_specs=[pl.BlockSpec(memory_space=pltpu.VMEM)] * 7,
        scratch_shapes=[
            pltpu.VMEM((MX * OWN, 128), F32),
            pltpu.VMEM((MX * OWN, 128), F32),
        ],
        compiler_params=pltpu.CompilerParams(vmem_limit_bytes=8 << 20),
        name="middle",
    )(mine, moved, weights, T["fwd_x"], T["rep_g"], T["red"], T["inv_x"])


def weight_grad_kernel(s0_ref, s1_ref, s23_ref, rg_ref, ru_ref, o_ref):
    parts = (s0_ref, s1_ref.at[:16], s23_ref)
    full = jnp.concatenate([part[...] for part in parts], axis=0)
    both = jnp.concatenate(split(full), axis=1)
    rg = rg_ref[...]
    ru = ru_ref[...]
    rg = jnp.concatenate([rg, rg], axis=0)
    ru = jnp.concatenate([ru, ru], axis=0)
    grep = mm(both, rg)
    g_real, g_imag = grep[:, :128], grep[:, 128:]
    slot = (lax.broadcasted_iota(jnp.int32, (64, 256), 1) // 4) % 8
    for t in range(8):
        urep = mm(jnp.where(slot == t, both, jnp.zeros_like(both)), ru)
        u_real, u_imag = urep[:, :128], urep[:, 128:]
        real = g_real * u_real + g_imag * u_imag
        imag = g_imag * u_real - g_real * u_imag
        real = real[:16] + real[16:32] + real[32:48] + real[48:]
        imag = imag[:16] + imag[16:32] + imag[32:48] + imag[48:]
        for a in range(4):
            o_ref[a, :, t * 128 : (t + 1) * 128] = real[a * 4 : (a + 1) * 4]
            o_ref[a, :, 1024 + t * 128 : 1024 + (t + 1) * 128] = imag[a * 4 : (a + 1) * 4]


def weight_grad(parts):
    return pl.pallas_call(
        weight_grad_kernel,
        out_shape=jax.ShapeDtypeStruct((4, OWN, 2 * C * C), F32),
        compiler_params=pltpu.CompilerParams(vmem_limit_bytes=4 << 20),
        name="weight_grad",
    )(*parts, T["rep_g"], T["rep_u"])


def inverse_kernel(
    d_ref, tz_ref, ly_ref, o_hbm, o_ref, f_ref, osems
):
    full = d_ref[...].astype(BF16)
    packed = []
    for odd in range(2):
        blocks = []
        for b in range(MY):
            at = ((b // 2 * 2 + odd) ^ BACK // 4) * MZ
            blocks.append(full[at : at + MZ])
        flat = jnp.concatenate(blocks, axis=0).T
        real = jnp.concatenate([flat[0:32], flat[64:96]], axis=0)
        imag = jnp.concatenate([flat[32:64], flat[96:128]], axis=0)
        for half in (slice(0, 128), slice(128, 256)):
            packed.append(jnp.concatenate([real[:, half], imag[:, half]], axis=1))
    tz = tz_ref[...]
    group = lax.broadcasted_iota(jnp.int32, (64, 256), 1) % 128 // (2 * MZ)
    for first in range(0, MY, ZB):
        rows = []
        for b in range(first, first + ZB):
            part = packed[b % 2 * 2 + b // 8]
            rows.append(jnp.where(group == b % 8 // 2, part, jnp.zeros_like(part)))
        res = mm(jnp.concatenate(rows, axis=0), tz)
        for b in range(first, first + ZB):
            h = res[(b - first) * 64 : (b - first + 1) * 64]
            for xx in range(PLANES):
                at = xx * C * IPAD + b
                f_ref[pl.ds(at, C, stride=IPAD), :] = h[xx * 32 : xx * 32 + 32, :128]
                f_ref[pl.ds(at + 16, C, stride=IPAD), :] = h[xx * 32 : xx * 32 + 32, 128:]

    def send(step):
        at = pl.ds(step * OSTEP, OSTEP)
        return pltpu.make_async_copy(o_ref.at[at], o_hbm.at[at], osems.at[step])

    ly = ly_ref[...]
    for step in range(IMGS // OSTEP):
        for k in range(step * OSTEP, (step + 1) * OSTEP, 2):
            at = k * IPAD
            block = f_ref[pl.ds(at, 72), :]
            pair = jnp.concatenate([block[:32], block[36:68]], axis=1)
            hi, lo = split(pair)
            res = mm(ly, jnp.concatenate([hi, lo, hi], axis=0)).astype(BF16)
            o_ref[k] = res[:, :128]
            o_ref[k + 1] = res[:, 128:]
        send(step).start()
    for step in range(IMGS // OSTEP):
        send(step).wait()


def inverse(spread):
    return pl.pallas_call(
        inverse_kernel,
        out_shape=jax.ShapeDtypeStruct((IMGS, NY, NZ), BF16),
        in_specs=[pl.BlockSpec(memory_space=pltpu.VMEM)] * 3,
        out_specs=HBM,
        scratch_shapes=[
            pltpu.VMEM((IMGS, NY, NZ), BF16),
            pltpu.VMEM((IMGS * IPAD, 128), F32),
            pltpu.SemaphoreType.DMA((IMGS // OSTEP,)),
        ],
        compiler_params=pltpu.CompilerParams(vmem_limit_bytes=8 << 20),
        name="inv_local",
    )(spread, T["inv_z"], T["inv_y"])


def body(u_field, preact, cotangent, weights):
    shape = (IMGS, NY, NZ)
    partial = forward(u_field.reshape(shape), preact.reshape(shape), cotangent.reshape(shape))
    partial, weights = lax.optimization_barrier((partial, weights))
    mine = jnp.full((16, 128), lax.axis_index("dp"), jnp.int32)
    moved = lax.all_to_all(partial, "slab", split_axis=0, concat_axis=0, axis_index_groups=ORDER, tiled=True)
    wide = widen(weights)
    own, to_far, to_core, back = middle(mine, moved.reshape(SLABS * 8, 128), wide)
    far = lax.ppermute(to_far, "dp", [(n, n ^ 2) for n in range(4)])
    spread = lax.all_to_all(back, "slab", split_axis=0, concat_axis=0, axis_index_groups=BACK_ORDER, tiled=True)
    field_grad = inverse(spread)
    far, field_grad = lax.optimization_barrier((far, field_grad))
    near = lax.ppermute(
        jnp.concatenate([to_core, far[16:]], axis=0), "dp", [(n, n ^ 1) for n in range(4)]
    )
    grad_weights = weight_grad((own, far, near))
    return grad_weights, field_grad.reshape(1, PLANES, C, NY, NZ)


def solution(mesh):
    placed = (
        P("dp", "slab", None, None, None),
        P("dp", "slab", None, None, None),
        P("dp", "slab", None, None, None),
        P(None, "slab", None),
    )
    return jax.shard_map(
        body,
        mesh=mesh,
        in_specs=placed,
        out_specs=(P("dp", "slab", None), P("dp", "slab", None, None, None)),
        check_vma=False,
    )
```

```python
import itertools
import math

import jax
import jax.numpy as jnp
import numpy as np
from jax import lax
from jax.experimental import pallas as pl
from jax.experimental.pallas import tpu as pltpu
from jax.sharding import PartitionSpec as P

C = 32
NX = 128
NY = 128
NZ = 128
MX = 16
MY = 16
MZ = 16
SLABS = 64
PLANES = NX // SLABS
IMGS = PLANES * C
OWN = MY * MZ // SLABS
F32 = jnp.float32
BF16 = jnp.bfloat16
AHEAD = 2
OTHERS = (0, 2, 3, 1)
TURN = 52
BACK = 53
ORDER = [[n ^ TURN for n in range(SLABS)]]
BACK_ORDER = [[n ^ BACK for n in range(SLABS)]]
CUTS = (0, 16, 40, 64)
OSTEP = 8
ZB = 2
PAD = 132
IPAD = 36


def np_twiddles(length, freqs):
    product = (np.arange(length, dtype=np.int64)[:, None] * freqs[None, :]) % length
    angle = product.astype(np.float32) * np.float32(2.0 * math.pi / length)
    return np.cos(angle).astype(np.float32), np.sin(angle).astype(np.float32)


def signed(count):
    index = np.arange(count)
    return np.where(index < count // 2, index, index - count)


def split_np(table):
    high = table.astype(jnp.bfloat16)
    low = (table - high.astype(np.float32)).astype(jnp.bfloat16)
    return high, low


def make_tables():
    cx, sx = np_twiddles(NX, signed(MX))
    cy, sy = np_twiddles(NY, signed(MY))
    cz, sz = np_twiddles(NZ, np.arange(MZ))
    t = {}
    rows = np.concatenate([cy.T, sy.T], 0)
    t["fwd_y"] = np.concatenate(split_np(rows), 1)
    low_c = cz.astype(jnp.bfloat16).astype(np.float32)
    low_s = (-sz).astype(jnp.bfloat16).astype(np.float32)
    real = np.concatenate([low_c, low_s], 0).T
    imag = np.concatenate([low_s, -low_c], 0).T
    wz = np.stack([real.reshape(4, 4, 2 * NZ), imag.reshape(4, 4, 2 * NZ)], 1)
    t["fwd_z"] = wz.reshape(2 * MZ, 2 * NZ).astype(jnp.bfloat16)
    mode_scale = np.where(np.arange(MZ) == 0, 0.5, 1.0) / (NX * NY * NZ)
    per_row = np.broadcast_to(mode_scale.reshape(4, 1, 4), (4, 2, 4)).reshape(2 * MZ, 1)
    is_g = (np.arange(128) // C) % 2 == 1
    t["scale"] = np.where(is_g[None, :], per_row, 1.0).astype(np.float32)
    cxs, sxs = cx.reshape(SLABS, PLANES, MX)[ORDER[0]], sx.reshape(SLABS, PLANES, MX)[ORDER[0]]
    lx = np.zeros((PLANES, 2, MX, 2, SLABS), np.float32)
    for xx in range(PLANES):
        lx[xx, 0, :, 0] = cxs[:, xx].T
        lx[xx, 0, :, 1] = sxs[:, xx].T
        lx[xx, 1, :, 0] = -sxs[:, xx].T
        lx[xx, 1, :, 1] = cxs[:, xx].T
    t["fwd_x"] = np.concatenate(split_np(lx.reshape(PLANES * 2 * MX, 2 * SLABS)), 0)
    rep = np.zeros((128, 2, 4, C), np.float32)
    for part in range(2):
        for ch in range(C):
            rep[part * 64 + 32 + ch, part, :, ch] = 1.0
    t["rep_g"] = rep.reshape(128, 256).astype(jnp.bfloat16)
    rep = np.zeros((2, 2, 8, 4, 2, 4, C), np.float32)
    for part in range(2):
        for r in range(4):
            rep[part, 0, :, r, part, r, :] = 1.0
    t["rep_u"] = rep.reshape(128, 256).astype(jnp.bfloat16)
    red = np.zeros((2, 4, C, 4, 8, 4), np.float32)
    for r in range(4):
        red[0, r, :, 0, :, r] = 1.0
        red[1, r, :, 1, :, r] = 1.0
        red[1, r, :, 2, :, r] = -1.0
        red[0, r, :, 3, :, r] = 1.0
    t["red"] = red.reshape(256, 128).astype(jnp.bfloat16)
    cxb, sxb = cx.reshape(SLABS, PLANES, MX)[BACK_ORDER[0]], sx.reshape(SLABS, PLANES, MX)[BACK_ORDER[0]]
    ld = np.stack([cxb, sxb], 2).reshape(SLABS, PLANES * 2 * MX)
    high, low = split_np(ld)
    t["inv_x"] = np.concatenate([high, high, low], 1)
    czb, szb = ((v.T.reshape(4, 4, NZ)[np.arange(4) ^ BACK % 4]).reshape(MZ, NZ) for v in (cz, sz))
    tz = np.stack([np.concatenate([czb, szb], 1), np.concatenate([-szb, czb], 1)])
    tz = np.broadcast_to(tz[:, None], (2, 8, MZ, 2 * NZ)).reshape(256, 2 * NZ)
    high, low = split_np(tz)
    odd = (np.arange(256) // MZ % 2 == 1)[:, None]
    t["inv_z"] = np.where(odd, low, high)
    ly = np.concatenate([cy, -sy], 1)
    high, low = split_np(ly)
    t["inv_y"] = np.concatenate([high, high, low], 1)
    return t


T = make_tables()


def split(value):
    high = value.astype(BF16)
    return high, (value - high.astype(F32)).astype(BF16)


def mm(a, b):
    return jnp.dot(a, b, preferred_element_type=F32)


def mm_nt(a, b):
    return lax.dot_general(a, b, (((1,), (1,)), ((), ())), preferred_element_type=F32)


HBM = pl.BlockSpec(memory_space=pltpu.HBM)


def forward_kernel(
    u_hbm, p_hbm, c_hbm, ty_hbm, wz_hbm, sc_hbm, o_hbm, o_ref, u_ref, p_ref, c_ref, ty_ref, wz_ref, sc_ref, xc_ref, xs_ref, sems, tsems, osems
):
    def chunk(src, dst, row, step):
        at = pl.ds(CUTS[step], CUTS[step + 1] - CUTS[step])
        return pltpu.make_async_copy(src.at[at], dst.at[at], sems.at[row, step])

    table = pltpu.make_async_copy(ty_hbm, ty_ref, tsems.at[0])
    late = [
        pltpu.make_async_copy(wz_hbm, wz_ref, tsems.at[1]),
        pltpu.make_async_copy(sc_hbm, sc_ref, tsems.at[2]),
    ]
    def fetch(step):
        chunk(p_hbm, p_ref, 1, step).start()
        chunk(c_hbm, c_ref, 2, step).start()
        chunk(u_hbm, u_ref, 0, step).start()

    fetch(0)
    table.start()
    for step in range(1, AHEAD):
        fetch(step)
    for one in late:
        one.start()
    table.wait()

    def arrived(step):
        for row, (src, dst) in enumerate(((u_hbm, u_ref), (p_hbm, p_ref), (c_hbm, c_ref))):
            chunk(src, dst, row, step).wait()

    def slope_of(k):
        if True:
            arg = p_ref[k].astype(F32) * math.sqrt(0.5)
            bell = jnp.exp2((arg * (-math.log2(math.e))) * arg) * (2.0 / math.sqrt(math.pi))
            slope = (lax.erf(arg) + 1.0) + arg * bell
            c_ref[k] = (c_ref[k].astype(F32) * slope).astype(BF16)

    ty = ty_ref[...]

    def image(k):
        if True:
            both = jnp.concatenate([u_ref[k], c_ref[k]], axis=1)
            part = mm(ty, jnp.concatenate([both, both], axis=0))
            base = (k // C) * 64 + k % C
            xc_ref[pl.ds(base, MY, stride=PAD), :] = part[:16, :128]
            xs_ref[pl.ds(base, MY, stride=PAD), :] = part[16:, :128]
            xc_ref[pl.ds(base + 32, MY, stride=PAD), :] = part[:16, 128:]
            xs_ref[pl.ds(base + 32, MY, stride=PAD), :] = part[16:, 128:]

    for step in range(len(CUTS)):
        if step < len(CUTS) - 1:
            arrived(step)
            if step + AHEAD < len(CUTS) - 1:
                fetch(step + AHEAD)
        if step < len(CUTS) - 1:
            for k in range(CUTS[step], CUTS[step + 1]):
                slope_of(k)
                if k >= 2:
                    image(k - 2)
        else:
            image(62)
            image(63)
    for one in late:
        one.wait()
    wz = wz_ref[...]
    scale = sc_ref[...]

    def send(part):
        at = pl.ds(part * 16, 16)
        return pltpu.make_async_copy(o_ref.at[at], o_hbm.at[at], osems.at[part])

    for b in range(MY):
        rows = slice(b * PAD, b * PAD + 128)
        both = jnp.concatenate([xc_ref[rows, :].astype(BF16), xs_ref[rows, :].astype(BF16)], axis=1)
        res = mm_nt(wz, both)
        res = res * scale
        for q in range(4):
            o_ref[(b * 4 + q) ^ TURN] = res[q * 8 : (q + 1) * 8]
        if b % 4 == 3:
            send(b // 4 ^ TURN // 16).start()
    for part in range(4):
        send(part).wait()


def forward(u, pre, cot):
    big = pltpu.VMEM((IMGS, NY, NZ), BF16)
    flat = pltpu.VMEM((MY * PAD, 128), F32)
    return pl.pallas_call(
        forward_kernel,
        out_shape=jax.ShapeDtypeStruct((SLABS, 8, 128), F32),
        in_specs=[HBM] * 6,
        out_specs=HBM,
        scratch_shapes=[
            pltpu.VMEM((SLABS, 8, 128), F32),
            big,
            big,
            big,
            pltpu.VMEM((32, 256), BF16),
            pltpu.VMEM((32, 256), BF16),
            pltpu.VMEM((32, 128), F32),
            flat,
            flat,
            pltpu.SemaphoreType.DMA((3, (len(CUTS) - 1))),
            pltpu.SemaphoreType.DMA((3,)),
            pltpu.SemaphoreType.DMA((4,)),
        ],
        name="fwd_local",
    )(u, pre, cot, T["fwd_y"], T["fwd_z"], T["scale"])


def widen_kernel(w_ref, o_ref):
    for a in range(MX):
        o_ref[pl.ds(4 * a, 4), :] = w_ref[a].astype(F32)


def widen(weights):
    return pl.pallas_call(
        widen_kernel,
        out_shape=jax.ShapeDtypeStruct((MX * OWN, 2 * C * C), F32),
        in_specs=[pl.BlockSpec(memory_space=pltpu.VMEM)],
        out_specs=pl.BlockSpec(memory_space=pltpu.VMEM),
        compiler_params=pltpu.CompilerParams(vmem_limit_bytes=4 << 20),
        name="widen",
    )(weights)


def middle_kernel(
    mine_ref, m_ref, wf_ref, lx_ref, rg_ref, red_ref, ld_ref, own0_ref, own1_ref, own2_ref, own3_ref, d_ref, own_ref, q_ref
):
    lx = lx_ref[...]
    lane = lax.broadcasted_iota(jnp.int32, (MX, 128), 1)
    left = lane < 64
    for cr in range(OWN):
        rhs = jnp.concatenate(
            [m_ref[pl.ds(cr, SLABS, stride=8), :], m_ref[pl.ds(4 + cr, SLABS, stride=8), :]], axis=0
        )
        hi, lo = split(rhs)
        res = mm(lx, hi)
        res = res[:64] + res[64:] + mm(lx[:64], lo)
        summed = res[:32] + pltpu.roll(res[32:], 64, 1)
        own_ref[pl.ds(cr, MX, stride=OWN), :] = jnp.where(
            left, summed[:16], pltpu.roll(summed[16:], 64, 1)
        )
    mine = mine_ref[...]
    quarter = [own_ref[c * 16 : (c + 1) * 16, :] for c in range(4)]
    for other, ref in zip(OTHERS, (own0_ref, own1_ref, own2_ref, own3_ref)):
        piece = quarter[3 ^ other]
        for c in range(3):
            piece = jnp.where(mine == c, quarter[c ^ other], piece)
        ref[...] = piece
    hi, lo = split(own_ref[...])
    rg = rg_ref[...]
    grep = mm(hi, rg) + mm(lo, rg)
    g_real, g_imag = grep[:, :128], grep[:, 128:]
    acc = jnp.zeros((MX * OWN, 128), F32)
    slot = (lax.broadcasted_iota(jnp.int32, (MX * OWN, 128), 1) // 4) % 8
    red = red_ref[...]
    for t in range(8):
        w_real = wf_ref[:, t * 128 : (t + 1) * 128]
        w_imag = wf_ref[:, 1024 + t * 128 : 1024 + (t + 1) * 128]
        rhi, rlo = split(w_real * g_real + w_imag * g_imag)
        ihi, ilo = split(w_real * g_imag - w_imag * g_real)
        res = mm(jnp.concatenate([rhi, ihi], axis=1), red)
        res += mm(jnp.concatenate([rlo, ilo], axis=1), red)
        acc = jnp.where(slot == t, res, acc)
    q_ref[...] = acc
    ld = ld_ref[...]
    for cr in range(OWN):
        q = q_ref[pl.ds(cr, MX, stride=OWN), :]
        r = pltpu.roll(q, 64, 1)
        zero = jnp.zeros_like(q)
        rhs = jnp.concatenate(
            [
                jnp.where(left, q, zero),
                jnp.where(left, r, zero),
                jnp.where(left, zero, r),
                jnp.where(left, zero, q),
            ],
            axis=0,
        )
        hi, lo = split(rhs)
        d_ref[pl.ds(cr, SLABS, stride=OWN), :] = mm(ld, jnp.concatenate([hi, lo, hi], axis=0))


def middle(mine, moved, weights):
    return pl.pallas_call(
        middle_kernel,
        out_shape=(jax.ShapeDtypeStruct((16, 128), F32),) * 4
        + (jax.ShapeDtypeStruct((SLABS * OWN, 128), F32),),
        in_specs=[pl.BlockSpec(memory_space=pltpu.VMEM)] * 7,
        scratch_shapes=[
            pltpu.VMEM((MX * OWN, 128), F32),
            pltpu.VMEM((MX * OWN, 128), F32),
        ],
        compiler_params=pltpu.CompilerParams(vmem_limit_bytes=8 << 20),
        name="middle",
    )(mine, moved, weights, T["fwd_x"], T["rep_g"], T["red"], T["inv_x"])


def weight_grad_kernel(s0_ref, s1_ref, s2_ref, s3_ref, rg_ref, ru_ref, o_ref):
    parts = (s0_ref, s1_ref, s2_ref, s3_ref)
    full = jnp.concatenate([part[...] for part in parts], axis=0)
    both = jnp.concatenate(split(full), axis=1)
    rg = rg_ref[...]
    ru = ru_ref[...]
    rg = jnp.concatenate([rg, rg], axis=0)
    ru = jnp.concatenate([ru, ru], axis=0)
    grep = mm(both, rg)
    g_real, g_imag = grep[:, :128], grep[:, 128:]
    slot = (lax.broadcasted_iota(jnp.int32, (64, 256), 1) // 4) % 8
    for t in range(8):
        urep = mm(jnp.where(slot == t, both, jnp.zeros_like(both)), ru)
        u_real, u_imag = urep[:, :128], urep[:, 128:]
        real = g_real * u_real + g_imag * u_imag
        imag = g_imag * u_real - g_real * u_imag
        real = real[:16] + real[16:32] + real[32:48] + real[48:]
        imag = imag[:16] + imag[16:32] + imag[32:48] + imag[48:]
        for a in range(4):
            o_ref[a, :, t * 128 : (t + 1) * 128] = real[a * 4 : (a + 1) * 4]
            o_ref[a, :, 1024 + t * 128 : 1024 + (t + 1) * 128] = imag[a * 4 : (a + 1) * 4]


def weight_grad(parts):
    return pl.pallas_call(
        weight_grad_kernel,
        out_shape=jax.ShapeDtypeStruct((4, OWN, 2 * C * C), F32),
        compiler_params=pltpu.CompilerParams(vmem_limit_bytes=4 << 20),
        name="weight_grad",
    )(*parts, T["rep_g"], T["rep_u"])


def inverse_kernel(
    d_ref, tz_ref, ly_ref, o_hbm, o_ref, f_ref, osems
):
    full = d_ref[...].astype(BF16)
    packed = []
    for odd in range(2):
        blocks = []
        for b in range(MY):
            at = ((b // 2 * 2 + odd) ^ BACK // 4) * MZ
            blocks.append(full[at : at + MZ])
        flat = jnp.concatenate(blocks, axis=0).T
        real = jnp.concatenate([flat[0:32], flat[64:96]], axis=0)
        imag = jnp.concatenate([flat[32:64], flat[96:128]], axis=0)
        for half in (slice(0, 128), slice(128, 256)):
            packed.append(jnp.concatenate([real[:, half], imag[:, half]], axis=1))
    tz = tz_ref[...]
    group = lax.broadcasted_iota(jnp.int32, (64, 256), 1) % 128 // (2 * MZ)
    for first in range(0, MY, ZB):
        rows = []
        for b in range(first, first + ZB):
            part = packed[b % 2 * 2 + b // 8]
            rows.append(jnp.where(group == b % 8 // 2, part, jnp.zeros_like(part)))
        res = mm(jnp.concatenate(rows, axis=0), tz)
        for b in range(first, first + ZB):
            h = res[(b - first) * 64 : (b - first + 1) * 64]
            for xx in range(PLANES):
                at = xx * C * IPAD + b
                f_ref[pl.ds(at, C, stride=IPAD), :] = h[xx * 32 : xx * 32 + 32, :128]
                f_ref[pl.ds(at + 16, C, stride=IPAD), :] = h[xx * 32 : xx * 32 + 32, 128:]

    def send(step):
        at = pl.ds(step * OSTEP, OSTEP)
        return pltpu.make_async_copy(o_ref.at[at], o_hbm.at[at], osems.at[step])

    ly = ly_ref[...]
    for step in range(IMGS // OSTEP):
        for k in range(step * OSTEP, (step + 1) * OSTEP, 2):
            at = k * IPAD
            block = f_ref[pl.ds(at, 72), :]
            pair = jnp.concatenate([block[:32], block[36:68]], axis=1)
            hi, lo = split(pair)
            res = mm(ly, jnp.concatenate([hi, lo, hi], axis=0)).astype(BF16)
            o_ref[k] = res[:, :128]
            o_ref[k + 1] = res[:, 128:]
        send(step).start()
    for step in range(IMGS // OSTEP):
        send(step).wait()


def inverse(spread):
    return pl.pallas_call(
        inverse_kernel,
        out_shape=jax.ShapeDtypeStruct((IMGS, NY, NZ), BF16),
        in_specs=[pl.BlockSpec(memory_space=pltpu.VMEM)] * 3,
        out_specs=HBM,
        scratch_shapes=[
            pltpu.VMEM((IMGS, NY, NZ), BF16),
            pltpu.VMEM((IMGS * IPAD, 128), F32),
            pltpu.SemaphoreType.DMA((IMGS // OSTEP,)),
        ],
        compiler_params=pltpu.CompilerParams(vmem_limit_bytes=8 << 20),
        name="inv_local",
    )(spread, T["inv_z"], T["inv_y"])


def body(u_field, preact, cotangent, weights):
    shape = (IMGS, NY, NZ)
    partial = forward(u_field.reshape(shape), preact.reshape(shape), cotangent.reshape(shape))
    partial, weights = lax.optimization_barrier((partial, weights))
    mine = jnp.full((16, 128), lax.axis_index("dp"), jnp.int32)
    moved = lax.all_to_all(partial, "slab", split_axis=0, concat_axis=0, axis_index_groups=ORDER, tiled=True)
    wide = widen(weights)
    *pieces, back = middle(mine, moved.reshape(SLABS * 8, 128), wide)
    for at, other in enumerate(OTHERS):
        if other:
            pieces[at] = lax.ppermute(pieces[at], "dp", [(n, n ^ other) for n in range(4)])
    spread = lax.all_to_all(back, "slab", split_axis=0, concat_axis=0, axis_index_groups=BACK_ORDER, tiled=True)
    field_grad = inverse(spread)
    pieces, field_grad = lax.optimization_barrier((pieces, field_grad))
    grad_weights = weight_grad(pieces)
    return grad_weights, field_grad.reshape(1, PLANES, C, NY, NZ)


def solution(mesh):
    placed = (
        P("dp", "slab", None, None, None),
        P("dp", "slab", None, None, None),
        P("dp", "slab", None, None, None),
        P(None, "slab", None),
    )
    return jax.shard_map(
        body,
        mesh=mesh,
        in_specs=placed,
        out_specs=(P("dp", "slab", None), P("dp", "slab", None, None, None)),
        check_vma=False,
    )
```

```python
import itertools
import math

import jax
import jax.numpy as jnp
import numpy as np
from jax import lax
from jax.experimental import pallas as pl
from jax.experimental.pallas import tpu as pltpu
from jax.sharding import PartitionSpec as P

C = 32
NX = 128
NY = 128
NZ = 128
MX = 16
MY = 16
MZ = 16
SLABS = 64
PLANES = NX // SLABS
IMGS = PLANES * C
OWN = MY * MZ // SLABS
F32 = jnp.float32
BF16 = jnp.bfloat16
AHEAD = 2
OTHERS = (0, 3, 2, 1)
TURN = 52
BACK = 52
ORDER = [[n ^ TURN for n in range(SLABS)]]
BACK_ORDER = [[n ^ BACK for n in range(SLABS)]]
CUTS = (0, 16, 40, 64)
OSTEP = 8
ZB = 2
PAD = 132
IPAD = 36


def np_twiddles(length, freqs):
    product = (np.arange(length, dtype=np.int64)[:, None] * freqs[None, :]) % length
    angle = product.astype(np.float32) * np.float32(2.0 * math.pi / length)
    return np.cos(angle).astype(np.float32), np.sin(angle).astype(np.float32)


def signed(count):
    index = np.arange(count)
    return np.where(index < count // 2, index, index - count)


def split_np(table):
    high = table.astype(jnp.bfloat16)
    low = (table - high.astype(np.float32)).astype(jnp.bfloat16)
    return high, low


def make_tables():
    cx, sx = np_twiddles(NX, signed(MX))
    cy, sy = np_twiddles(NY, signed(MY))
    cz, sz = np_twiddles(NZ, np.arange(MZ))
    t = {}
    rows = np.concatenate([cy.T, sy.T], 0)
    t["fwd_y"] = np.concatenate(split_np(rows), 1)
    low_c = cz.astype(jnp.bfloat16).astype(np.float32)
    low_s = (-sz).astype(jnp.bfloat16).astype(np.float32)
    real = np.concatenate([low_c, low_s], 0).T
    imag = np.concatenate([low_s, -low_c], 0).T
    wz = np.stack([real.reshape(4, 4, 2 * NZ), imag.reshape(4, 4, 2 * NZ)], 1)
    t["fwd_z"] = wz.reshape(2 * MZ, 2 * NZ).astype(jnp.bfloat16)
    mode_scale = np.where(np.arange(MZ) == 0, 0.5, 1.0) / (NX * NY * NZ)
    per_row = np.broadcast_to(mode_scale.reshape(4, 1, 4), (4, 2, 4)).reshape(2 * MZ, 1)
    is_g = (np.arange(128) // C) % 2 == 1
    t["scale"] = np.where(is_g[None, :], per_row, 1.0).astype(np.float32)
    cxs, sxs = cx.reshape(SLABS, PLANES, MX)[ORDER[0]], sx.reshape(SLABS, PLANES, MX)[ORDER[0]]
    lx = np.zeros((PLANES, 2, MX, 2, SLABS), np.float32)
    for xx in range(PLANES):
        lx[xx, 0, :, 0] = cxs[:, xx].T
        lx[xx, 0, :, 1] = sxs[:, xx].T
        lx[xx, 1, :, 0] = -sxs[:, xx].T
        lx[xx, 1, :, 1] = cxs[:, xx].T
    t["fwd_x"] = np.concatenate(split_np(lx.reshape(PLANES * 2 * MX, 2 * SLABS)), 0)
    rep = np.zeros((128, 2, 4, C), np.float32)
    for part in range(2):
        for ch in range(C):
            rep[part * 64 + 32 + ch, part, :, ch] = 1.0
    t["rep_g"] = rep.reshape(128, 256).astype(jnp.bfloat16)
    rep = np.zeros((2, 2, 8, 4, 2, 4, C), np.float32)
    for part in range(2):
        for r in range(4):
            rep[part, 0, :, r, part, r, :] = 1.0
    t["rep_u"] = rep.reshape(128, 256).astype(jnp.bfloat16)
    red = np.zeros((2, 4, C, 4, 8, 4), np.float32)
    for r in range(4):
        red[0, r, :, 0, :, r] = 1.0
        red[1, r, :, 1, :, r] = 1.0
        red[1, r, :, 2, :, r] = -1.0
        red[0, r, :, 3, :, r] = 1.0
    t["red"] = red.reshape(256, 128).astype(jnp.bfloat16)
    cxb, sxb = cx.reshape(SLABS, PLANES, MX)[BACK_ORDER[0]], sx.reshape(SLABS, PLANES, MX)[BACK_ORDER[0]]
    ld = np.stack([cxb, sxb], 2).reshape(SLABS, PLANES * 2 * MX)
    high, low = split_np(ld)
    t["inv_x"] = np.concatenate([high, high, low], 1)
    czb, szb = ((v.T.reshape(4, 4, NZ)[np.arange(4) ^ BACK % 4]).reshape(MZ, NZ) for v in (cz, sz))
    tz = np.stack([np.concatenate([czb, szb], 1), np.concatenate([-szb, czb], 1)])
    tz = np.broadcast_to(tz[:, None], (2, 8, MZ, 2 * NZ)).reshape(256, 2 * NZ)
    high, low = split_np(tz)
    odd = (np.arange(256) // MZ % 2 == 1)[:, None]
    t["inv_z"] = np.where(odd, low, high)
    ly = np.concatenate([cy, -sy], 1)
    high, low = split_np(ly)
    t["inv_y"] = np.concatenate([high, high, low], 1)
    return t


T = make_tables()


def split(value):
    high = value.astype(BF16)
    return high, (value - high.astype(F32)).astype(BF16)


def mm(a, b):
    return jnp.dot(a, b, preferred_element_type=F32)


def mm_nt(a, b):
    return lax.dot_general(a, b, (((1,), (1,)), ((), ())), preferred_element_type=F32)


HBM = pl.BlockSpec(memory_space=pltpu.HBM)


def forward_kernel(
    u_hbm, p_hbm, c_hbm, ty_hbm, wz_hbm, sc_hbm, o_hbm, o_ref, u_ref, p_ref, c_ref, ty_ref, wz_ref, sc_ref, xc_ref, xs_ref, sems, tsems, osems
):
    def chunk(src, dst, row, step):
        at = pl.ds(CUTS[step], CUTS[step + 1] - CUTS[step])
        return pltpu.make_async_copy(src.at[at], dst.at[at], sems.at[row, step])

    table = pltpu.make_async_copy(ty_hbm, ty_ref, tsems.at[0])
    late = [
        pltpu.make_async_copy(wz_hbm, wz_ref, tsems.at[1]),
        pltpu.make_async_copy(sc_hbm, sc_ref, tsems.at[2]),
    ]
    def fetch(step):
        chunk(p_hbm, p_ref, 1, step).start()
        chunk(c_hbm, c_ref, 2, step).start()
        chunk(u_hbm, u_ref, 0, step).start()

    fetch(0)
    table.start()
    for step in range(1, AHEAD):
        fetch(step)
    for one in late:
        one.start()
    table.wait()

    def arrived(step):
        for row, (src, dst) in enumerate(((u_hbm, u_ref), (p_hbm, p_ref), (c_hbm, c_ref))):
            chunk(src, dst, row, step).wait()

    def slope_of(k):
        if True:
            arg = p_ref[k].astype(F32) * math.sqrt(0.5)
            bell = jnp.exp2((arg * (-math.log2(math.e))) * arg) * (2.0 / math.sqrt(math.pi))
            slope = (lax.erf(arg) + 1.0) + arg * bell
            c_ref[k] = (c_ref[k].astype(F32) * slope).astype(BF16)

    ty = ty_ref[...]

    def image(k):
        if True:
            both = jnp.concatenate([u_ref[k], c_ref[k]], axis=1)
            part = mm(ty, jnp.concatenate([both, both], axis=0))
            base = (k // C) * 64 + k % C
            xc_ref[pl.ds(base, MY, stride=PAD), :] = part[:16, :128]
            xs_ref[pl.ds(base, MY, stride=PAD), :] = part[16:, :128]
            xc_ref[pl.ds(base + 32, MY, stride=PAD), :] = part[:16, 128:]
            xs_ref[pl.ds(base + 32, MY, stride=PAD), :] = part[16:, 128:]

    for step in range(len(CUTS)):
        if step < len(CUTS) - 1:
            arrived(step)
            if step + AHEAD < len(CUTS) - 1:
                fetch(step + AHEAD)
        if step < len(CUTS) - 1:
            for k in range(CUTS[step], CUTS[step + 1]):
                slope_of(k)
                if k >= 2:
                    image(k - 2)
        else:
            image(62)
            image(63)
    for one in late:
        one.wait()
    wz = wz_ref[...]
    scale = sc_ref[...]

    def send(part):
        at = pl.ds(part * 16, 16)
        return pltpu.make_async_copy(o_ref.at[at], o_hbm.at[at], osems.at[part])

    for b in range(MY):
        rows = slice(b * PAD, b * PAD + 128)
        both = jnp.concatenate([xc_ref[rows, :].astype(BF16), xs_ref[rows, :].astype(BF16)], axis=1)
        res = mm_nt(wz, both)
        res = res * scale
        for q in range(4):
            o_ref[(b * 4 + q) ^ TURN] = res[q * 8 : (q + 1) * 8]
        if b % 4 == 3:
            send(b // 4 ^ TURN // 16).start()
    for part in range(4):
        send(part).wait()


def forward(u, pre, cot):
    big = pltpu.VMEM((IMGS, NY, NZ), BF16)
    flat = pltpu.VMEM((MY * PAD, 128), F32)
    return pl.pallas_call(
        forward_kernel,
        out_shape=jax.ShapeDtypeStruct((SLABS, 8, 128), F32),
        in_specs=[HBM] * 6,
        out_specs=HBM,
        scratch_shapes=[
            pltpu.VMEM((SLABS, 8, 128), F32),
            big,
            big,
            big,
            pltpu.VMEM((32, 256), BF16),
            pltpu.VMEM((32, 256), BF16),
            pltpu.VMEM((32, 128), F32),
            flat,
            flat,
            pltpu.SemaphoreType.DMA((3, (len(CUTS) - 1))),
            pltpu.SemaphoreType.DMA((3,)),
            pltpu.SemaphoreType.DMA((4,)),
        ],
        name="fwd_local",
    )(u, pre, cot, T["fwd_y"], T["fwd_z"], T["scale"])


def widen_kernel(w_ref, o_ref):
    for a in range(MX):
        o_ref[pl.ds(4 * a, 4), :] = w_ref[a].astype(F32)


def widen(weights):
    return pl.pallas_call(
        widen_kernel,
        out_shape=jax.ShapeDtypeStruct((MX * OWN, 2 * C * C), F32),
        in_specs=[pl.BlockSpec(memory_space=pltpu.VMEM)],
        out_specs=pl.BlockSpec(memory_space=pltpu.VMEM),
        compiler_params=pltpu.CompilerParams(vmem_limit_bytes=4 << 20),
        name="widen",
    )(weights)


def middle_kernel(
    mine_ref, m_ref, wf_ref, lx_ref, rg_ref, red_ref, ld_ref, own0_ref, own1_ref, own2_ref, own3_ref, d_ref, own_ref, q_ref
):
    lx = lx_ref[...]
    lane = lax.broadcasted_iota(jnp.int32, (MX, 128), 1)
    left = lane < 64
    for cr in range(OWN):
        rhs = jnp.concatenate(
            [m_ref[pl.ds(cr, SLABS, stride=8), :], m_ref[pl.ds(4 + cr, SLABS, stride=8), :]], axis=0
        )
        hi, lo = split(rhs)
        res = mm(lx, hi)
        res = res[:64] + res[64:] + mm(lx[:64], lo)
        summed = res[:32] + pltpu.roll(res[32:], 64, 1)
        own_ref[pl.ds(cr, MX, stride=OWN), :] = jnp.where(
            left, summed[:16], pltpu.roll(summed[16:], 64, 1)
        )
    mine = mine_ref[...]
    quarter = [own_ref[c * 16 : (c + 1) * 16, :] for c in range(4)]
    for other, ref in zip(OTHERS, (own0_ref, own1_ref, own2_ref, own3_ref)):
        piece = quarter[3 ^ other]
        for c in range(3):
            piece = jnp.where(mine == c, quarter[c ^ other], piece)
        ref[...] = piece
    hi, lo = split(own_ref[...])
    rg = rg_ref[...]
    grep = mm(hi, rg) + mm(lo, rg)
    g_real, g_imag = grep[:, :128], grep[:, 128:]
    acc = jnp.zeros((MX * OWN, 128), F32)
    slot = (lax.broadcasted_iota(jnp.int32, (MX * OWN, 128), 1) // 4) % 8
    red = red_ref[...]
    for t in range(8):
        w_real = wf_ref[:, t * 128 : (t + 1) * 128]
        w_imag = wf_ref[:, 1024 + t * 128 : 1024 + (t + 1) * 128]
        rhi, rlo = split(w_real * g_real + w_imag * g_imag)
        ihi, ilo = split(w_real * g_imag - w_imag * g_real)
        res = mm(jnp.concatenate([rhi, ihi], axis=1), red)
        res += mm(jnp.concatenate([rlo, ilo], axis=1), red)
        acc = jnp.where(slot == t, res, acc)
    q_ref[...] = acc
    ld = ld_ref[...]
    for cr in range(OWN):
        q = q_ref[pl.ds(cr, MX, stride=OWN), :]
        r = pltpu.roll(q, 64, 1)
        zero = jnp.zeros_like(q)
        rhs = jnp.concatenate(
            [
                jnp.where(left, q, zero),
                jnp.where(left, r, zero),
                jnp.where(left, zero, r),
                jnp.where(left, zero, q),
            ],
            axis=0,
        )
        hi, lo = split(rhs)
        d_ref[pl.ds(cr, SLABS, stride=OWN), :] = mm(ld, jnp.concatenate([hi, lo, hi], axis=0))


def middle(mine, moved, weights):
    return pl.pallas_call(
        middle_kernel,
        out_shape=(jax.ShapeDtypeStruct((16, 128), F32),) * 4
        + (jax.ShapeDtypeStruct((SLABS * OWN, 128), F32),),
        in_specs=[pl.BlockSpec(memory_space=pltpu.VMEM)] * 7,
        scratch_shapes=[
            pltpu.VMEM((MX * OWN, 128), F32),
            pltpu.VMEM((MX * OWN, 128), F32),
        ],
        compiler_params=pltpu.CompilerParams(vmem_limit_bytes=8 << 20),
        name="middle",
    )(mine, moved, weights, T["fwd_x"], T["rep_g"], T["red"], T["inv_x"])


def weight_grad_kernel(s0_ref, s1_ref, s2_ref, s3_ref, rg_ref, ru_ref, o_ref):
    parts = (s0_ref, s1_ref, s2_ref, s3_ref)
    full = jnp.concatenate([part[...] for part in parts], axis=0)
    both = jnp.concatenate(split(full), axis=1)
    rg = rg_ref[...]
    ru = ru_ref[...]
    rg = jnp.concatenate([rg, rg], axis=0)
    ru = jnp.concatenate([ru, ru], axis=0)
    grep = mm(both, rg)
    g_real, g_imag = grep[:, :128], grep[:, 128:]
    slot = (lax.broadcasted_iota(jnp.int32, (64, 256), 1) // 4) % 8
    for t in range(8):
        urep = mm(jnp.where(slot == t, both, jnp.zeros_like(both)), ru)
        u_real, u_imag = urep[:, :128], urep[:, 128:]
        real = g_real * u_real + g_imag * u_imag
        imag = g_imag * u_real - g_real * u_imag
        real = real[:16] + real[16:32] + real[32:48] + real[48:]
        imag = imag[:16] + imag[16:32] + imag[32:48] + imag[48:]
        for a in range(4):
            o_ref[a, :, t * 128 : (t + 1) * 128] = real[a * 4 : (a + 1) * 4]
            o_ref[a, :, 1024 + t * 128 : 1024 + (t + 1) * 128] = imag[a * 4 : (a + 1) * 4]


def weight_grad(parts):
    return pl.pallas_call(
        weight_grad_kernel,
        out_shape=jax.ShapeDtypeStruct((4, OWN, 2 * C * C), F32),
        compiler_params=pltpu.CompilerParams(vmem_limit_bytes=4 << 20),
        name="weight_grad",
    )(*parts, T["rep_g"], T["rep_u"])


def inverse_kernel(
    d_ref, tz_ref, ly_ref, o_hbm, o_ref, f_ref, osems
):
    full = d_ref[...].astype(BF16)
    packed = []
    for odd in range(2):
        blocks = []
        for b in range(MY):
            at = ((b // 2 * 2 + odd) ^ BACK // 4) * MZ
            blocks.append(full[at : at + MZ])
        flat = jnp.concatenate(blocks, axis=0).T
        real = jnp.concatenate([flat[0:32], flat[64:96]], axis=0)
        imag = jnp.concatenate([flat[32:64], flat[96:128]], axis=0)
        for half in (slice(0, 128), slice(128, 256)):
            packed.append(jnp.concatenate([real[:, half], imag[:, half]], axis=1))
    tz = tz_ref[...]
    group = lax.broadcasted_iota(jnp.int32, (64, 256), 1) % 128 // (2 * MZ)
    for first in range(0, MY, ZB):
        rows = []
        for b in range(first, first + ZB):
            part = packed[b % 2 * 2 + b // 8]
            rows.append(jnp.where(group == b % 8 // 2, part, jnp.zeros_like(part)))
        res = mm(jnp.concatenate(rows, axis=0), tz)
        for b in range(first, first + ZB):
            h = res[(b - first) * 64 : (b - first + 1) * 64]
            for xx in range(PLANES):
                at = xx * C * IPAD + b
                f_ref[pl.ds(at, C, stride=IPAD), :] = h[xx * 32 : xx * 32 + 32, :128]
                f_ref[pl.ds(at + 16, C, stride=IPAD), :] = h[xx * 32 : xx * 32 + 32, 128:]

    def send(step):
        at = pl.ds(step * OSTEP, OSTEP)
        return pltpu.make_async_copy(o_ref.at[at], o_hbm.at[at], osems.at[step])

    ly = ly_ref[...]
    for step in range(IMGS // OSTEP):
        for k in range(step * OSTEP, (step + 1) * OSTEP, 2):
            at = k * IPAD
            block = f_ref[pl.ds(at, 72), :]
            pair = jnp.concatenate([block[:32], block[36:68]], axis=1)
            hi, lo = split(pair)
            res = mm(ly, jnp.concatenate([hi, lo, hi], axis=0)).astype(BF16)
            o_ref[k] = res[:, :128]
            o_ref[k + 1] = res[:, 128:]
        send(step).start()
    for step in range(IMGS // OSTEP):
        send(step).wait()


def inverse(spread):
    return pl.pallas_call(
        inverse_kernel,
        out_shape=jax.ShapeDtypeStruct((IMGS, NY, NZ), BF16),
        in_specs=[pl.BlockSpec(memory_space=pltpu.VMEM)] * 3,
        out_specs=HBM,
        scratch_shapes=[
            pltpu.VMEM((IMGS, NY, NZ), BF16),
            pltpu.VMEM((IMGS * IPAD, 128), F32),
            pltpu.SemaphoreType.DMA((IMGS // OSTEP,)),
        ],
        compiler_params=pltpu.CompilerParams(vmem_limit_bytes=8 << 20),
        name="inv_local",
    )(spread, T["inv_z"], T["inv_y"])


def body(u_field, preact, cotangent, weights):
    shape = (IMGS, NY, NZ)
    partial = forward(u_field.reshape(shape), preact.reshape(shape), cotangent.reshape(shape))
    partial, weights = lax.optimization_barrier((partial, weights))
    mine = jnp.full((16, 128), lax.axis_index("dp"), jnp.int32)
    moved = lax.all_to_all(partial, "slab", split_axis=0, concat_axis=0, axis_index_groups=ORDER, tiled=True)
    wide = widen(weights)
    *pieces, back = middle(mine, moved.reshape(SLABS * 8, 128), wide)
    for at, other in enumerate(OTHERS):
        if other:
            pieces[at] = lax.ppermute(pieces[at], "dp", [(n, n ^ other) for n in range(4)])
    spread = lax.all_to_all(back, "slab", split_axis=0, concat_axis=0, axis_index_groups=BACK_ORDER, tiled=True)
    field_grad = inverse(spread)
    pieces, field_grad = lax.optimization_barrier((pieces, field_grad))
    grad_weights = weight_grad(pieces)
    return grad_weights, field_grad.reshape(1, PLANES, C, NY, NZ)


def solution(mesh):
    placed = (
        P("dp", "slab", None, None, None),
        P("dp", "slab", None, None, None),
        P("dp", "slab", None, None, None),
        P(None, "slab", None),
    )
    return jax.shard_map(
        body,
        mesh=mesh,
        in_specs=placed,
        out_specs=(P("dp", "slab", None), P("dp", "slab", None, None, None)),
        check_vma=False,
    )
```
